32 devices in a mesh: branch: 2 (over x), dp: 16 (over z, y, core).
Axes of the slice: x: 2, y: 2, z: 4, core: 2. Of those that a mesh axis runs over, the one named last changes fastest.
Arguments:
- inputs: bfloat16 [32, 1024, 768], P('dp'), may hold values from -6 to 6
- segments: int32 [32, 1024], P('dp'), may hold values from 0 to 7, never falling along the last dimension, each value on 1 to 512 neighbouring positions
- query_weight: bfloat16 [768, 384], replicated, may hold values from -0.21875 to 0.21875
- query_bias: float32 [384], replicated, may hold values from -1 to 1
- branch_weights: bfloat16 [2, 2, 768, 384], P('branch'), may hold values from -0.21875 to 0.21875
- value_bias: float32 [384], replicated, may hold values from -1 to 1
- depthwise: float32 [9, 768], replicated, may hold values from -2 to 2
- point_bias: float32 [384], replicated, may hold values from -1 to 1
- kernel_weight: bfloat16 [384, 54], replicated, may hold values from -0.3125 to 0.3125
- kernel_bias: float32 [54], replicated, may hold values from -2 to 2
- conv_bias: float32 [384], replicated, may hold values from -1 to 1
- output_weight: bfloat16 [768, 768], replicated, may hold values from -0.875 to 0.875
- output_bias: float32 [768], replicated, may hold values from -1 to 1
- first_gain: float32 [768], replicated, may hold values from 0.5 to 1.5
- first_shift: float32 [768], replicated, may hold values from -1 to 1
- up_weight: bfloat16 [2, 384, 1536], replicated, may hold values from -0.3125 to 0.3125
- up_bias: float32 [2, 1536], replicated, may hold values from -1 to 1
- down_weight: bfloat16 [2, 1536, 384], replicated, may hold values from -0.15625 to 0.15625
- down_bias: float32 [2, 384], replicated, may hold values from -1 to 1
- second_gain: float32 [768], replicated, may hold values from 0.5 to 1.5
- second_shift: float32 [768], replicated, may hold values from -1 to 1
- cotangent: bfloat16 [32, 1024, 768], P('dp', 'branch'), may hold values from -6 to 6
Outputs:
- activations: bfloat16 [32, 1024, 768], P('dp', 'branch')
- input_grad: float32 [32, 1024, 768], P('dp', 'branch')
- query_weight_grad: float32 [768, 384], replicated
- query_bias_grad: float32 [384], replicated
- branch_weights_grad: float32 [2, 2, 768, 384], P('branch')
- value_bias_grad: float32 [384], replicated
- depthwise_kernel_gradient: float32 [9, 768], replicated
- point_bias_grad: float32 [384], replicated
- kernel_weight_grad: float32 [384, 54], replicated
- kernel_bias_grad: float32 [54], replicated
- conv_bias_grad: float32 [384], replicated
- output_weight_grad: float32 [768, 768], replicated
- output_bias_grad: float32 [768], replicated
- first_gain_grad: float32 [768], replicated
- first_shift_grad: float32 [768], replicated
- up_weight_grad: float32 [2, 384, 1536], replicated
- up_bias_grad: float32 [2, 1536], replicated
- down_weight_grad: float32 [2, 1536, 384], replicated
- down_bias_grad: float32 [2, 384], replicated
- second_gain_grad: float32 [768], replicated
- second_shift_grad: float32 [768], replicated
The draws below stay inside these ranges and needn't reach their ends.
Inputs may be any that keep to these rules, and one draw needn't show every extreme that they name: `segments`: in each sequence the document ids never fall, every document holds 1 to half of 1024 tokens, and some document holds exactly half of 1024.
All inputs are finite; a program needn't handle non-finite values.
Results may differ from the reference program's by a relative error of at most 0.02.
Values may be sent and summed in bfloat16 or wider, within the bound.
No kernel may reach another device: no remote copies, remote signals or barrier semaphores. Data moves between devices by JAX's collectives and lax.ppermute only.
A program may use at most 256 MiB of HBM per device.

```python
import math
import jax
import jax.numpy as jnp
import numpy as np
from jax import lax

D = 768
HEADS = 6
HEAD = 64
KERNEL = 9
FF = 3072
GROUPS = 2
LEN = 1024
DOCS = 8
SEQS = 32


def steps_of(rng, shape, cuts, least, high):
    def one(dim, shards_of):
        draws = jax.random.uniform(jax.random.fold_in(jax.random.fold_in(rng, 6), dim), (shards_of,), jnp.float32, least / len(cuts), high / len(cuts))
        return jnp.repeat(jnp.exp(draws), shape[dim] // shards_of).reshape((-1,) + (1,) * (len(shape) - dim - 1))

    factor_of = one(*cuts[0])
    for cut in cuts[1:]:
        factor_of = factor_of * one(*cut)
    return factor_of


def profile(amount, total, limit, slope):
    loads = [(1 << 20) // math.isqrt(standing ** slope) + 1 for standing in range(2, amount + 1)]
    rest, holding = total - limit - (amount - 1), [1] * (amount - 1)
    while rest > 0:
        free = [i for i in range(amount - 1) if holding[i] < limit]
        whole, budget = sum([loads[i] for i in free]), rest
        for i in free:
            extra = min(limit - holding[i], max(1, budget * loads[i] // whole), rest)
            holding[i] = holding[i] + extra
            rest = rest - extra
    return np.array([limit] + holding)


def uneven(own_key, count, total, bound, slope):
    if count == 2:
        one = jax.random.randint(own_key, (), max(1, total - bound), min(bound, total - 1) + 1)
        return jnp.stack([one, total - one])
    lengths = jnp.asarray(profile(count, total, bound, slope), jnp.int32)
    twos = (count - 1) // 2
    source_of, taker = lengths[1:1 + 2 * twos:2], lengths[2:2 + 2 * twos:2]
    slack = jnp.minimum(source_of - 1, bound - taker)
    moved = jax.random.randint(jax.random.fold_in(own_key, 1), (twos,), 0, 1 << 20) % (slack + 1)
    lengths = lengths.at[1:1 + 2 * twos:2].set(source_of - moved).at[2:2 + 2 * twos:2].set(taker + moved)
    return lengths[jax.random.permutation(jax.random.fold_in(own_key, 2), count)]


def scatter_about(rng, extent, deviation, bound, cuts=(), dtype=jnp.bfloat16):
    gain = steps_of(rng, extent, cuts, -0.22, 0.18) if cuts else 1.0
    values = jax.random.normal(rng, extent, jnp.float32) * deviation * gain
    return jnp.minimum(jnp.maximum(values, -bound), bound).astype(dtype)


def setup_inputs(seed: int = 0) -> dict:
    streams_of = jax.random.split(jax.random.key(seed), 23)
    return {
        "inputs": scatter_about(streams_of[0], (SEQS, LEN, D), 1.0, 6.0, ((0, 16),)),
        "segments": jax.vmap(lambda own: jnp.searchsorted(jnp.cumsum(uneven(own, DOCS, LEN, LEN // 2, 2)), jnp.arange(LEN), side="right"))(jax.random.split(streams_of[1], SEQS)).reshape((SEQS, LEN)).astype(jnp.int32),
        "query_weight": scatter_about(streams_of[2], (D, HEADS * HEAD), D ** -0.5, 0.21875),
        "query_bias": scatter_about(streams_of[3], (HEADS * HEAD,), 0.2, 1.0, (), jnp.float32),
        "branch_weights": scatter_about(streams_of[4], (2, 2, D, HEADS * HEAD), D ** -0.5, 0.21875, ((0, 2),)),
        "value_bias": scatter_about(streams_of[5], (HEADS * HEAD,), 0.2, 1.0, (), jnp.float32),
        "depthwise": scatter_about(streams_of[6], (KERNEL, D), KERNEL ** -0.5, 2.0, (), jnp.float32),
        "point_bias": scatter_about(streams_of[7], (HEADS * HEAD,), 0.2, 1.0, (), jnp.float32),
        "kernel_weight": scatter_about(streams_of[8], (HEADS * HEAD, HEADS * KERNEL), (HEADS * HEAD) ** -0.5, 0.3125),
        "kernel_bias": scatter_about(streams_of[9], (HEADS * KERNEL,), 0.5, 2.0, (), jnp.float32),
        "conv_bias": scatter_about(streams_of[10], (HEADS * HEAD,), 0.2, 1.0, (), jnp.float32),
        "output_weight": scatter_about(streams_of[11], (D, D), (D // 16) ** -0.5, 0.875),
        "output_bias": scatter_about(streams_of[12], (D,), 0.2, 1.0, (), jnp.float32),
        "first_gain": jnp.clip(1.0 + 0.1 * jax.random.normal(streams_of[13], (D,), jnp.float32), 0.5, 1.5),
        "first_shift": scatter_about(streams_of[14], (D,), 0.2, 1.0, (), jnp.float32),
        "up_weight": scatter_about(streams_of[15], (GROUPS, D // GROUPS, FF // GROUPS), (D // GROUPS) ** -0.5, 0.3125),
        "up_bias": scatter_about(streams_of[16], (GROUPS, FF // GROUPS), 0.2, 1.0, (), jnp.float32),
        "down_weight": scatter_about(streams_of[17], (GROUPS, FF // GROUPS, D // GROUPS), (FF // GROUPS) ** -0.5, 0.15625),
        "down_bias": scatter_about(streams_of[18], (GROUPS, D // GROUPS), 0.2, 1.0, (), jnp.float32),
        "second_gain": jnp.clip(1.0 + 0.1 * jax.random.normal(streams_of[19], (D,), jnp.float32), 0.5, 1.5),
        "second_shift": scatter_about(streams_of[20], (D,), 0.2, 1.0, (), jnp.float32),
        "cotangent": scatter_about(streams_of[21], (SEQS, LEN, D), 1.0, 6.0, ((0, 16), (1, 2))),
    }


EPS = 1e-12
BIG = -1e+30

@jax.custom_vjp
def low(v):
    return lax.optimization_barrier(v.astype(jnp.bfloat16)).astype(jnp.float32)

@jax.custom_vjp
def lowered_backward(v):
    return v

def low_keep(v):
    return (low(v), None)

def low_pass(kept, grad):
    return (grad,)

def back_keep(v):
    return (v, None)

def back_low(kept, grad):
    return (low(grad),)
low.defvjp(low_keep, low_pass)
lowered_backward.defvjp(back_keep, back_low)

def rounded(array_in):
    return lowered_backward(low(array_in))

def project(left_operand, right_operand):
    return jnp.einsum('vzt,ta->vza', left_operand, right_operand, precision=lax.Precision.HIGHEST)

def shifted(array_in, offset):
    half_window = KERNEL // 2
    widths = [(0, 0)] * array_in.ndim
    widths[1] = (half_window, half_window)
    padded = jnp.pad(array_in, widths)
    return lax.slice_in_dim(padded, half_window + offset, half_window + offset + array_in.shape[1], axis=1)

def window_masks(segments):
    half_window = KERNEL // 2
    padded = jnp.pad(segments, ((0, 0), (half_window, half_window)), constant_values=-1)
    tap_masks = []
    for tap_index in range(KERNEL):
        shifted_ids = lax.slice_in_dim(padded, tap_index, tap_index + segments.shape[1], axis=1)
        tap_masks.append((shifted_ids == segments).astype(jnp.float32))
    return tap_masks

def layer_norm(residual, norm_gain, norm_shift):
    center = residual - lax.optimization_barrier(jnp.mean(residual, axis=-1, keepdims=True))
    spread = lax.optimization_barrier(jnp.mean(center * center, axis=-1, keepdims=True))
    return center * lax.rsqrt(spread + EPS) * norm_gain + norm_shift

def attend(queries, key_rows, value_rows, segments):
    seq_count, length, _ = queries.shape
    row_block = min(512, length)
    score_scale = HEAD ** (-0.5)
    query_heads = queries.reshape(seq_count, length // row_block, row_block, HEADS, HEAD).transpose(1, 0, 2, 3, 4)
    seg_blocks = segments.reshape(seq_count, length // row_block, row_block).transpose(1, 0, 2)
    key_heads = key_rows.reshape(seq_count, length, HEADS, HEAD)
    value_heads = value_rows.reshape(seq_count, length, HEADS, HEAD)

    def one_block(pieces):
        query_block, seg_block = pieces
        scores = jnp.einsum('sqhe,skhe->shqk', query_block, key_heads, precision=lax.Precision.HIGHEST) * score_scale
        same_doc = seg_block[:, None, :, None] == segments[:, None, None, :]
        scores = lowered_backward(jnp.where(same_doc, scores, BIG))
        weights = low(jax.nn.softmax(scores, axis=-1))
        return jnp.einsum('shqk,skhe->sqhe', weights, value_heads, precision=lax.Precision.HIGHEST)
    outputs = lax.map(jax.checkpoint(one_block), (query_heads, seg_blocks))
    return outputs.transpose(1, 0, 2, 3, 4).reshape(seq_count, length, HEADS * HEAD)

def convolve(inputs, queries, segments, depthwise, point_weight, point_bias, kernel_weight, kernel_bias, value_weight, conv_bias):
    tap_masks = window_masks(segments)
    half_window = KERNEL // 2
    seq_count, length, _ = inputs.shape
    depth_out = jnp.zeros(inputs.shape, jnp.float32)
    for tap_index in range(KERNEL):
        depth_out = depth_out + depthwise[tap_index] * shifted(inputs, tap_index - half_window) * tap_masks[tap_index][..., None]
    key_conv = rounded(project(low(depth_out), point_weight) + point_bias)
    mixing = low(key_conv * queries)
    logits = lowered_backward(project(mixing, kernel_weight) + kernel_bias)
    tap_weights = low(jax.nn.softmax(logits.reshape(seq_count, length, HEADS, KERNEL), axis=-1))
    values = rounded(project(inputs, value_weight) + conv_bias).reshape(seq_count, length, HEADS, HEAD)
    mixed = jnp.zeros(values.shape, jnp.float32)
    for tap_index in range(KERNEL):
        mixed = mixed + tap_weights[..., tap_index:tap_index + 1] * shifted(values, tap_index - half_window) * tap_masks[tap_index][..., None, None]
    return mixed.reshape(seq_count, length, HEADS * HEAD)

def block_layer(inputs, segments, params):
    query_weight, query_bias, branch_weights, value_bias, depthwise, point_bias, kernel_weight, kernel_bias, conv_bias, output_weight, output_bias, first_gain, first_shift, up_weight, up_bias, down_weight, down_bias, second_gain, second_shift = params
    queries = rounded(project(inputs, query_weight) + query_bias)
    key_rows = rounded(project(inputs, branch_weights[0, 0]))
    value_rows = rounded(project(inputs, branch_weights[0, 1]) + value_bias)
    attended = attend(queries, key_rows, value_rows, segments)
    mixed = convolve(inputs, queries, segments, depthwise, branch_weights[1, 0], point_bias, kernel_weight, kernel_bias, branch_weights[1, 1], conv_bias)
    joined_parts = rounded(jnp.concatenate([attended, mixed], axis=-1))
    hidden = lowered_backward(project(joined_parts, output_weight) + output_bias)
    normed_one = layer_norm(inputs + hidden, first_gain, first_shift)
    seq_count, length, features = normed_one.shape
    grouped = low(normed_one).reshape(seq_count, length, GROUPS, features // GROUPS)
    up_proj = lowered_backward(jnp.einsum('slgi,gio->slgo', grouped, up_weight, precision=lax.Precision.HIGHEST) + up_bias)
    active = low(jax.nn.gelu(up_proj, approximate=False))
    lowered = lowered_backward(jnp.einsum('slgo,goi->slgi', active, down_weight, precision=lax.Precision.HIGHEST) + down_bias)
    return layer_norm(normed_one + lowered.reshape(seq_count, length, features), second_gain, second_shift)

def reference(inputs, segments, query_weight, query_bias, branch_weights, value_bias, depthwise, point_bias, kernel_weight, kernel_bias, conv_bias, output_weight, output_bias, first_gain, first_shift, up_weight, up_bias, down_weight, down_bias, second_gain, second_shift, cotangent):
    params = tuple((argument.astype(jnp.float32) for argument in (query_weight, query_bias, branch_weights, value_bias, depthwise, point_bias, kernel_weight, kernel_bias, conv_bias, output_weight, output_bias, first_gain, first_shift, up_weight, up_bias, down_weight, down_bias, second_gain, second_shift)))
    per_step = math.gcd(SEQS, max(1, 4096 // LEN))
    step_count = SEQS // per_step
    stacked_in = inputs.astype(jnp.float32).reshape(step_count, per_step, LEN, D)
    stacked_seg = segments.astype(jnp.int32).reshape(step_count, per_step, LEN)
    stacked_cot = cotangent.astype(jnp.float32).reshape(step_count, per_step, LEN, D)

    def one_step(summed, pieces):
        block_in, block_seg, block_cot = pieces

        def run_layer(values, weights):
            return block_layer(values, block_seg, weights)
        result, pullback = jax.vjp(run_layer, block_in, params)
        grad_in, grad_params = pullback(block_cot)
        summed = tuple((earlier + addend for earlier, addend in zip(summed, grad_params)))
        return (summed, (result.astype(jnp.bfloat16), grad_in))
    start_sums = tuple((jnp.zeros_like(argument) for argument in params))
    summed, (results, grads_in) = lax.scan(one_step, start_sums, (stacked_in, stacked_seg, stacked_cot))
    activations = results.reshape(SEQS, LEN, D)
    input_grad = grads_in.reshape(SEQS, LEN, D)
    return (activations, input_grad, summed[0], summed[1], summed[2], summed[3], summed[4], summed[5], summed[6], summed[7], summed[8], summed[9], summed[10], summed[11], summed[12], summed[13], summed[14], summed[15], summed[16], summed[17], summed[18])
```

```python
import jax
import jax.numpy as jnp
from jax import lax
from jax.experimental import pallas as pl
from jax.experimental.pallas import tpu as pltpu
from jax.sharding import PartitionSpec as P

HEADS = 6
HEAD = 64
KERNEL = 9
HALF = KERNEL // 2
GROUPS = 2
DOCS = 8
EPS = 1e-12
BIG = -1e30
SCALE = HEAD**-0.5

PAD = 16
SLOTS = 10
LANES = 128
f32 = jnp.float32
bf16 = jnp.bfloat16


def mm(a, b):
    return jnp.dot(a, b, preferred_element_type=f32)


def mm_nt(a, b):
    return lax.dot_general(a, b, (((1,), (1,)), ((), ())), preferred_element_type=f32)


def mm_tn(a, b):
    return lax.dot_general(a, b, (((0,), (0,)), ((), ())), preferred_element_type=f32)


def params(mib):
    return pltpu.CompilerParams(vmem_limit_bytes=mib * 1024 * 1024)


def cost(flops, nbytes):
    return pl.CostEstimate(flops=int(flops), bytes_accessed=int(nbytes), transcendentals=0)


def window(ref, start, rows, cols):
    return ref[pl.ds(pl.multiple_of(start + PAD - 8, 8), rows + 16), cols]


def moved(win, offset, rows):
    total = rows + 16
    if offset == 0:
        return win[8 : 8 + rows]
    return pltpu.roll(win, (-offset) % total, 0)[8 : 8 + rows]


def clear_pads(ref, length):
    width = ref.shape[1]
    ref[0:PAD, :] = jnp.zeros((PAD, width), f32)
    ref[PAD + length : PAD + length + PAD, :] = jnp.zeros((PAD, width), f32)


def front_body(x_ref, maskc_ref, wq_ref, bq_ref, dw_ref, q_ref, dl_ref, pad):
    length, width = x_ref.shape
    clear_pads(pad, length)
    rows = 32

    @pl.loop(0, length // 128)
    def _(i):
        t0 = pl.multiple_of(i * 128, 128)
        pad[pl.ds(pl.multiple_of(t0 + PAD, 16), 128), :] = x_ref[pl.ds(t0, 128), :].astype(f32)

    @pl.loop(0, length // 256)
    def _(i):
        t0 = pl.multiple_of(i * 256, 256)
        q_ref[pl.ds(t0, 256), :] = (mm(x_ref[pl.ds(t0, 256), :], wq_ref[...]) + bq_ref[...]).astype(
            bf16
        )

    @pl.loop(0, length // rows)
    def _(i):
        t0 = pl.multiple_of(i * rows, rows)
        mask = maskc_ref[pl.ds(t0, rows), :]
        masks = [jnp.broadcast_to(mask[:, j : j + 1], (rows, LANES)) for j in range(KERNEL)]
        for c in range(width // LANES):
            cols = slice(c * LANES, (c + 1) * LANES)
            win = window(pad, t0, rows, cols)
            total = jnp.zeros((rows, LANES), f32)
            for j in range(KERNEL):
                total = total + dw_ref[j : j + 1, cols] * moved(win, j - HALF, rows) * masks[j]
            dl_ref[pl.ds(t0, rows), cols] = total.astype(bf16)


def front(x, maskc, wq, bq, dw):
    length, width = x.shape
    inner = wq.shape[1]
    return pl.pallas_call(
        front_body,
        out_shape=(
            jax.ShapeDtypeStruct((length, inner), bf16),
            jax.ShapeDtypeStruct((length, width), bf16),
        ),
        scratch_shapes=[pltpu.VMEM((length + 2 * PAD, width), f32)],
        compiler_params=params(40),
        cost_estimate=cost(2e10, 8e6),
        name="front",
    )(x, maskc, wq, bq, dw)


def conv_taps(taps, pad, expand_ref, spread, out_ref, length):
    rows = 32
    block = 256
    inner = out_ref.shape[1]

    @pl.loop(0, length // block)
    def _(b):
        b0 = pl.multiple_of(b * block, block)
        for j in range(KERNEL):
            spread[:, j * inner : (j + 1) * inner] = mm(
                taps[pl.ds(b0, block), :], expand_ref[:, j * inner : (j + 1) * inner]
            )

        @pl.loop(0, block // rows)
        def _(i):
            r0 = pl.multiple_of(i * rows, rows)
            t0 = pl.multiple_of(b0 + r0, rows)
            for c in range(inner // LANES):
                cols = slice(c * LANES, (c + 1) * LANES)
                win = window(pad, t0, rows, cols)
                total = jnp.zeros((rows, LANES), f32)
                for j in range(KERNEL):
                    part = spread[pl.ds(r0, rows), j * inner + c * LANES : j * inner + (c + 1) * LANES]
                    total = total + part * moved(win, j - HALF, rows)
                out_ref[pl.ds(t0, rows), cols] = total.astype(bf16)


def taps_in_rows(low_taps, taps, length):
    stacked = jnp.concatenate(low_taps + [jnp.zeros((LANES - 8 * KERNEL, length), f32)], axis=0)
    for b in range(length // LANES):
        piece = stacked[:, b * LANES : (b + 1) * LANES]
        taps[b * LANES : (b + 1) * LANES, :] = jnp.transpose(piece).astype(bf16)


def mixers_body(
    place_ref, x_ref, q_ref, dl_ref, maskr_ref, own_ref, got_ref, got2_ref, bv_ref, bp_ref, bc_ref,
    kw_ref, kb_ref, expand_ref,
    k_ref, v_ref, kc_ref, cv_ref, probs_ref, mixed_ref, w_ref,
    pad, mixing, taps, spread,
):
    length = x_ref.shape[0]
    clear_pads(pad, length)
    side, core = place_ref[0], place_ref[1]
    for n in range(2):
        w_ref[2 * side + n] = own_ref[n]
    w_ref[2 - 2 * side + core] = got_ref[...]
    w_ref[3 - 2 * side - core] = got2_ref[...]

    @pl.loop(0, length // 256)
    def _(i):
        t0 = pl.multiple_of(i * 256, 256)
        now = pl.ds(t0, 256)
        x = x_ref[now, :]
        cv = (mm(x, w_ref[3]) + bc_ref[...]).astype(bf16)
        cv_ref[now, :] = cv
        pad[pl.ds(pl.multiple_of(t0 + PAD, 16), 256), :] = cv.astype(f32)
        kc = (mm(dl_ref[now, :], w_ref[2]) + bp_ref[...]).astype(bf16)
        kc_ref[now, :] = kc
        mixing[now, :] = (kc.astype(f32) * q_ref[now, :].astype(f32)).astype(bf16)
        k_ref[now, :] = mm(x, w_ref[0]).astype(bf16)
        v_ref[now, :] = (mm(x, w_ref[1]) + bv_ref[...]).astype(bf16)

    logits = mm_nt(kw_ref[...], mixing[...]) + kb_ref[:, 0:1]
    rows = [logits[8 * j : 8 * j + 8, :] for j in range(KERNEL)]
    peak = rows[0]
    for r in rows[1:]:
        peak = jnp.maximum(peak, r)
    powers = [jnp.exp(r - peak) for r in rows]
    whole = powers[0]
    for r in powers[1:]:
        whole = whole + r
    share = 1.0 / whole
    low_taps = []
    for j in range(KERNEL):
        probs = powers[j] * share
        probs_ref[8 * j : 8 * j + 8, :] = probs
        low_taps.append(probs.astype(bf16).astype(f32) * maskr_ref[j : j + 1, :])
    taps_in_rows(low_taps, taps, length)
    conv_taps(taps, pad, expand_ref, spread, mixed_ref, length)


def mixers(place, x, q, dl, maskr, own, got, got2, bv, bp, bc, kw, kb, expand):
    length, width = x.shape
    inner = q.shape[1]
    act = jax.ShapeDtypeStruct((length, inner), bf16)
    vm = pl.BlockSpec(memory_space=pltpu.VMEM)
    return pl.pallas_call(
        mixers_body,
        in_specs=[pl.BlockSpec(memory_space=pltpu.SMEM)] + [vm] * 13,
        out_specs=(vm,) * 7,
        out_shape=(
            act, act, act, act, jax.ShapeDtypeStruct((8 * KERNEL, length), f32), act,
            jax.ShapeDtypeStruct((4, width, inner), bf16),
        ),
        scratch_shapes=[
            pltpu.VMEM((length + 2 * PAD, inner), f32),
            pltpu.VMEM((length, inner), bf16),
            pltpu.VMEM((length, LANES), bf16),
            pltpu.VMEM((256, KERNEL * inner), f32),
        ],
        compiler_params=params(48),
        cost_estimate=cost(2e10, 1e7),
        name="mixers",
    )(place, x, q, dl, maskr, own, got, got2, bv, bp, bc, kw, kb, expand)


def head_lanes(shape, head):
    lane = lax.broadcasted_iota(jnp.int32, shape, 1)
    return (lane < HEAD) if head == 0 else (lane >= HEAD)


def only(pair, head):
    return jnp.where(head_lanes(pair.shape, head), pair, jnp.zeros_like(pair))


def attend_body(q_ref, k_ref, v_ref, segc_ref, o_ref, of_ref, lse_ref, kx, vx, qx):
    length = q_ref.shape[0]
    block = 256
    lane = lax.broadcasted_iota(jnp.int32, (length, LANES), 1)
    seg = segc_ref[:, 0:LANES]
    same = seg == lane
    qx[:, 0:LANES] = (q_ref[...].astype(f32) * SCALE).astype(bf16)
    qx[:, LANES:] = jnp.where(same, 1.0, 0.0).astype(bf16)
    other = jnp.where((lane < DOCS) & jnp.logical_not(same), BIG, 0.0).astype(bf16)
    for h in range(2):
        kx[h, :, 0:LANES] = only(k_ref[...].astype(f32), h).astype(bf16)
        kx[h, :, LANES:] = other
    vx[:, 0:LANES] = v_ref[...]
    vx[:, LANES:] = jnp.ones((length, LANES), bf16)

    @pl.loop(0, length // block)
    def _(i):
        t0 = pl.multiple_of(i * block, block)
        now = pl.ds(t0, block)
        outs, totals = [], []
        for h in range(2):
            scores = mm_nt(qx[now, :], kx[h])
            peak = jnp.max(scores, axis=-1, keepdims=True)
            powers = jnp.exp(scores - peak).astype(bf16)
            both = mm(powers, vx[...])
            whole = both[:, LANES:]
            outs.append(both[:, 0:LANES] / whole)
            totals.append(peak + jnp.log(whole))
        left = head_lanes((block, LANES), 0)
        out = jnp.where(left, outs[0], outs[1])
        of_ref[now, :] = out
        o_ref[now, :] = out.astype(bf16)
        lse_ref[now, :] = jnp.where(left, totals[0], totals[1])


def attend(q, k, v, segc):
    length, inner = q.shape
    pair = pl.BlockSpec((length, LANES), lambda p: (0, p))
    fixed = pl.BlockSpec((length, LANES), lambda p: (0, 0))
    return pl.pallas_call(
        attend_body,
        grid=(inner // LANES,),
        in_specs=[pair, pair, pair, fixed],
        out_specs=(pair, pair, pair),
        out_shape=(
            jax.ShapeDtypeStruct((length, inner), bf16),
            jax.ShapeDtypeStruct((length, inner), f32),
            jax.ShapeDtypeStruct((length, inner), f32),
        ),
        scratch_shapes=[
            pltpu.VMEM((2, length, 2 * LANES), bf16),
            pltpu.VMEM((length, 2 * LANES), bf16),
            pltpu.VMEM((length, 2 * LANES), bf16),
        ],
        compiler_params=params(40),
        cost_estimate=cost(2e10, 1e7),
        name="attend",
    )(q, k, v, segc)


def pieces(value):
    first = value.astype(bf16).astype(f32)
    rest = value - first
    second = rest.astype(bf16).astype(f32)
    return first, second, rest - second


def extra_lanes(base, values, lane):
    out = base
    for n, value in enumerate(values):
        out = jnp.where(lane == DOCS + n, value, out)
    return out


def attend_back_body(
    q_ref, k_ref, v_ref, do_ref, of_ref, lse_ref, segc_ref, dq_ref, dk_ref, dv_ref,
    kx, vx, qx, dx, kt, dk_sum, dv_sum,
):
    length = q_ref.shape[0]
    block = 256
    lane = lax.broadcasted_iota(jnp.int32, (length, LANES), 1)
    seg = segc_ref[:, 0:LANES]
    same = seg == lane
    q = q_ref[...].astype(f32) * SCALE
    k = k_ref[...].astype(f32)
    v = v_ref[...].astype(f32)
    do = do_ref[...].astype(f32)
    dots = do * of_ref[...]
    lses = lse_ref[...]
    here = jnp.where(same, 1.0, 0.0)
    other = jnp.where((lane < DOCS) & jnp.logical_not(same), BIG, 0.0)
    ones = jnp.where((lane >= DOCS) & (lane < DOCS + 3), 1.0, 0.0)
    for h in range(2):
        kx[h, :, 0:LANES] = only(k, h).astype(bf16)
        kx[h, :, LANES:] = (other + ones).astype(bf16)
        vx[h, :, 0:LANES] = only(v, h).astype(bf16)
        vx[h, :, LANES:] = ones.astype(bf16)
        qx[h, :, 0:LANES] = only(q, h).astype(bf16)
        minus = [-p for p in pieces(lses[:, h * HEAD : h * HEAD + 1])]
        qx[h, :, LANES:] = extra_lanes(here, minus, lane).astype(bf16)
        dx[h, :, 0:LANES] = only(do, h).astype(bf16)
        dot = jnp.sum(only(dots, h), axis=-1, keepdims=True)
        minus = [-p for p in pieces(dot)]
        dx[h, :, LANES:] = extra_lanes(jnp.zeros_like(here), minus, lane).astype(bf16)
        kt[h] = jnp.transpose(only(k, h)).astype(bf16)
    dk_sum[...] = jnp.zeros_like(dk_sum)
    dv_sum[...] = jnp.zeros_like(dv_sum)

    @pl.loop(0, length // block)
    def _(i):
        t0 = pl.multiple_of(i * block, block)
        now = pl.ds(t0, block)
        dq = jnp.zeros((LANES, block), f32)
        for h in range(2):
            for b in range(length // block):
                keys = slice(b * block, (b + 1) * block)
                probs = jnp.exp(mm_nt(kx[h, keys, :], qx[h, now, :]))
                grads = mm_nt(vx[h, keys, :], dx[h, now, :])
                score = (probs * grads).astype(bf16)
                dv_sum[keys, :] += mm(probs.astype(bf16), dx[h, now, 0:LANES])
                dk_sum[keys, :] += mm(score, qx[h, now, 0:LANES])
                dq = dq + mm(kt[h, :, keys], score)
        dq_ref[now, :] = jnp.transpose(dq) * SCALE

    dk_ref[...] = dk_sum[...].astype(bf16)
    dv_ref[...] = dv_sum[...].astype(bf16)


def attend_back(pair_no, q, k, v, do, of, lse, segc):
    length, inner = q.shape
    pair = pl.BlockSpec((length, LANES), lambda p: (0, pair_no))
    fixed = pl.BlockSpec((length, LANES), lambda p: (0, 0))
    wide = pltpu.VMEM((2, length, 2 * LANES), bf16)
    return pl.pallas_call(
        attend_back_body,
        grid=(1,),
        in_specs=[pair] * 6 + [fixed],
        out_specs=(fixed, fixed, fixed),
        out_shape=(
            jax.ShapeDtypeStruct((length, LANES), f32),
            jax.ShapeDtypeStruct((length, LANES), bf16),
            jax.ShapeDtypeStruct((length, LANES), bf16),
        ),
        scratch_shapes=[
            wide, wide, wide, wide,
            pltpu.VMEM((2, LANES, length), bf16),
            pltpu.VMEM((length, LANES), f32),
            pltpu.VMEM((length, LANES), f32),
        ],
        compiler_params=params(48),
        cost_estimate=cost(1.2e10, 4e6),
        name="attend_back",
    )(q, k, v, do, of, lse, segc)


def normal_cdf(value):
    power = jnp.exp(-0.5 * (value * value))
    size = jnp.abs(value)
    t = 1.0 / (1.0 + (0.3275911 * 0.7071067811865476) * size)
    poly = 1.061405429 * t - 1.453152027
    poly = poly * t + 1.421413741
    poly = poly * t - 0.284496736
    poly = poly * t + 0.254829592
    tail = (0.5 * poly) * (t * power)
    return jnp.where(value < 0.0, tail, 1.0 - tail), power * 0.3989422804014327


def row_mean(value):
    return jnp.mean(value, axis=-1, keepdims=True)


def fold(value):
    rows, width = value.shape
    return jnp.sum(value.reshape(rows // 8, 8, width), axis=0)


def slabs(count, rows, unroll, body):
    def step(i, carry):
        body(pl.ds(pl.multiple_of(i * rows, rows), rows))
        return carry

    lax.fori_loop(0, count // rows, step, 0, unroll=unroll)


def ffn_body(
    place_ref, at_ref, mx_ref, x_ref, cot_a_ref, cot_b_ref, wo_ref, bo_ref, g1_ref, s1_ref, wu_ref,
    bu_ref, wd_ref, bd_ref, g2_ref, s2_ref,
    act_own_ref, act_far_ref, res_ref, cg_ref, keep_ref, send_ref, small_ref,
    slope, active, up_grad, grouped, low_grad, hid_grad, joined, sums, up_sums, wide, norm, inverse,
):
    step = pl.program_id(0)
    block = at_ref.shape[0]
    blocks = active.shape[0] // block
    inner = at_ref.shape[1]
    width = x_ref.shape[1]
    part = width // GROUPS
    hidden = wu_ref.shape[2]
    chunk = 768
    rows, unroll = block, 1

    @pl.when(step == 0)
    def _():
        sums[...] = jnp.zeros_like(sums)
        up_sums[...] = jnp.zeros_like(up_sums)

    @pl.when(step < blocks)
    def _():
        t0 = pl.multiple_of(step * block, block)
        now = pl.ds(t0, block)
        own = step < blocks // 2
        joined[now, 0:inner] = at_ref[...]
        joined[now, inner:] = mx_ref[...]
        wide[...] = mm(joined[now, :], wo_ref[...])

        def first(slab):
            resid = x_ref[slab, :].astype(f32) + (wide[slab, :] + bo_ref[...])
            center = resid - row_mean(resid)
            inv = lax.rsqrt(row_mean(center * center) + EPS)
            inverse[slab, :] = jnp.broadcast_to(inv, (rows, LANES))
            normed = center * inv
            norm[slab, :] = normed
            grouped[pl.ds(pl.multiple_of(t0 + slab.start, rows), rows), :] = (
                normed * g1_ref[...] + s1_ref[...]
            ).astype(bf16)

        slabs(block, rows, unroll, first)

        for g in range(GROUPS):
            mine = slice(g * part, (g + 1) * part)
            low = None
            for c in range(hidden // chunk):
                cols = slice(c * chunk, (c + 1) * chunk)
                up = mm(grouped[now, mine], wu_ref[g, :, cols]) + bu_ref[g : g + 1, cols]
                cdf, density = normal_cdf(up)
                act = (up * cdf).astype(bf16)
                at = slice(g * hidden + c * chunk, g * hidden + (c + 1) * chunk)
                active[now, at] = act
                slope[:, at] = cdf + up * density
                add = mm(act, wd_ref[g, cols, :])
                low = add if low is None else low + add
            wide[:, mine] = low + bd_ref[g : g + 1, :]

        def second(slab):
            here = pl.ds(pl.multiple_of(t0 + slab.start, rows), rows)
            resid = (norm[slab, :] * g1_ref[...] + s1_ref[...]) + wide[slab, :]
            center = resid - row_mean(resid)
            inv = lax.rsqrt(row_mean(center * center) + EPS)
            normed = center * inv
            result = (normed * g2_ref[...] + s2_ref[...]).astype(bf16)
            hid_grad[here, :] = result
            grad = jnp.where(own, cot_a_ref[slab, :], cot_b_ref[slab, :]).astype(f32)
            sums[0:8, :] += fold(grad * normed)
            sums[8:16, :] += fold(grad)
            gs = grad * g2_ref[...]
            resid = inv * (gs - row_mean(gs) - normed * row_mean(gs * normed))
            wide[slab, :] = resid
            lg = resid.astype(bf16)
            low_grad[here, :] = lg
            sums[16:24, :] += fold(lg.astype(f32))

        slabs(block, rows, unroll, second)

        @pl.when(own)
        def _():
            act_own_ref[...] = hid_grad[now, :]

        @pl.when(jnp.logical_not(own))
        def _():
            act_far_ref[...] = hid_grad[now, :]

        for g in range(GROUPS):
            mine = slice(g * part, (g + 1) * part)
            back = None
            for c in range(hidden // chunk):
                cols = slice(c * chunk, (c + 1) * chunk)
                at = slice(g * hidden + c * chunk, g * hidden + (c + 1) * chunk)
                ag = mm_nt(low_grad[now, mine], wd_ref[g, cols, :])
                ug = (ag * slope[:, at]).astype(bf16)
                up_grad[now, at] = ug
                up_sums[:, at] += fold(ug.astype(f32))
                add = mm_nt(ug, wu_ref[g, :, cols])
                back = add if back is None else back + add
            wide[:, mine] += back

        def third(slab):
            here = pl.ds(pl.multiple_of(t0 + slab.start, rows), rows)
            grad = wide[slab, :]
            normed = norm[slab, :]
            inv = inverse[slab, 0:1]
            sums[24:32, :] += fold(grad * normed)
            sums[32:40, :] += fold(grad)
            gs = grad * g1_ref[...]
            resid = inv * (gs - row_mean(gs) - normed * row_mean(gs * normed))
            res_ref[slab, :] = resid
            hg = resid.astype(bf16)
            hid_grad[here, :] = hg
            sums[40:48, :] += fold(hg.astype(f32))

        slabs(block, rows, unroll, third)
        cg_ref[...] = mm_nt(hid_grad[now, :], wo_ref[...]).astype(bf16)

    per = hidden // 768

    def weight_grad(half, n):
        mine = slice(half * part, (half + 1) * part)
        if n < per:
            cols = slice(half * hidden + n * 768, half * hidden + (n + 1) * 768)
            return mm_tn(active[:, cols], low_grad[:, mine]).astype(bf16)
        if n < 2 * per:
            n -= per
            cols = slice(half * hidden + n * 768, half * hidden + (n + 1) * 768)
            value = mm_tn(grouped[:, mine], up_grad[:, cols]).astype(bf16)
        else:
            value = mm_tn(joined[:, mine], hid_grad[...]).astype(bf16)
        return jnp.concatenate([value[:, 0:part], value[:, part:]], axis=0)

    for n in range(2 * per + 1):

        @pl.when(step == blocks + n)
        def _():
            for half in range(2):
                store_half(
                    place_ref[1], half, keep_ref, send_ref, slice(None), weight_grad(half, n)
                )

    @pl.when(step == blocks)
    def _():
        across = width // 384
        small_ref[...] = jnp.zeros_like(small_ref)
        for n in range(6):
            line = jnp.sum(sums[8 * n : 8 * n + 8, :], axis=0, keepdims=True)
            for c in range(across):
                small_ref[across * n + c : across * n + c + 1, :] = line[:, c * 384 : (c + 1) * 384]
        line = jnp.sum(up_sums[...], axis=0, keepdims=True)
        for c in range(GROUPS * hidden // 384):
            at = 6 * across + c
            small_ref[at : at + 1, :] = line[:, c * 384 : (c + 1) * 384]


def store_half(core, half, keep_ref, send_ref, rows, value):
    @pl.when(core == half)
    def _():
        keep_ref[rows, :] = value

    @pl.when(core != half)
    def _():
        send_ref[rows, :] = value


def ffn(at, mx, x, cot, cot_far, place, wo, bo, g1, s1, wu, bu, wd, bd, g2, s2):
    length, width = x.shape
    inner = at.shape[1]
    block = length // 2
    blocks = length // block
    near = blocks // 2
    hidden = wu.shape[2]
    gsteps = 2 * (hidden // 768) + 1

    def turn(step, side_ref):
        s = jnp.minimum(step, blocks - 1)
        return (s + side_ref[0] * near) % blocks

    def tok(cols):
        return pl.BlockSpec((block, cols), lambda s, b: (turn(s, b), 0))

    def full(shape):
        return pl.BlockSpec(shape, lambda s, b: (0,) * len(shape), pipeline_mode=pl.Buffered(1))

    def near_map(s, b):
        return (jnp.minimum(s, near - 1), 0)

    def far_map(s, b):
        return (jnp.clip(s - near, 0, near - 1), 0)

    def cot_map(s, b):
        return (b[0], jnp.minimum(s, near - 1), 0)

    return pl.pallas_call(
        ffn_body,
        grid_spec=pltpu.PrefetchScalarGridSpec(
            num_scalar_prefetch=1,
            grid=(blocks + gsteps,),
            in_specs=[
                tok(inner), tok(inner), tok(width),
                pl.BlockSpec((None, block, width), cot_map),
                pl.BlockSpec((block, width), far_map),
                full(wo.shape), full(bo.shape), full(g1.shape), full(s1.shape), full(wu.shape),
                full(bu.shape), full(wd.shape), full(bd.shape), full(g2.shape), full(s2.shape),
            ],
            out_specs=(
                pl.BlockSpec((block, width), near_map),
                pl.BlockSpec((block, width), far_map),
                tok(width),
                tok(width),
                pl.BlockSpec((768, 384), lambda s, b: (jnp.maximum(s - blocks, 0), 0)),
                pl.BlockSpec((768, 384), lambda s, b: (jnp.maximum(s - blocks, 0), 0)),
                pl.BlockSpec((32, 384), lambda s, b: (0, 0)),
            ),
            scratch_shapes=[
                pltpu.VMEM((block, GROUPS * hidden), f32),
                pltpu.VMEM((length, GROUPS * hidden), bf16),
                pltpu.VMEM((length, GROUPS * hidden), bf16),
                pltpu.VMEM((length, width), bf16),
                pltpu.VMEM((length, width), bf16),
                pltpu.VMEM((length, width), bf16),
                pltpu.VMEM((length, width), bf16),
                pltpu.VMEM((48, width), f32),
                pltpu.VMEM((8, GROUPS * hidden), f32),
                pltpu.VMEM((block, width), f32),
                pltpu.VMEM((block, width), f32),
                pltpu.VMEM((block, LANES), f32),
            ],
        ),
        out_shape=(
            jax.ShapeDtypeStruct((length // 2, width), bf16),
            jax.ShapeDtypeStruct((length // 2, width), bf16),
            jax.ShapeDtypeStruct((length, width), f32),
            jax.ShapeDtypeStruct((length, width), bf16),
            jax.ShapeDtypeStruct((gsteps * 768, 384), bf16),
            jax.ShapeDtypeStruct((gsteps * 768, 384), bf16),
            jax.ShapeDtypeStruct((32, 384), f32),
        ),
        compiler_params=params(60),
        cost_estimate=cost(4e10, 3e7),
        name="ffn",
    )(place, at, mx, x, cot, cot_far, wo, bo, g1, s1, wu, bu, wd, bd, g2, s2)


def conv_back_body(
    q_ref, kc_ref, cv_ref, probs_ref, cg_ref, maskr_ref, w_ref, kw_ref, gather_ref,
    qc_ref, dg_ref, kcg, kwg_ref, small_ref,
    pad, prod, taps, kvg, sums,
):
    length, inner = q_ref.shape
    block, rows = 256, 32
    clear_pads(pad, length)

    @pl.loop(0, length // block)
    def _(i):
        t0 = pl.multiple_of(i * block, block)
        pad[pl.ds(pl.multiple_of(t0 + PAD, 16), block), :] = cv_ref[pl.ds(t0, block), :].astype(f32)

    tap_grads = []
    for b in range(length // block):

        @pl.loop(0, block // rows)
        def _(i):
            r0 = pl.multiple_of(i * rows, rows)
            t0 = pl.multiple_of(b * block + r0, rows)
            for c in range(inner // LANES):
                cols = slice(c * LANES, (c + 1) * LANES)
                win = window(pad, t0, rows, cols)
                mg = cg_ref[pl.ds(t0, rows), inner + c * LANES : inner + (c + 1) * LANES].astype(f32)
                for j in range(KERNEL):
                    prod[pl.ds(r0, rows), j * inner + c * LANES : j * inner + (c + 1) * LANES] = (
                        mg * moved(win, j - HALF, rows)
                    ).astype(bf16)

        tap_grads.append(jnp.transpose(mm(prod[...], gather_ref[...])))
    tap_grad = jnp.concatenate(tap_grads, axis=1)
    probs = [probs_ref[8 * j : 8 * j + 8, :] for j in range(KERNEL)]
    grads = [tap_grad[8 * j : 8 * j + 8, :] * maskr_ref[j : j + 1, :] for j in range(KERNEL)]
    dot = probs[0] * grads[0]
    for j in range(1, KERNEL):
        dot = dot + probs[j] * grads[j]
    rest = jnp.zeros((LANES - 8 * KERNEL, length), f32)
    logit = [(probs[j] * (grads[j] - dot)).astype(bf16).astype(f32) for j in range(KERNEL)]
    logit = jnp.concatenate(logit + [rest], axis=0)
    small_ref[...] = jnp.zeros_like(small_ref)
    for b in range(length // LANES):
        taps[b * LANES : (b + 1) * LANES, :] = jnp.transpose(
            logit[:, b * LANES : (b + 1) * LANES]
        ).astype(bf16)
    small_ref[0:1, 0:LANES] = jnp.sum(taps[...].astype(f32), axis=0, keepdims=True)
    sums[...] = jnp.zeros_like(sums)

    @pl.loop(0, length // block)
    def _(i):
        now = pl.ds(pl.multiple_of(i * block, block), block)
        mix_grad = mm(taps[now, :], kw_ref[...])
        q = q_ref[now, :].astype(f32)
        kc = kc_ref[now, :].astype(f32)
        low = (mix_grad * q).astype(bf16)
        kcg[now, :] = low
        kvg[now, :] = (kc * q).astype(bf16)
        sums[...] += fold(low.astype(f32))
        qc_ref[now, :] = mix_grad * kc
        dg_ref[now, :] = mm_nt(low, w_ref[2])

    kwg_ref[...] = mm_tn(taps[...], kvg[...]).astype(bf16)
    small_ref[1:2, :] = jnp.sum(sums[...], axis=0, keepdims=True)


def conv_back(q, kc, cv, probs, cg, maskr, weights, kw, gather):
    length, inner = q.shape
    width = cg.shape[1]
    return pl.pallas_call(
        conv_back_body,
        out_shape=(
            jax.ShapeDtypeStruct((length, inner), f32),
            jax.ShapeDtypeStruct((length, width), f32),
            jax.ShapeDtypeStruct((length, inner), bf16),
            jax.ShapeDtypeStruct((LANES, inner), bf16),
            jax.ShapeDtypeStruct((8, inner), f32),
        ),
        scratch_shapes=[
            pltpu.VMEM((length + 2 * PAD, inner), f32),
            pltpu.VMEM((256, KERNEL * inner), bf16),
            pltpu.VMEM((length, LANES), bf16),
            pltpu.VMEM((length, inner), bf16),
            pltpu.VMEM((8, inner), f32),
        ],
        compiler_params=params(48),
        cost_estimate=cost(1.2e10, 1e7),
        name="conv_back",
    )(q, kc, cv, probs, cg, maskr, weights, kw, gather)


def conv_values_body(
    place_ref, x_ref, dl_ref, kcg_ref, probs_ref, cg_ref, maskr_ref, expand_ref,
    vg_ref, kept_ref, sent_ref, small_ref,
    pad, taps, spread,
):
    length, width = x_ref.shape
    inner = kcg_ref.shape[1]
    block = 256
    clear_pads(pad, length)

    @pl.loop(0, length // block)
    def _(i):
        t0 = pl.multiple_of(i * block, block)
        pad[pl.ds(pl.multiple_of(t0 + PAD, 16), block), :] = cg_ref[
            pl.ds(t0, block), inner:
        ].astype(f32)

    low_taps = []
    for j in range(KERNEL):
        back = KERNEL - 1 - j
        low = probs_ref[8 * back : 8 * back + 8, :].astype(bf16).astype(f32)
        low = low * maskr_ref[back : back + 1, :]
        shift = (HALF - j) % length
        low_taps.append(pltpu.roll(low, shift, 1) if shift else low)
    taps_in_rows(low_taps, taps, length)
    conv_taps(taps, pad, expand_ref, spread, vg_ref, length)
    total = jnp.zeros((8, inner), f32)
    for i in range(length // block):
        total = total + fold(vg_ref[i * block : (i + 1) * block, :].astype(f32))
    small_ref[...] = jnp.zeros_like(small_ref)
    small_ref[0:1, :] = jnp.sum(total, axis=0, keepdims=True)
    core = place_ref[1]
    rows = slice(0, width)
    store_half(core, 0, kept_ref, sent_ref, rows, mm_tn(dl_ref[...], kcg_ref[...]).astype(bf16))
    store_half(core, 1, kept_ref, sent_ref, rows, mm_tn(x_ref[...], vg_ref[...]).astype(bf16))


def conv_values(place, x, dl, kcg, probs, cg, maskr, expand):
    length, width = x.shape
    inner = kcg.shape[1]
    vm = pl.BlockSpec(memory_space=pltpu.VMEM)
    return pl.pallas_call(
        conv_values_body,
        in_specs=[pl.BlockSpec(memory_space=pltpu.SMEM)] + [vm] * 7,
        out_specs=(vm,) * 4,
        out_shape=(
            jax.ShapeDtypeStruct((length, inner), bf16),
            jax.ShapeDtypeStruct((width + LANES, inner), bf16),
            jax.ShapeDtypeStruct((width + LANES, inner), bf16),
            jax.ShapeDtypeStruct((8, inner), f32),
        ),
        scratch_shapes=[
            pltpu.VMEM((length + 2 * PAD, inner), f32),
            pltpu.VMEM((length, LANES), bf16),
            pltpu.VMEM((256, KERNEL * inner), f32),
        ],
        compiler_params=params(48),
        cost_estimate=cost(1.2e10, 1e7),
        name="conv_values",
    )(place, x, dl, kcg, probs, cg, maskr, expand)


def depth_back_body(
    place_ref, x_ref, dg_ref, maskc_ref, dw_ref, kwg_ref, sf_ref, sc_ref, sv_ref, sw_ref,
    kept_ref, sent_ref, dx_ref, keep_ref, send_ref, gpad, dkg,
):
    length, width = x_ref.shape
    block, rows = 256, 32
    clear_pads(gpad, length)
    dkg[...] = jnp.zeros_like(dkg)

    @pl.loop(0, length // block)
    def _(i):
        t0 = pl.multiple_of(i * block, block)
        gpad[pl.ds(pl.multiple_of(t0 + PAD, 16), block), :] = dg_ref[pl.ds(t0, block), :]

    @pl.loop(0, length // rows)
    def _(i):
        t0 = pl.multiple_of(i * rows, rows)
        mask = maskc_ref[pl.ds(t0, rows), :]
        masks = [jnp.broadcast_to(mask[:, j : j + 1], (rows, LANES)) for j in range(KERNEL)]
        for c in range(width // LANES):
            cols = slice(c * LANES, (c + 1) * LANES)
            win = window(gpad, t0, rows, cols)
            x = x_ref[pl.ds(t0, rows), cols].astype(f32)
            total = jnp.zeros((rows, LANES), f32)
            for j in range(KERNEL):
                back = KERNEL - 1 - j
                part = moved(win, j - HALF, rows) * masks[j]
                total = total + dw_ref[back : back + 1, cols] * part
                dkg[8 * back : 8 * back + 8, cols] += fold(part * x)
            dx_ref[pl.ds(t0, rows), cols] = total

    across = width // 384
    lines = []
    for j in range(KERNEL):
        line = jnp.sum(dkg[8 * j : 8 * j + 8, :], axis=0, keepdims=True)
        lines += [line[:, c * 384 : (c + 1) * 384] for c in range(across)]
    smalls = [sf_ref[...], sc_ref[...], sv_ref[...], sw_ref[...]] + lines
    used = sum(v.shape[0] for v in smalls)
    smalls = jnp.concatenate(smalls + [jnp.zeros((LANES - used, 384), f32)], axis=0)
    core = place_ref[1]
    keep_ref[0:width, :] = kept_ref[0:width, :]
    send_ref[0:width, :] = sent_ref[0:width, :]
    rows = slice(width, width + LANES)
    store_half(core, 0, keep_ref, send_ref, rows, kwg_ref[...])
    store_half(core, 1, keep_ref, send_ref, rows, smalls.astype(bf16))


def depth_back(place, x, dg, maskc, dw, kwg, sf, sc, sv, sw, kept, sent):
    length, width = x.shape
    vm = pl.BlockSpec(memory_space=pltpu.VMEM)
    return pl.pallas_call(
        depth_back_body,
        in_specs=[pl.BlockSpec(memory_space=pltpu.SMEM)] + [vm] * 11,
        out_specs=(vm,) * 3,
        out_shape=(
            jax.ShapeDtypeStruct((length, width), f32),
            jax.ShapeDtypeStruct(kept.shape, bf16),
            jax.ShapeDtypeStruct(kept.shape, bf16),
        ),
        scratch_shapes=[
            pltpu.VMEM((length + 2 * PAD, width), f32),
            pltpu.VMEM((8 * KERNEL, width), f32),
        ],
        compiler_params=params(40),
        cost_estimate=cost(1.2e10, 1e7),
        name="depth_back",
    )(place, x, dg, maskc, dw, kwg, sf, sc, sv, sw, kept, sent)


def wgrad_body(
    place_ref, x_ref, *refs
):
    pairs = 3
    dqs, dks, dvs = refs[0:pairs], refs[pairs : 2 * pairs], refs[2 * pairs : 3 * pairs]
    qc_ref, keep_ref, send_ref, dqkv_ref, small_ref = refs[3 * pairs :]
    length, width = x_ref.shape
    inner = qc_ref.shape[1]
    for p in range(pairs):
        cols = slice(p * LANES, (p + 1) * LANES)
        dqkv_ref[:, cols] = (dqs[p][...] + qc_ref[:, cols]).astype(bf16)
        dqkv_ref[:, inner + p * LANES : inner + (p + 1) * LANES] = dks[p][...]
        dqkv_ref[:, 2 * inner + p * LANES : 2 * inner + (p + 1) * LANES] = dvs[p][...]
    core = place_ref[1]
    step = 384
    count = 3 * (width // step)
    for n in range(count):
        which, piece = divmod(n, width // step)
        value = mm_tn(
            x_ref[:, piece * step : (piece + 1) * step],
            dqkv_ref[:, which * inner : (which + 1) * inner],
        ).astype(bf16)
        half, at = divmod(n, count // 2)
        store_half(core, half, keep_ref, send_ref, slice(at * step, (at + 1) * step), value)
    total = jnp.zeros((8, 3 * inner), f32)
    for i in range(length // 256):
        total = total + fold(dqkv_ref[i * 256 : (i + 1) * 256, :].astype(f32))
    line = jnp.sum(total, axis=0, keepdims=True)
    small_ref[...] = jnp.zeros_like(small_ref)
    for which in range(3):
        small_ref[which : which + 1, :] = line[:, which * inner : (which + 1) * inner]


def wgrad(place, x, dqs, dks, dvs, qc):
    length, width = x.shape
    inner = qc.shape[1]
    rows = 3 * width // 2
    vm = pl.BlockSpec(memory_space=pltpu.VMEM)
    return pl.pallas_call(
        wgrad_body,
        in_specs=[pl.BlockSpec(memory_space=pltpu.SMEM)] + [vm] * 11,
        out_specs=(vm,) * 4,
        out_shape=(
            jax.ShapeDtypeStruct((rows, inner), bf16),
            jax.ShapeDtypeStruct((rows, inner), bf16),
            jax.ShapeDtypeStruct((length, 3 * inner), bf16),
            jax.ShapeDtypeStruct((8, inner), f32),
        ),
        compiler_params=params(40),
        cost_estimate=cost(6e9, 1e7),
        name="wgrad",
    )(place, x, *dqs, *dks, *dvs, qc)


def xgrad_body(place_ref, dqkv_ref, vg_ref, dxd_ref, res_ref, wq_ref, w_ref, out_ref):
    inner = vg_ref.shape[1]
    total = res_ref[...] + dxd_ref[...]
    total = total + mm_nt(vg_ref[...], w_ref[3])
    total = total + mm_nt(dqkv_ref[:, 0:inner], wq_ref[...])
    total = total + mm_nt(dqkv_ref[:, inner : 2 * inner], w_ref[0])
    total = total + mm_nt(dqkv_ref[:, 2 * inner :], w_ref[1])
    out_ref[...] = total.astype(out_ref.dtype)


def xgrad(place, far, dqkv, vg, dxd, res, wq, weights):
    length, width = res.shape
    inner = vg.shape[1]
    block = 256
    near = length // 2 // block

    def tok(cols):
        def index(s, b):
            half = 1 - b[0] if far else b[0]
            return (half * near + s, 0)

        return pl.BlockSpec((block, cols), index)

    def full(shape):
        return pl.BlockSpec(shape, lambda s, b: (0,) * len(shape), pipeline_mode=pl.Buffered(1))

    return pl.pallas_call(
        xgrad_body,
        grid_spec=pltpu.PrefetchScalarGridSpec(
            num_scalar_prefetch=1,
            grid=(near,),
            in_specs=[
                tok(3 * inner), tok(inner), tok(width), tok(width), full(wq.shape),
                full(weights.shape),
            ],
            out_specs=pl.BlockSpec((block, width), lambda s, b: (s, 0)),
        ),
        out_shape=jax.ShapeDtypeStruct((length // 2, width), bf16 if far else f32),
        compiler_params=params(40),
        cost_estimate=cost(3e9, 8e6),
        name="xgrad_far" if far else "xgrad_own",
    )(place, dqkv, vg, dxd, res, wq, weights)


def unpack_ffn_body(place_ref, mine_ref, got_ref, down_ref, up_ref, out_ref):
    step = pl.program_id(0)
    per = pl.num_programs(0) // 2
    own = step // per == place_ref[1]
    value = jnp.where(own, mine_ref[...], got_ref[...]).astype(f32)
    n = step % per
    half = value.shape[0] // 2

    @pl.when(n < per // 2)
    def _():
        down_ref[...] = value

    @pl.when((n >= per // 2) & (n < per - 1))
    def _():
        up_ref[:, 0:384] = value[:half]
        up_ref[:, 384:] = value[half:]

    @pl.when(n == per - 1)
    def _():
        out_ref[:, 0:384] = value[:half]
        out_ref[:, 384:] = value[half:]


def unpack_ffn(place, mine, got, hidden):
    rows, part = mine.shape
    per = rows // 768
    each = per // 2

    def source(half_of):
        def index(s, b):
            half = b[1] if half_of else 1 - b[1]
            return (jnp.clip(s - per * half, 0, per - 1), 0)

        return pl.BlockSpec((768, part), index)

    return pl.pallas_call(
        unpack_ffn_body,
        grid_spec=pltpu.PrefetchScalarGridSpec(
            num_scalar_prefetch=1,
            grid=(2 * per,),
            in_specs=[source(True), source(False)],
            out_specs=(
                pl.BlockSpec(
                    (768, part), lambda s, b: (each * (s // per) + jnp.minimum(s % per, each - 1), 0)
                ),
                pl.BlockSpec(
                    (None, part, 768),
                    lambda s, b: (s // per, 0, jnp.clip(s % per - each, 0, each - 1)),
                ),
                pl.BlockSpec((part, 2 * part), lambda s, b: (s // per, 0)),
            ),
        ),
        out_shape=(
            jax.ShapeDtypeStruct((GROUPS * hidden, part), f32),
            jax.ShapeDtypeStruct((GROUPS, part, hidden), f32),
            jax.ShapeDtypeStruct((2 * part, 2 * part), f32),
        ),
        compiler_params=params(32),
        cost_estimate=cost(1e6, 2e7),
        name="unpack_ffn",
    )(place, mine, got)


def unpack_mixers_body(place_ref, cm_ref, cg_ref, am_ref, ag_ref, query_ref, stack_ref):
    width = query_ref.shape[0]
    half = width // 2
    for core in range(2):

        @pl.when(place_ref[1] == core)
        def _():
            conv = (cm_ref, cg_ref) if core == 0 else (cg_ref, cm_ref)
            rest = (am_ref, ag_ref) if core == 0 else (ag_ref, am_ref)
            query_ref[...] = rest[0][0:width, :].astype(f32)

            @pl.when(place_ref[0] == 0)
            def _():
                stack_ref[0, 0:half, :] = rest[0][width:, :].astype(f32)
                stack_ref[0, half:, :] = rest[1][0:half, :].astype(f32)
                stack_ref[1] = rest[1][half:, :].astype(f32)

            @pl.when(place_ref[0] != 0)
            def _():
                stack_ref[0] = conv[0][0:width, :].astype(f32)
                stack_ref[1] = conv[1][0:width, :].astype(f32)


def unpack_mixers(place, conv_mine, conv_got, mine, got):
    inner = conv_mine.shape[1]
    width = mine.shape[0] * 2 // 3
    vm = pl.BlockSpec(memory_space=pltpu.VMEM)
    return pl.pallas_call(
        unpack_mixers_body,
        in_specs=[pl.BlockSpec(memory_space=pltpu.SMEM)] + [vm] * 4,
        out_specs=(vm, vm),
        out_shape=(
            jax.ShapeDtypeStruct((width, inner), f32),
            jax.ShapeDtypeStruct((2, width, inner), f32),
        ),
        compiler_params=params(32),
        cost_estimate=cost(1e6, 8e6),
        name="unpack_mixers",
    )(place, conv_mine, conv_got, mine, got)


AXES = ("branch", "dp")


def joint(value, count, masks):
    return lax.ppermute(value, AXES, [(i, i ^ masks[i & 1]) for i in range(count)])


class Sum:
    def __init__(self, kept, sent, index, count, plan):
        self.index, self.count = index, count
        self.plan = [[(1, 1)]] + plan
        self.depth = 0
        self.value, self.sent = kept, [sent]
        self.got = None
        self.down = True

    def hops(self):
        first = self.plan[self.depth]
        if len(first) == 1:
            return first
        (a, b), (c, d) = first
        return [(a, b), (c, d), (a ^ c, b ^ d)]

    def spot(self):
        at = jnp.int32(0)
        for n, masks in enumerate(self.plan[self.depth]):
            mask = jnp.where(self.index % 2 == 0, masks[0], masks[1])
            at = at + jnp.where((self.index & mask) != 0, 1 << n, 0)
        return at

    def start(self):
        sent = self.sent if self.down else [self.value] * 3
        self.got = [joint(v, self.count, masks) for v, masks in zip(sent, self.hops())]

    def finish(self):
        got, self.got = self.got, None
        if self.down:
            total = [self.value] + got
            if self.depth + 1 == len(self.plan):
                self.value, self.sent = added(total), []
                self.down = False
                return
            self.depth += 1
            spot = self.spot()
            ways = len(self.hops()) + 1
            rows = self.value.shape[0] // ways
            pieces = []
            for k in range(ways):
                at = (spot ^ k) * rows
                pieces.append(added([lax.dynamic_slice_in_dim(v, at, rows, 0) for v in total]))
            self.value, self.sent = pieces[0], pieces[1:]
            return
        spot = self.spot()
        rows = self.value.shape[0]
        if len(got) == 1:
            first = spot == 0
            self.value = jnp.concatenate(
                [jnp.where(first, self.value, got[0]), jnp.where(first, got[0], self.value)]
            )
        else:
            whole = jnp.zeros((4 * rows, self.value.shape[1]), self.value.dtype)
            for k, piece in enumerate([self.value] + got):
                whole = lax.dynamic_update_slice_in_dim(whole, piece, (spot ^ k) * rows, 0)
            self.value = whole
        self.depth -= 1

    @property
    def last(self):
        return not self.down and self.depth == 0

    def live(self):
        return [self.value] + self.sent

    def put(self, values):
        self.value, self.sent = values[0], list(values[1:])

    def halves(self):
        while True:
            if self.got is None:
                self.start()
            if self.last:
                return self.value, self.got[0]
            self.finish()


def added(values):
    total = values[0].astype(f32)
    for v in values[1:]:
        total = total + v.astype(f32)
    return total.astype(bf16)


def tick(finish, start, held=()):
    for chain in finish:
        if chain.got is not None and not chain.last:
            chain.finish()
    chains = [chain for chain in dict.fromkeys(list(finish) + list(start)) if chain.got is None]
    flat = [v for chain in chains for v in chain.live()]
    tied = lax.optimization_barrier(tuple(flat) + tuple(held))
    at = 0
    for chain in chains:
        n = len(chain.live())
        chain.put(tied[at : at + n])
        at += n
    for chain in start:
        if chain.got is None:
            chain.start()
    return tied[at:]


def local(sizes):
    branches, ranks = sizes["branch"], sizes["dp"]
    count = branches * ranks
    bits = []
    while (2 << len(bits)) < ranks:
        bits.append(2 << len(bits))
    along = ranks
    far = [[(b, b) for b in bits[n : n + 2]] for n in range(1, len(bits), 2)]
    pairs = [[(bits[0], along)], [(along, bits[0])]] + far
    fours = [[(along, along), (bits[0], bits[0])]] + far

    def run(
        inputs, segments, query_weight, query_bias, branch_weights, value_bias, depthwise,
        point_bias, kernel_weight, kernel_bias, conv_bias, output_weight, output_bias, first_gain,
        first_shift, up_weight, up_bias, down_weight, down_bias, second_gain, second_shift,
        cotangent,
    ):
        seqs, length, width = inputs.shape
        inner = query_weight.shape[1]
        hidden = up_weight.shape[2]
        part = width // GROUPS
        side = lax.axis_index("branch").astype(jnp.int32)
        rank = lax.axis_index("dp").astype(jnp.int32)
        core = rank % 2
        index = side * ranks + rank
        place = jnp.stack([side, core])
        first = side == 0

        def across(value):
            return joint(value, count, (along, along))

        got = across(lax.dynamic_index_in_dim(branch_weights[0], core, 0, keepdims=False))
        x = lax.dynamic_index_in_dim(inputs, side, 0, keepdims=False)
        seg = lax.dynamic_index_in_dim(segments, side, 0, keepdims=False)

        spots = jnp.arange(length)
        around = spots[None, :] + (jnp.arange(KERNEL) - HALF)[:, None]
        inside = (around >= 0) & (around < length)
        padded = jnp.pad(seg, (HALF, HALF), constant_values=-1)
        near = jnp.stack([lax.slice_in_dim(padded, j, j + length) for j in range(KERNEL)])
        maskr = ((near == seg[None, :]) & inside).astype(f32)
        maskr = jnp.pad(maskr, ((0, 16 - KERNEL), (0, 0)))
        maskc = maskr.T
        segc = jnp.broadcast_to(seg[:, None], (length, LANES))

        kw = kernel_weight.reshape(inner, HEADS, KERNEL).transpose(2, 1, 0)
        kw = jnp.pad(kw, ((0, 0), (0, 8 - HEADS), (0, 0))).reshape(8 * KERNEL, inner)
        kw_wide = jnp.pad(kw, ((0, LANES - 8 * KERNEL), (0, 0)))
        kb = kernel_bias.reshape(HEADS, KERNEL).T
        kb = jnp.pad(kb, ((0, 0), (0, 8 - HEADS))).reshape(8 * KERNEL, 1)
        kb = jnp.broadcast_to(kb, (8 * KERNEL, LANES))

        lane = jnp.arange(KERNEL * inner)
        slot = (lane // inner) * 8 + (lane % inner) // HEAD
        expand = (jnp.arange(LANES)[:, None] == slot[None, :]).astype(bf16)
        gather = (slot[:, None] == jnp.arange(LANES)[None, :]).astype(bf16)

        q, dl = front(x, maskc, query_weight, query_bias[None], depthwise)
        cot_sent = lax.dynamic_index_in_dim(cotangent, 1 - side, 0, keepdims=False)
        got, cot_sent = lax.optimization_barrier((got, cot_sent))
        got2 = joint(got, count, (1, 1))
        cot_far = across(cot_sent)
        k, v, kc, cv, probs, mixed, weights = mixers(
            place, x, q, dl, maskr, branch_weights[0], got, got2, value_bias[None],
            point_bias[None], conv_bias[None], kw, kb, expand,
        )
        attended, attended_f, lse = attend(q, k, v, segc)

        act_own, act_far, resid, cg, keep, send, small_f = ffn(
            attended, mixed, x, cotangent, cot_far, place, output_weight, output_bias[None],
            first_gain[None], first_shift[None], up_weight, up_bias, down_weight,
            down_bias, second_gain[None], second_shift[None],
        )
        ffn_sum = Sum(keep, send, index, count, pairs)
        (cg,) = tick([], [ffn_sum], [cg])
        act_got = across(act_far)
        qc, dg, kcg, kwg, small_c = conv_back(
            q, kc, cv, probs, cg, maskr, weights, kw_wide, gather
        )
        cg, qc = tick([ffn_sum], [ffn_sum], [cg, qc])
        back = []
        for pair in range(inner // LANES):
            out = attend_back(pair, q, k, v, cg, attended_f, lse, segc)
            if pair == 0:
                cg, *out = lax.optimization_barrier((cg, *out))
            else:
                cg, act_got, *out = tick([ffn_sum], [ffn_sum], [cg, act_got, *out])
            back.append(tuple(out))
        dqs, dks, dvs = zip(*back)
        keep, send, dqkv, small_w = wgrad(place, x, dqs, dks, dvs, qc)
        last_sum = Sum(keep, send, index, count, fours)
        (kcg,) = tick([], [last_sum], [kcg])
        vg, keep, send, small_v = conv_values(place, x, dl, kcg, probs, cg, maskr, expand)
        dg, vg = tick([last_sum], [last_sum], [dg, vg])
        dxd, keep, send = depth_back(
            place, x, dg, maskc, depthwise, kwg, small_f, small_c, small_v, small_w, keep, send
        )
        conv_sum = Sum(keep, send, index, count, fours)
        (dxd,) = tick([ffn_sum], [ffn_sum, conv_sum], [dxd])
        far = xgrad(place, True, dqkv, vg, dxd, resid, query_weight, weights)
        dxd, far = lax.optimization_barrier((dxd, far))
        grad_got = across(far)
        own = xgrad(place, False, dqkv, vg, dxd, resid, query_weight, weights)
        (own,) = tick([last_sum, conv_sum], [last_sum, conv_sum], [own])
        activations = jnp.stack(
            [jnp.where(first, act_own, act_got), jnp.where(first, act_got, act_own)]
        )
        grad_got, activations = tick([last_sum], [last_sum], [grad_got, activations])
        grad_far = grad_got.astype(f32)
        input_grad = jnp.stack([jnp.where(first, own, grad_far), jnp.where(first, grad_far, own)])
        (input_grad,) = tick([ffn_sum, conv_sum], [ffn_sum, conv_sum], [input_grad])
        tick([last_sum, conv_sum], [last_sum, conv_sum])
        tick([ffn_sum, conv_sum], [ffn_sum, conv_sum])
        tick([last_sum], [last_sum])
        tick([ffn_sum, conv_sum], [ffn_sum, conv_sum])

        last_halves = last_sum.halves()
        conv_halves = conv_sum.halves()
        small_mine, small_got = (v[width:] for v in conv_halves)
        query_grad, stack = unpack_mixers(place, *conv_halves, *last_halves)
        ffn_halves = ffn_sum.halves()
        down, up, out = unpack_ffn(place, *ffn_halves, hidden)
        down = down.reshape(GROUPS, hidden, part)

        even = core == 0
        kernel_grad = jnp.where(even, small_mine, small_got).astype(f32)
        small = jnp.where(even, small_got, small_mine).astype(f32)
        kernel_grad = kernel_grad[: 8 * KERNEL].reshape(KERNEL, 8, inner)[:, :HEADS]
        kernel_grad = kernel_grad.transpose(2, 1, 0).reshape(inner, HEADS * KERNEL)
        lines = width // inner
        smalls = small[: 6 * lines].reshape(6, width)
        up_bias_grad = small[6 * lines : 6 * lines + GROUPS * hidden // inner]
        up_bias_grad = up_bias_grad.reshape(GROUPS, hidden)
        kb_grad, point_bias_grad, conv_bias_grad = small[32], small[33], small[40]
        query_bias_grad, value_bias_grad = small[48], small[50]
        depth_grad = small[56 : 56 + KERNEL * lines].reshape(KERNEL, width)
        kb_grad = kb_grad[: 8 * KERNEL].reshape(KERNEL, 8)[:, :HEADS].T.reshape(-1)

        return (
            activations, input_grad, query_grad, query_bias_grad, stack[None],
            value_bias_grad, depth_grad, point_bias_grad, kernel_grad, kb_grad,
            conv_bias_grad, out, smalls[5], smalls[3], smalls[4], up, up_bias_grad, down,
            smalls[2].reshape(GROUPS, part), smalls[0], smalls[1],
        )

    return run


def solution(mesh):
    whole = P()
    tokens = P("dp", "branch", None)
    stack = P("branch", None, None, None)
    placed = (
        (P("dp", None, None), P("dp", None), whole, whole, stack) + (whole,) * 16 + (tokens,)
    )
    return jax.shard_map(
        local(dict(mesh.shape)),
        mesh=mesh,
        in_specs=placed,
        out_specs=(tokens, tokens, whole, whole, stack) + (whole,) * 16,
        check_vma=False,
    )
```

```python
import jax
import jax.numpy as jnp
from jax import lax
from jax.experimental import pallas as pl
from jax.experimental.pallas import tpu as pltpu
from jax.sharding import Mesh
from jax.sharding import PartitionSpec as P

HEADS = 6
HEAD = 64
KERNEL = 9
HALF = KERNEL // 2
GROUPS = 2
DOCS = 8
EPS = 1e-12
BIG = -1e30
SCALE = HEAD**-0.5

PAD = 16
SLOTS = 10
LANES = 128
f32 = jnp.float32
bf16 = jnp.bfloat16


def mm(a, b):
    return jnp.dot(a, b, preferred_element_type=f32)


def mm_nt(a, b):
    return lax.dot_general(a, b, (((1,), (1,)), ((), ())), preferred_element_type=f32)


def mm_tn(a, b):
    return lax.dot_general(a, b, (((0,), (0,)), ((), ())), preferred_element_type=f32)


def params(mib):
    return pltpu.CompilerParams(vmem_limit_bytes=mib * 1024 * 1024)


def cost(flops, nbytes):
    return pl.CostEstimate(flops=int(flops), bytes_accessed=int(nbytes), transcendentals=0)


def window(ref, start, rows, cols):
    return ref[pl.ds(pl.multiple_of(start + PAD - 8, 8), rows + 16), cols]


def moved(win, offset, rows):
    total = rows + 16
    if offset == 0:
        return win[8 : 8 + rows]
    return pltpu.roll(win, (-offset) % total, 0)[8 : 8 + rows]


def clear_pads(ref, length):
    width = ref.shape[1]
    ref[0:PAD, :] = jnp.zeros((PAD, width), f32)
    ref[PAD + length : PAD + length + PAD, :] = jnp.zeros((PAD, width), f32)


def front_body(x_ref, maskc_ref, wq_ref, bq_ref, dw_ref, q_ref, dl_ref, pad):
    length, width = x_ref.shape
    clear_pads(pad, length)
    rows = 32

    @pl.loop(0, length // 128)
    def _(i):
        t0 = pl.multiple_of(i * 128, 128)
        pad[pl.ds(pl.multiple_of(t0 + PAD, 16), 128), :] = x_ref[pl.ds(t0, 128), :].astype(f32)

    @pl.loop(0, length // 256)
    def _(i):
        t0 = pl.multiple_of(i * 256, 256)
        q_ref[pl.ds(t0, 256), :] = (mm(x_ref[pl.ds(t0, 256), :], wq_ref[...]) + bq_ref[...]).astype(
            bf16
        )

    @pl.loop(0, length // rows)
    def _(i):
        t0 = pl.multiple_of(i * rows, rows)
        mask = maskc_ref[pl.ds(t0, rows), :]
        masks = [jnp.broadcast_to(mask[:, j : j + 1], (rows, LANES)) for j in range(KERNEL)]
        for c in range(width // LANES):
            cols = slice(c * LANES, (c + 1) * LANES)
            win = window(pad, t0, rows, cols)
            total = jnp.zeros((rows, LANES), f32)
            for j in range(KERNEL):
                total = total + dw_ref[j : j + 1, cols] * moved(win, j - HALF, rows) * masks[j]
            dl_ref[pl.ds(t0, rows), cols] = total.astype(bf16)


def front(x, maskc, wq, bq, dw):
    length, width = x.shape
    inner = wq.shape[1]
    return pl.pallas_call(
        front_body,
        out_shape=(
            jax.ShapeDtypeStruct((length, inner), bf16),
            jax.ShapeDtypeStruct((length, width), bf16),
        ),
        scratch_shapes=[pltpu.VMEM((length + 2 * PAD, width), f32)],
        compiler_params=params(40),
        cost_estimate=cost(2e10, 8e6),
        name="front",
    )(x, maskc, wq, bq, dw)


def conv_taps(taps, pad, expand_ref, spread, out_ref, length):
    rows = 32
    block = 256
    inner = out_ref.shape[1]

    @pl.loop(0, length // block)
    def _(b):
        b0 = pl.multiple_of(b * block, block)
        for j in range(KERNEL):
            spread[:, j * inner : (j + 1) * inner] = mm(
                taps[pl.ds(b0, block), :], expand_ref[:, j * inner : (j + 1) * inner]
            )

        @pl.loop(0, block // rows)
        def _(i):
            r0 = pl.multiple_of(i * rows, rows)
            t0 = pl.multiple_of(b0 + r0, rows)
            for c in range(inner // LANES):
                cols = slice(c * LANES, (c + 1) * LANES)
                win = window(pad, t0, rows, cols)
                total = jnp.zeros((rows, LANES), f32)
                for j in range(KERNEL):
                    part = spread[pl.ds(r0, rows), j * inner + c * LANES : j * inner + (c + 1) * LANES]
                    total = total + part * moved(win, j - HALF, rows)
                out_ref[pl.ds(t0, rows), cols] = total.astype(bf16)


def taps_in_rows(low_taps, taps, length):
    stacked = jnp.concatenate(low_taps + [jnp.zeros((LANES - 8 * KERNEL, length), f32)], axis=0)
    for b in range(length // LANES):
        piece = stacked[:, b * LANES : (b + 1) * LANES]
        taps[b * LANES : (b + 1) * LANES, :] = jnp.transpose(piece).astype(bf16)


def mixers_body(
    place_ref, x_ref, q_ref, dl_ref, maskr_ref, own_ref, got_ref, got2_ref, bv_ref, bp_ref, bc_ref,
    kw_ref, kb_ref, expand_ref,
    k_ref, v_ref, kc_ref, cv_ref, probs_ref, mixed_ref, w_ref,
    pad, mixing, taps, spread,
):
    length = x_ref.shape[0]
    clear_pads(pad, length)
    side, core = place_ref[0], place_ref[1]
    for n in range(2):
        w_ref[2 * side + n] = own_ref[n]
    w_ref[2 - 2 * side + core] = got_ref[...]
    w_ref[3 - 2 * side - core] = got2_ref[...]

    @pl.loop(0, length // 256)
    def _(i):
        t0 = pl.multiple_of(i * 256, 256)
        now = pl.ds(t0, 256)
        x = x_ref[now, :]
        cv = (mm(x, w_ref[3]) + bc_ref[...]).astype(bf16)
        cv_ref[now, :] = cv
        pad[pl.ds(pl.multiple_of(t0 + PAD, 16), 256), :] = cv.astype(f32)
        kc = (mm(dl_ref[now, :], w_ref[2]) + bp_ref[...]).astype(bf16)
        kc_ref[now, :] = kc
        mixing[now, :] = (kc.astype(f32) * q_ref[now, :].astype(f32)).astype(bf16)
        k_ref[now, :] = mm(x, w_ref[0]).astype(bf16)
        v_ref[now, :] = (mm(x, w_ref[1]) + bv_ref[...]).astype(bf16)

    logits = mm_nt(kw_ref[...], mixing[...]) + kb_ref[:, 0:1]
    rows = [logits[8 * j : 8 * j + 8, :] for j in range(KERNEL)]
    peak = rows[0]
    for r in rows[1:]:
        peak = jnp.maximum(peak, r)
    powers = [jnp.exp(r - peak) for r in rows]
    whole = powers[0]
    for r in powers[1:]:
        whole = whole + r
    share = 1.0 / whole
    low_taps = []
    for j in range(KERNEL):
        probs = powers[j] * share
        probs_ref[8 * j : 8 * j + 8, :] = probs
        low_taps.append(probs.astype(bf16).astype(f32) * maskr_ref[j : j + 1, :])
    taps_in_rows(low_taps, taps, length)
    conv_taps(taps, pad, expand_ref, spread, mixed_ref, length)


def mixers(place, x, q, dl, maskr, own, got, got2, bv, bp, bc, kw, kb, expand):
    length, width = x.shape
    inner = q.shape[1]
    act = jax.ShapeDtypeStruct((length, inner), bf16)
    vm = pl.BlockSpec(memory_space=pltpu.VMEM)
    return pl.pallas_call(
        mixers_body,
        in_specs=[pl.BlockSpec(memory_space=pltpu.SMEM)] + [vm] * 13,
        out_specs=(vm,) * 7,
        out_shape=(
            act, act, act, act, jax.ShapeDtypeStruct((8 * KERNEL, length), f32), act,
            jax.ShapeDtypeStruct((4, width, inner), bf16),
        ),
        scratch_shapes=[
            pltpu.VMEM((length + 2 * PAD, inner), f32),
            pltpu.VMEM((length, inner), bf16),
            pltpu.VMEM((length, LANES), bf16),
            pltpu.VMEM((256, KERNEL * inner), f32),
        ],
        compiler_params=params(48),
        cost_estimate=cost(2e10, 1e7),
        name="mixers",
    )(place, x, q, dl, maskr, own, got, got2, bv, bp, bc, kw, kb, expand)


def head_lanes(shape, head):
    lane = lax.broadcasted_iota(jnp.int32, shape, 1)
    return (lane < HEAD) if head == 0 else (lane >= HEAD)


def only(pair, head):
    return jnp.where(head_lanes(pair.shape, head), pair, jnp.zeros_like(pair))


def attend_body(q_ref, k_ref, v_ref, segc_ref, o_ref, of_ref, lse_ref, kx, vx, qx):
    length = q_ref.shape[0]
    block = length
    lane = lax.broadcasted_iota(jnp.int32, (length, LANES), 1)
    seg = segc_ref[:, 0:LANES]
    same = seg == lane
    qx[:, 0:LANES] = (q_ref[...].astype(f32) * SCALE).astype(bf16)
    qx[:, LANES:] = jnp.where(same, 1.0, 0.0).astype(bf16)
    other = jnp.where((lane < DOCS) & jnp.logical_not(same), BIG, 0.0).astype(bf16)
    for h in range(2):
        kx[h, :, 0:LANES] = only(k_ref[...].astype(f32), h).astype(bf16)
        kx[h, :, LANES:] = other
    vx[:, 0:LANES] = v_ref[...]
    vx[:, LANES:] = jnp.ones((length, LANES), bf16)

    @pl.loop(0, length // block)
    def _(i):
        t0 = pl.multiple_of(i * block, block)
        now = pl.ds(t0, block)
        outs, totals = [], []
        for h in range(2):
            scores = mm_nt(qx[now, :], kx[h])
            peak = jnp.max(scores, axis=-1, keepdims=True)
            powers = jnp.exp(scores - peak).astype(bf16)
            both = mm(powers, vx[...])
            whole = both[:, LANES:]
            outs.append(both[:, 0:LANES] / whole)
            totals.append(peak + jnp.log(whole))
        left = head_lanes((block, LANES), 0)
        out = jnp.where(left, outs[0], outs[1])
        of_ref[now, :] = out
        o_ref[now, :] = out.astype(bf16)
        lse_ref[now, :] = jnp.where(left, totals[0], totals[1])


def attend(q, k, v, segc):
    length, inner = q.shape
    pair = pl.BlockSpec((length, LANES), lambda p: (0, p))
    fixed = pl.BlockSpec((length, LANES), lambda p: (0, 0))
    return pl.pallas_call(
        attend_body,
        grid=(inner // LANES,),
        in_specs=[pair, pair, pair, fixed],
        out_specs=(pair, pair, pair),
        out_shape=(
            jax.ShapeDtypeStruct((length, inner), bf16),
            jax.ShapeDtypeStruct((length, inner), f32),
            jax.ShapeDtypeStruct((length, inner), f32),
        ),
        scratch_shapes=[
            pltpu.VMEM((2, length, 2 * LANES), bf16),
            pltpu.VMEM((length, 2 * LANES), bf16),
            pltpu.VMEM((length, 2 * LANES), bf16),
        ],
        compiler_params=params(40),
        cost_estimate=cost(2e10, 1e7),
        name="attend",
    )(q, k, v, segc)


def pieces(value):
    first = value.astype(bf16).astype(f32)
    rest = value - first
    second = rest.astype(bf16).astype(f32)
    return first, second, rest - second


def extra_lanes(base, values, lane):
    out = base
    for n, value in enumerate(values):
        out = jnp.where(lane == DOCS + n, value, out)
    return out


def attend_back_body(
    q_ref, k_ref, v_ref, do_ref, of_ref, lse_ref, segc_ref, dq_ref, dk_ref, dv_ref,
    kx, vx, qx, dx, kt,
):
    length = q_ref.shape[0]
    lane = lax.broadcasted_iota(jnp.int32, (length, LANES), 1)
    seg = segc_ref[:, 0:LANES]
    same = seg == lane
    q = q_ref[...].astype(f32) * SCALE
    k = k_ref[...].astype(f32)
    v = v_ref[...].astype(f32)
    do = do_ref[...].astype(f32)
    dots = do * of_ref[...]
    lses = lse_ref[...]
    here = jnp.where(same, 1.0, 0.0)
    other = jnp.where((lane < DOCS) & jnp.logical_not(same), BIG, 0.0)
    ones = jnp.where((lane >= DOCS) & (lane < DOCS + 3), 1.0, 0.0)
    for h in range(2):
        kx[h, :, 0:LANES] = only(k, h).astype(bf16)
        kx[h, :, LANES:] = (other + ones).astype(bf16)
        vx[h, :, 0:LANES] = only(v, h).astype(bf16)
        vx[h, :, LANES:] = ones.astype(bf16)
        qx[h, :, 0:LANES] = only(q, h).astype(bf16)
        minus = [-p for p in pieces(lses[:, h * HEAD : h * HEAD + 1])]
        qx[h, :, LANES:] = extra_lanes(here, minus, lane).astype(bf16)
        dx[h, :, 0:LANES] = only(do, h).astype(bf16)
        dot = jnp.sum(only(dots, h), axis=-1, keepdims=True)
        minus = [-p for p in pieces(dot)]
        dx[h, :, LANES:] = extra_lanes(jnp.zeros_like(here), minus, lane).astype(bf16)
        kt[h] = jnp.transpose(only(k, h)).astype(bf16)
    dq, dk, dv = [], [], []
    for h in range(2):
        probs = jnp.exp(mm_nt(kx[h], qx[h]))
        grads = mm_nt(vx[h], dx[h])
        score = (probs * grads).astype(bf16)
        dv.append(mm(probs.astype(bf16), dx[h, :, 0:LANES]))
        dk.append(mm(score, qx[h, :, 0:LANES]))
        dq.append(mm(kt[h], score))
    dq_ref[...] = jnp.transpose(dq[0] + dq[1]) * SCALE
    dk_ref[...] = (dk[0] + dk[1]).astype(bf16)
    dv_ref[...] = (dv[0] + dv[1]).astype(bf16)


def attend_back(pair_no, q, k, v, do, of, lse, segc):
    length, inner = q.shape
    pair = pl.BlockSpec((length, LANES), lambda p: (0, pair_no))
    fixed = pl.BlockSpec((length, LANES), lambda p: (0, 0))
    wide = pltpu.VMEM((2, length, 2 * LANES), bf16)
    return pl.pallas_call(
        attend_back_body,
        grid=(1,),
        in_specs=[pair] * 6 + [fixed],
        out_specs=(fixed, fixed, fixed),
        out_shape=(
            jax.ShapeDtypeStruct((length, LANES), f32),
            jax.ShapeDtypeStruct((length, LANES), bf16),
            jax.ShapeDtypeStruct((length, LANES), bf16),
        ),
        scratch_shapes=[
            wide, wide, wide, wide,
            pltpu.VMEM((2, LANES, length), bf16),
        ],
        compiler_params=params(48),
        cost_estimate=cost(1.2e10, 4e6),
        name="attend_back",
    )(q, k, v, do, of, lse, segc)


def normal_cdf(value):
    power = jnp.exp(-0.5 * (value * value))
    size = jnp.abs(value)
    t = 1.0 / (1.0 + (0.3275911 * 0.7071067811865476) * size)
    poly = 1.061405429 * t - 1.453152027
    poly = poly * t + 1.421413741
    poly = poly * t - 0.284496736
    poly = poly * t + 0.254829592
    tail = (0.5 * poly) * (t * power)
    return jnp.where(value < 0.0, tail, 1.0 - tail), power * 0.3989422804014327


def row_mean(value):
    return jnp.mean(value, axis=-1, keepdims=True)


def fold(value):
    rows, width = value.shape
    return jnp.sum(value.reshape(rows // 8, 8, width), axis=0)


def slabs(count, rows, unroll, body):
    def step(i, carry):
        body(pl.ds(pl.multiple_of(i * rows, rows), rows))
        return carry

    lax.fori_loop(0, count // rows, step, 0, unroll=unroll)


def ffn_body(
    place_ref, at_ref, mx_ref, x_ref, cot_a_ref, cot_b_ref, wo_ref, bo_ref, g1_ref, s1_ref, wu_ref,
    bu_ref, wd_ref, bd_ref, g2_ref, s2_ref,
    act_own_ref, act_far_ref, res_ref, cg_ref, keep_ref, send_ref, small_ref,
    slope, active, up_grad, grouped, low_grad, hid_grad, joined, sums, up_sums, wide, norm, inverse,
):
    step = pl.program_id(0)
    block = at_ref.shape[0]
    blocks = active.shape[0] // block
    inner = at_ref.shape[1]
    width = x_ref.shape[1]
    part = width // GROUPS
    hidden = wu_ref.shape[2]
    chunk = 768
    rows, unroll = block, 1

    @pl.when(step == 0)
    def _():
        sums[...] = jnp.zeros_like(sums)
        up_sums[...] = jnp.zeros_like(up_sums)

    @pl.when(step < blocks)
    def _():
        t0 = pl.multiple_of(step * block, block)
        now = pl.ds(t0, block)
        own = step < blocks // 2
        joined[now, 0:inner] = at_ref[...]
        joined[now, inner:] = mx_ref[...]
        wide[...] = mm(joined[now, :], wo_ref[...])

        def first(slab):
            resid = x_ref[slab, :].astype(f32) + (wide[slab, :] + bo_ref[...])
            center = resid - row_mean(resid)
            inv = lax.rsqrt(row_mean(center * center) + EPS)
            inverse[slab, :] = jnp.broadcast_to(inv, (rows, LANES))
            normed = center * inv
            norm[slab, :] = normed
            grouped[pl.ds(pl.multiple_of(t0 + slab.start, rows), rows), :] = (
                normed * g1_ref[...] + s1_ref[...]
            ).astype(bf16)

        slabs(block, rows, unroll, first)

        for g in range(GROUPS):
            mine = slice(g * part, (g + 1) * part)
            low = None
            for c in range(hidden // chunk):
                cols = slice(c * chunk, (c + 1) * chunk)
                up = mm(grouped[now, mine], wu_ref[g, :, cols]) + bu_ref[g : g + 1, cols]
                cdf, density = normal_cdf(up)
                act = (up * cdf).astype(bf16)
                at = slice(g * hidden + c * chunk, g * hidden + (c + 1) * chunk)
                active[now, at] = act
                slope[:, at] = cdf + up * density
                add = mm(act, wd_ref[g, cols, :])
                low = add if low is None else low + add
            wide[:, mine] = low + bd_ref[g : g + 1, :]

        def second(slab):
            here = pl.ds(pl.multiple_of(t0 + slab.start, rows), rows)
            resid = (norm[slab, :] * g1_ref[...] + s1_ref[...]) + wide[slab, :]
            center = resid - row_mean(resid)
            inv = lax.rsqrt(row_mean(center * center) + EPS)
            normed = center * inv
            result = (normed * g2_ref[...] + s2_ref[...]).astype(bf16)
            hid_grad[here, :] = result
            grad = jnp.where(own, cot_a_ref[slab, :], cot_b_ref[slab, :]).astype(f32)
            sums[0:8, :] += fold(grad * normed)
            sums[8:16, :] += fold(grad)
            gs = grad * g2_ref[...]
            resid = inv * (gs - row_mean(gs) - normed * row_mean(gs * normed))
            wide[slab, :] = resid
            lg = resid.astype(bf16)
            low_grad[here, :] = lg
            sums[16:24, :] += fold(lg.astype(f32))

        slabs(block, rows, unroll, second)

        @pl.when(own)
        def _():
            act_own_ref[...] = hid_grad[now, :]

        @pl.when(jnp.logical_not(own))
        def _():
            act_far_ref[...] = hid_grad[now, :]

        for g in range(GROUPS):
            mine = slice(g * part, (g + 1) * part)
            back = None
            for c in range(hidden // chunk):
                cols = slice(c * chunk, (c + 1) * chunk)
                at = slice(g * hidden + c * chunk, g * hidden + (c + 1) * chunk)
                ag = mm_nt(low_grad[now, mine], wd_ref[g, cols, :])
                ug = (ag * slope[:, at]).astype(bf16)
                up_grad[now, at] = ug
                up_sums[:, at] += fold(ug.astype(f32))
                add = mm_nt(ug, wu_ref[g, :, cols])
                back = add if back is None else back + add
            wide[:, mine] += back

        def third(slab):
            here = pl.ds(pl.multiple_of(t0 + slab.start, rows), rows)
            grad = wide[slab, :]
            normed = norm[slab, :]
            inv = inverse[slab, 0:1]
            sums[24:32, :] += fold(grad * normed)
            sums[32:40, :] += fold(grad)
            gs = grad * g1_ref[...]
            resid = inv * (gs - row_mean(gs) - normed * row_mean(gs * normed))
            res_ref[slab, :] = resid
            hg = resid.astype(bf16)
            hid_grad[here, :] = hg
            sums[40:48, :] += fold(hg.astype(f32))

        slabs(block, rows, unroll, third)
        cg_ref[...] = mm_nt(hid_grad[now, :], wo_ref[...]).astype(bf16)

    per = hidden // 768

    def weight_grad(half, n):
        mine = slice(half * part, (half + 1) * part)
        if n < per:
            cols = slice(half * hidden + n * 768, half * hidden + (n + 1) * 768)
            return mm_tn(active[:, cols], low_grad[:, mine]).astype(bf16)
        if n < 2 * per:
            n -= per
            cols = slice(half * hidden + n * 768, half * hidden + (n + 1) * 768)
            value = mm_tn(grouped[:, mine], up_grad[:, cols]).astype(bf16)
        else:
            value = mm_tn(joined[:, mine], hid_grad[...]).astype(bf16)
        return jnp.concatenate([value[:, 0:part], value[:, part:]], axis=0)

    for n in range(2 * per + 1):

        @pl.when(step == blocks + n)
        def _():
            for half in range(2):
                store_half(
                    place_ref[1], half, keep_ref, send_ref, slice(None), weight_grad(half, n)
                )

    @pl.when(step == blocks)
    def _():
        across = width // 384
        small_ref[...] = jnp.zeros_like(small_ref)
        for n in range(6):
            line = jnp.sum(sums[8 * n : 8 * n + 8, :], axis=0, keepdims=True)
            for c in range(across):
                small_ref[across * n + c : across * n + c + 1, :] = line[:, c * 384 : (c + 1) * 384]
        line = jnp.sum(up_sums[...], axis=0, keepdims=True)
        for c in range(GROUPS * hidden // 384):
            at = 6 * across + c
            small_ref[at : at + 1, :] = line[:, c * 384 : (c + 1) * 384]


def store_half(core, half, keep_ref, send_ref, rows, value):
    @pl.when(core == half)
    def _():
        keep_ref[rows, :] = value

    @pl.when(core != half)
    def _():
        send_ref[rows, :] = value


def ffn(at, mx, x, cot, cot_far, place, wo, bo, g1, s1, wu, bu, wd, bd, g2, s2):
    length, width = x.shape
    inner = at.shape[1]
    block = length // 2
    blocks = length // block
    near = blocks // 2
    hidden = wu.shape[2]
    gsteps = 2 * (hidden // 768) + 1

    def turn(step, side_ref):
        s = jnp.minimum(step, blocks - 1)
        return (s + side_ref[0] * near) % blocks

    def tok(cols):
        return pl.BlockSpec((block, cols), lambda s, b: (turn(s, b), 0))

    def full(shape):
        return pl.BlockSpec(shape, lambda s, b: (0,) * len(shape), pipeline_mode=pl.Buffered(1))

    def near_map(s, b):
        return (jnp.minimum(s, near - 1), 0)

    def far_map(s, b):
        return (jnp.clip(s - near, 0, near - 1), 0)

    def cot_map(s, b):
        return (b[0], jnp.minimum(s, near - 1), 0)

    return pl.pallas_call(
        ffn_body,
        grid_spec=pltpu.PrefetchScalarGridSpec(
            num_scalar_prefetch=1,
            grid=(blocks + gsteps,),
            in_specs=[
                tok(inner), tok(inner), tok(width),
                pl.BlockSpec((None, block, width), cot_map),
                pl.BlockSpec((block, width), far_map),
                full(wo.shape), full(bo.shape), full(g1.shape), full(s1.shape), full(wu.shape),
                full(bu.shape), full(wd.shape), full(bd.shape), full(g2.shape), full(s2.shape),
            ],
            out_specs=(
                pl.BlockSpec((block, width), near_map),
                pl.BlockSpec((block, width), far_map),
                tok(width),
                tok(width),
                pl.BlockSpec((768, 384), lambda s, b: (jnp.maximum(s - blocks, 0), 0)),
                pl.BlockSpec((768, 384), lambda s, b: (jnp.maximum(s - blocks, 0), 0)),
                pl.BlockSpec((32, 384), lambda s, b: (0, 0)),
            ),
            scratch_shapes=[
                pltpu.VMEM((block, GROUPS * hidden), f32),
                pltpu.VMEM((length, GROUPS * hidden), bf16),
                pltpu.VMEM((length, GROUPS * hidden), bf16),
                pltpu.VMEM((length, width), bf16),
                pltpu.VMEM((length, width), bf16),
                pltpu.VMEM((length, width), bf16),
                pltpu.VMEM((length, width), bf16),
                pltpu.VMEM((48, width), f32),
                pltpu.VMEM((8, GROUPS * hidden), f32),
                pltpu.VMEM((block, width), f32),
                pltpu.VMEM((block, width), f32),
                pltpu.VMEM((block, LANES), f32),
            ],
        ),
        out_shape=(
            jax.ShapeDtypeStruct((length // 2, width), bf16),
            jax.ShapeDtypeStruct((length // 2, width), bf16),
            jax.ShapeDtypeStruct((length, width), f32),
            jax.ShapeDtypeStruct((length, width), bf16),
            jax.ShapeDtypeStruct((gsteps * 768, 384), bf16),
            jax.ShapeDtypeStruct((gsteps * 768, 384), bf16),
            jax.ShapeDtypeStruct((32, 384), f32),
        ),
        compiler_params=params(60),
        cost_estimate=cost(4e10, 3e7),
        name="ffn",
    )(place, at, mx, x, cot, cot_far, wo, bo, g1, s1, wu, bu, wd, bd, g2, s2)


def conv_back_body(
    q_ref, kc_ref, cv_ref, probs_ref, cg_ref, maskr_ref, w_ref, kw_ref, gather_ref,
    qc_ref, dg_ref, kcg, kwg_ref, small_ref,
    pad, prod, taps, kvg, sums,
):
    length, inner = q_ref.shape
    block, rows = 256, 32
    clear_pads(pad, length)

    @pl.loop(0, length // block)
    def _(i):
        t0 = pl.multiple_of(i * block, block)
        pad[pl.ds(pl.multiple_of(t0 + PAD, 16), block), :] = cv_ref[pl.ds(t0, block), :].astype(f32)

    tap_grads = []
    for b in range(length // block):

        @pl.loop(0, block // rows)
        def _(i):
            r0 = pl.multiple_of(i * rows, rows)
            t0 = pl.multiple_of(b * block + r0, rows)
            for c in range(inner // LANES):
                cols = slice(c * LANES, (c + 1) * LANES)
                win = window(pad, t0, rows, cols)
                mg = cg_ref[pl.ds(t0, rows), inner + c * LANES : inner + (c + 1) * LANES].astype(f32)
                for j in range(KERNEL):
                    prod[pl.ds(r0, rows), j * inner + c * LANES : j * inner + (c + 1) * LANES] = (
                        mg * moved(win, j - HALF, rows)
                    ).astype(bf16)

        tap_grads.append(jnp.transpose(mm(prod[...], gather_ref[...])))
    tap_grad = jnp.concatenate(tap_grads, axis=1)
    probs = [probs_ref[8 * j : 8 * j + 8, :] for j in range(KERNEL)]
    grads = [tap_grad[8 * j : 8 * j + 8, :] * maskr_ref[j : j + 1, :] for j in range(KERNEL)]
    dot = probs[0] * grads[0]
    for j in range(1, KERNEL):
        dot = dot + probs[j] * grads[j]
    rest = jnp.zeros((LANES - 8 * KERNEL, length), f32)
    logit = [(probs[j] * (grads[j] - dot)).astype(bf16).astype(f32) for j in range(KERNEL)]
    logit = jnp.concatenate(logit + [rest], axis=0)
    small_ref[...] = jnp.zeros_like(small_ref)
    for b in range(length // LANES):
        taps[b * LANES : (b + 1) * LANES, :] = jnp.transpose(
            logit[:, b * LANES : (b + 1) * LANES]
        ).astype(bf16)
    small_ref[0:1, 0:LANES] = jnp.sum(taps[...].astype(f32), axis=0, keepdims=True)
    sums[...] = jnp.zeros_like(sums)

    @pl.loop(0, length // block)
    def _(i):
        now = pl.ds(pl.multiple_of(i * block, block), block)
        mix_grad = mm(taps[now, :], kw_ref[...])
        q = q_ref[now, :].astype(f32)
        kc = kc_ref[now, :].astype(f32)
        low = (mix_grad * q).astype(bf16)
        kcg[now, :] = low
        kvg[now, :] = (kc * q).astype(bf16)
        sums[...] += fold(low.astype(f32))
        qc_ref[now, :] = mix_grad * kc
        dg_ref[now, :] = mm_nt(low, w_ref[2])

    kwg_ref[...] = mm_tn(taps[...], kvg[...]).astype(bf16)
    small_ref[1:2, :] = jnp.sum(sums[...], axis=0, keepdims=True)


def conv_back(q, kc, cv, probs, cg, maskr, weights, kw, gather):
    length, inner = q.shape
    width = cg.shape[1]
    return pl.pallas_call(
        conv_back_body,
        out_shape=(
            jax.ShapeDtypeStruct((length, inner), f32),
            jax.ShapeDtypeStruct((length, width), f32),
            jax.ShapeDtypeStruct((length, inner), bf16),
            jax.ShapeDtypeStruct((LANES, inner), bf16),
            jax.ShapeDtypeStruct((8, inner), f32),
        ),
        scratch_shapes=[
            pltpu.VMEM((length + 2 * PAD, inner), f32),
            pltpu.VMEM((256, KERNEL * inner), bf16),
            pltpu.VMEM((length, LANES), bf16),
            pltpu.VMEM((length, inner), bf16),
            pltpu.VMEM((8, inner), f32),
        ],
        compiler_params=params(48),
        cost_estimate=cost(1.2e10, 1e7),
        name="conv_back",
    )(q, kc, cv, probs, cg, maskr, weights, kw, gather)


def conv_values_body(
    place_ref, x_ref, dl_ref, kcg_ref, probs_ref, cg_ref, maskr_ref, expand_ref,
    vg_ref, kept_ref, sent_ref, small_ref,
    pad, taps, spread,
):
    length, width = x_ref.shape
    inner = kcg_ref.shape[1]
    block = 256
    clear_pads(pad, length)

    @pl.loop(0, length // block)
    def _(i):
        t0 = pl.multiple_of(i * block, block)
        pad[pl.ds(pl.multiple_of(t0 + PAD, 16), block), :] = cg_ref[
            pl.ds(t0, block), inner:
        ].astype(f32)

    low_taps = []
    for j in range(KERNEL):
        back = KERNEL - 1 - j
        low = probs_ref[8 * back : 8 * back + 8, :].astype(bf16).astype(f32)
        low = low * maskr_ref[back : back + 1, :]
        shift = (HALF - j) % length
        low_taps.append(pltpu.roll(low, shift, 1) if shift else low)
    taps_in_rows(low_taps, taps, length)
    conv_taps(taps, pad, expand_ref, spread, vg_ref, length)
    total = jnp.zeros((8, inner), f32)
    for i in range(length // block):
        total = total + fold(vg_ref[i * block : (i + 1) * block, :].astype(f32))
    small_ref[...] = jnp.zeros_like(small_ref)
    small_ref[0:1, :] = jnp.sum(total, axis=0, keepdims=True)
    core = place_ref[1]
    rows = slice(0, width)
    store_half(core, 0, kept_ref, sent_ref, rows, mm_tn(dl_ref[...], kcg_ref[...]).astype(bf16))
    store_half(core, 1, kept_ref, sent_ref, rows, mm_tn(x_ref[...], vg_ref[...]).astype(bf16))


def conv_values(place, x, dl, kcg, probs, cg, maskr, expand):
    length, width = x.shape
    inner = kcg.shape[1]
    vm = pl.BlockSpec(memory_space=pltpu.VMEM)
    return pl.pallas_call(
        conv_values_body,
        in_specs=[pl.BlockSpec(memory_space=pltpu.SMEM)] + [vm] * 7,
        out_specs=(vm,) * 4,
        out_shape=(
            jax.ShapeDtypeStruct((length, inner), bf16),
            jax.ShapeDtypeStruct((width + LANES, inner), bf16),
            jax.ShapeDtypeStruct((width + LANES, inner), bf16),
            jax.ShapeDtypeStruct((8, inner), f32),
        ),
        scratch_shapes=[
            pltpu.VMEM((length + 2 * PAD, inner), f32),
            pltpu.VMEM((length, LANES), bf16),
            pltpu.VMEM((256, KERNEL * inner), f32),
        ],
        compiler_params=params(48),
        cost_estimate=cost(1.2e10, 1e7),
        name="conv_values",
    )(place, x, dl, kcg, probs, cg, maskr, expand)


def depth_back_body(
    place_ref, x_ref, dg_ref, maskc_ref, dw_ref, kwg_ref, sf_ref, sc_ref, sv_ref, sw_ref,
    kept_ref, sent_ref, dx_ref, keep_ref, send_ref, gpad, dkg,
):
    length, width = x_ref.shape
    block, rows = 256, 32
    clear_pads(gpad, length)
    dkg[...] = jnp.zeros_like(dkg)

    @pl.loop(0, length // block)
    def _(i):
        t0 = pl.multiple_of(i * block, block)
        gpad[pl.ds(pl.multiple_of(t0 + PAD, 16), block), :] = dg_ref[pl.ds(t0, block), :]

    @pl.loop(0, length // rows)
    def _(i):
        t0 = pl.multiple_of(i * rows, rows)
        mask = maskc_ref[pl.ds(t0, rows), :]
        masks = [jnp.broadcast_to(mask[:, j : j + 1], (rows, LANES)) for j in range(KERNEL)]
        for c in range(width // LANES):
            cols = slice(c * LANES, (c + 1) * LANES)
            win = window(gpad, t0, rows, cols)
            x = x_ref[pl.ds(t0, rows), cols].astype(f32)
            total = jnp.zeros((rows, LANES), f32)
            for j in range(KERNEL):
                back = KERNEL - 1 - j
                part = moved(win, j - HALF, rows) * masks[j]
                total = total + dw_ref[back : back + 1, cols] * part
                dkg[8 * back : 8 * back + 8, cols] += fold(part * x)
            dx_ref[pl.ds(t0, rows), cols] = total

    across = width // 384
    lines = []
    for j in range(KERNEL):
        line = jnp.sum(dkg[8 * j : 8 * j + 8, :], axis=0, keepdims=True)
        lines += [line[:, c * 384 : (c + 1) * 384] for c in range(across)]
    smalls = [sf_ref[...], sc_ref[...], sv_ref[...], sw_ref[...]] + lines
    used = sum(v.shape[0] for v in smalls)
    smalls = jnp.concatenate(smalls + [jnp.zeros((LANES - used, 384), f32)], axis=0)
    core = place_ref[1]
    keep_ref[0:width, :] = kept_ref[0:width, :]
    send_ref[0:width, :] = sent_ref[0:width, :]
    rows = slice(width, width + LANES)
    store_half(core, 0, keep_ref, send_ref, rows, kwg_ref[...])
    store_half(core, 1, keep_ref, send_ref, rows, smalls.astype(bf16))


def depth_back(place, x, dg, maskc, dw, kwg, sf, sc, sv, sw, kept, sent):
    length, width = x.shape
    vm = pl.BlockSpec(memory_space=pltpu.VMEM)
    return pl.pallas_call(
        depth_back_body,
        in_specs=[pl.BlockSpec(memory_space=pltpu.SMEM)] + [vm] * 11,
        out_specs=(vm,) * 3,
        out_shape=(
            jax.ShapeDtypeStruct((length, width), f32),
            jax.ShapeDtypeStruct(kept.shape, bf16),
            jax.ShapeDtypeStruct(kept.shape, bf16),
        ),
        scratch_shapes=[
            pltpu.VMEM((length + 2 * PAD, width), f32),
            pltpu.VMEM((8 * KERNEL, width), f32),
        ],
        compiler_params=params(40),
        cost_estimate=cost(1.2e10, 1e7),
        name="depth_back",
    )(place, x, dg, maskc, dw, kwg, sf, sc, sv, sw, kept, sent)


def wgrad_body(
    place_ref, x_ref, *refs
):
    pairs = 3
    dqs, dks, dvs = refs[0:pairs], refs[pairs : 2 * pairs], refs[2 * pairs : 3 * pairs]
    qc_ref, keep_ref, send_ref, dqkv_ref, small_ref = refs[3 * pairs :]
    length, width = x_ref.shape
    inner = qc_ref.shape[1]
    for p in range(pairs):
        cols = slice(p * LANES, (p + 1) * LANES)
        dqkv_ref[:, cols] = (dqs[p][...] + qc_ref[:, cols]).astype(bf16)
        dqkv_ref[:, inner + p * LANES : inner + (p + 1) * LANES] = dks[p][...]
        dqkv_ref[:, 2 * inner + p * LANES : 2 * inner + (p + 1) * LANES] = dvs[p][...]
    core = place_ref[1]
    step = 384
    count = 3 * (width // step)
    for n in range(count):
        which, piece = divmod(n, width // step)
        value = mm_tn(
            x_ref[:, piece * step : (piece + 1) * step],
            dqkv_ref[:, which * inner : (which + 1) * inner],
        ).astype(bf16)
        half, at = divmod(n, count // 2)
        store_half(core, half, keep_ref, send_ref, slice(at * step, (at + 1) * step), value)
    total = jnp.zeros((8, 3 * inner), f32)
    for i in range(length // 256):
        total = total + fold(dqkv_ref[i * 256 : (i + 1) * 256, :].astype(f32))
    line = jnp.sum(total, axis=0, keepdims=True)
    small_ref[...] = jnp.zeros_like(small_ref)
    for which in range(3):
        small_ref[which : which + 1, :] = line[:, which * inner : (which + 1) * inner]


def wgrad(place, x, dqs, dks, dvs, qc):
    length, width = x.shape
    inner = qc.shape[1]
    rows = 3 * width // 2
    vm = pl.BlockSpec(memory_space=pltpu.VMEM)
    return pl.pallas_call(
        wgrad_body,
        in_specs=[pl.BlockSpec(memory_space=pltpu.SMEM)] + [vm] * 11,
        out_specs=(vm,) * 4,
        out_shape=(
            jax.ShapeDtypeStruct((rows, inner), bf16),
            jax.ShapeDtypeStruct((rows, inner), bf16),
            jax.ShapeDtypeStruct((length, 3 * inner), bf16),
            jax.ShapeDtypeStruct((8, inner), f32),
        ),
        compiler_params=params(40),
        cost_estimate=cost(6e9, 1e7),
        name="wgrad",
    )(place, x, *dqs, *dks, *dvs, qc)


def xgrad_body(place_ref, dqkv_ref, vg_ref, dxd_ref, res_ref, wq_ref, w_ref, out_ref):
    inner = vg_ref.shape[1]
    total = res_ref[...] + dxd_ref[...]
    total = total + mm_nt(vg_ref[...], w_ref[3])
    total = total + mm_nt(dqkv_ref[:, 0:inner], wq_ref[...])
    total = total + mm_nt(dqkv_ref[:, inner : 2 * inner], w_ref[0])
    total = total + mm_nt(dqkv_ref[:, 2 * inner :], w_ref[1])
    out_ref[...] = total.astype(out_ref.dtype)


def xgrad(place, far, dqkv, vg, dxd, res, wq, weights):
    length, width = res.shape
    inner = vg.shape[1]
    block = 256
    near = length // 2 // block

    def tok(cols):
        def index(s, b):
            half = 1 - b[0] if far else b[0]
            return (half * near + s, 0)

        return pl.BlockSpec((block, cols), index)

    def full(shape):
        return pl.BlockSpec(shape, lambda s, b: (0,) * len(shape), pipeline_mode=pl.Buffered(1))

    return pl.pallas_call(
        xgrad_body,
        grid_spec=pltpu.PrefetchScalarGridSpec(
            num_scalar_prefetch=1,
            grid=(near,),
            in_specs=[
                tok(3 * inner), tok(inner), tok(width), tok(width), full(wq.shape),
                full(weights.shape),
            ],
            out_specs=pl.BlockSpec((block, width), lambda s, b: (s, 0)),
        ),
        out_shape=jax.ShapeDtypeStruct((length // 2, width), bf16 if far else f32),
        compiler_params=params(40),
        cost_estimate=cost(3e9, 8e6),
        name="xgrad_far" if far else "xgrad_own",
    )(place, dqkv, vg, dxd, res, wq, weights)


def unpack_ffn_body(place_ref, mine_ref, got_ref, down_ref, up_ref, out_ref):
    step = pl.program_id(0)
    per = pl.num_programs(0) // 2
    own = step // per == place_ref[1]
    value = jnp.where(own, mine_ref[...], got_ref[...]).astype(f32)
    n = step % per
    half = value.shape[0] // 2

    @pl.when(n < per // 2)
    def _():
        down_ref[...] = value

    @pl.when((n >= per // 2) & (n < per - 1))
    def _():
        up_ref[:, 0:384] = value[:half]
        up_ref[:, 384:] = value[half:]

    @pl.when(n == per - 1)
    def _():
        out_ref[:, 0:384] = value[:half]
        out_ref[:, 384:] = value[half:]


def unpack_ffn(place, mine, got, hidden):
    rows, part = mine.shape
    per = rows // 768
    each = per // 2

    def source(half_of):
        def index(s, b):
            half = b[1] if half_of else 1 - b[1]
            return (jnp.clip(s - per * half, 0, per - 1), 0)

        return pl.BlockSpec((768, part), index)

    return pl.pallas_call(
        unpack_ffn_body,
        grid_spec=pltpu.PrefetchScalarGridSpec(
            num_scalar_prefetch=1,
            grid=(2 * per,),
            in_specs=[source(True), source(False)],
            out_specs=(
                pl.BlockSpec(
                    (768, part), lambda s, b: (each * (s // per) + jnp.minimum(s % per, each - 1), 0)
                ),
                pl.BlockSpec(
                    (None, part, 768),
                    lambda s, b: (s // per, 0, jnp.clip(s % per - each, 0, each - 1)),
                ),
                pl.BlockSpec((part, 2 * part), lambda s, b: (s // per, 0)),
            ),
        ),
        out_shape=(
            jax.ShapeDtypeStruct((GROUPS * hidden, part), f32),
            jax.ShapeDtypeStruct((GROUPS, part, hidden), f32),
            jax.ShapeDtypeStruct((2 * part, 2 * part), f32),
        ),
        compiler_params=params(32),
        cost_estimate=cost(1e6, 2e7),
        name="unpack_ffn",
    )(place, mine, got)


def unpack_mixers_body(place_ref, cm_ref, cg_ref, am_ref, ag_ref, order_ref, *outs):
    (
        query_ref, query_bias_ref, stack_ref, value_bias_ref, depth_ref, point_ref, kernel_ref,
        kernel_bias_ref, conv_ref, out_bias_ref, gain1_ref, shift1_ref, up_bias_ref, down_bias_ref,
        gain2_ref, shift2_ref,
    ) = outs
    width = query_ref.shape[0]
    half = width // 2
    across = width // 384
    for core in range(2):

        @pl.when(place_ref[1] == core)
        def _():
            conv = (cm_ref, cg_ref) if core == 0 else (cg_ref, cm_ref)
            rest = (am_ref, ag_ref) if core == 0 else (ag_ref, am_ref)
            query_ref[...] = rest[0][0:width, :].astype(f32)

            @pl.when(place_ref[0] == 0)
            def _():
                stack_ref[0, 0:half, :] = rest[0][width:, :].astype(f32)
                stack_ref[0, half:, :] = rest[1][0:half, :].astype(f32)
                stack_ref[1] = rest[1][half:, :].astype(f32)

            @pl.when(place_ref[0] != 0)
            def _():
                stack_ref[0] = conv[0][0:width, :].astype(f32)
                stack_ref[1] = conv[1][0:width, :].astype(f32)

            kernel_ref[...] = mm_tn(conv[0][width:, :], order_ref[...])
            small = conv[1][width:, :]
            kernel_bias_ref[...] = mm(small[32:40, 0:LANES], order_ref[...])[0:1]
            small = small.astype(f32)
            for n, ref in enumerate((gain2_ref, shift2_ref, None, gain1_ref, shift1_ref, out_bias_ref)):
                for c in range(across):
                    line = small[across * n + c : across * n + c + 1, :]
                    if ref is None:
                        down_bias_ref[c : c + 1, :] = line
                    else:
                        ref[:, c * 384 : (c + 1) * 384] = line
            per = up_bias_ref.shape[1] // 384
            for g in range(GROUPS):
                for c in range(per):
                    at = 6 * across + g * per + c
                    up_bias_ref[g : g + 1, c * 384 : (c + 1) * 384] = small[at : at + 1, :]
            point_ref[...] = small[33:34, :]
            conv_ref[...] = small[40:41, :]
            query_bias_ref[...] = small[48:49, :]
            value_bias_ref[...] = small[50:51, :]
            for j in range(KERNEL):
                for c in range(across):
                    at = 56 + across * j + c
                    depth_ref[j : j + 1, c * 384 : (c + 1) * 384] = small[at : at + 1, :]


def unpack_mixers(place, conv_mine, conv_got, mine, got, order, hidden):
    inner = conv_mine.shape[1]
    width = mine.shape[0] * 2 // 3
    vm = pl.BlockSpec(memory_space=pltpu.VMEM)
    shapes = (
        (width, inner), (1, inner), (2, width, inner), (1, inner), (KERNEL, width), (1, inner),
        (inner, HEADS * KERNEL), (1, HEADS * KERNEL), (1, inner), (1, width), (1, width),
        (1, width), (GROUPS, hidden), (GROUPS, width // GROUPS), (1, width), (1, width),
    )
    return pl.pallas_call(
        unpack_mixers_body,
        in_specs=[pl.BlockSpec(memory_space=pltpu.SMEM)] + [vm] * 5,
        out_specs=(vm,) * len(shapes),
        out_shape=tuple(jax.ShapeDtypeStruct(shape, f32) for shape in shapes),
        compiler_params=params(32),
        cost_estimate=cost(1e6, 8e6),
        name="unpack_mixers",
    )(place, conv_mine, conv_got, mine, got, order)


AXES = ("branch", "chip", "core")
CHIPS = ("branch", "chip")


def joint(value, count, masks):
    return lax.ppermute(value, AXES, [(i, i ^ masks[i & 1]) for i in range(count)])


def added(values):
    total = values[0].astype(f32)
    for v in values[1:]:
        total = total + v.astype(f32)
    return total.astype(bf16)


class Sum:
    def __init__(self, kept, sent, index, count, plan):
        self.index, self.count = index, count
        self.plan = [[(1, 1)]] + plan
        self.depth = 0
        self.value, self.sent = kept, [sent]
        self.got = None
        self.down = True

    def hops(self):
        phase = self.plan[self.depth]
        if len(phase) == 1:
            return phase
        (a, b), (c, d) = phase
        return [(a, b), (c, d), (a ^ c, b ^ d)]

    def spot(self):
        at = jnp.int32(0)
        for n, masks in enumerate(self.plan[self.depth]):
            mask = jnp.where(self.index % 2 == 0, masks[0], masks[1])
            at = at + jnp.where((self.index & mask) != 0, 1 << n, 0)
        return at

    def start(self):
        if self.plan[self.depth] is None:
            ways = self.count // 2
            sent = self.value
            if not self.down:
                sent = jnp.broadcast_to(sent[None], (ways,) + sent.shape)
                sent = sent.reshape(-1, sent.shape[-1])
            self.got = [lax.all_to_all(sent, CHIPS, split_axis=0, concat_axis=0, tiled=True)]
            return
        hops = self.hops()
        sent = self.sent if self.down else [self.value] * len(hops)
        self.got = [joint(v, self.count, masks) for v, masks in zip(sent, hops)]

    def finish(self):
        got, self.got = self.got, None
        if not self.down:
            self.value = self.joined(got)
            self.depth -= 1
            return
        if self.plan[self.depth] is None:
            ways = self.count // 2
            pieces = got[0].reshape(ways, got[0].shape[0] // ways, got[0].shape[1])
            total = [jnp.sum(pieces.astype(f32), axis=0)]
        else:
            total = [self.value] + got
        self.depth += 1
        if self.depth == len(self.plan) or self.plan[self.depth] is None:
            self.value, self.sent = added(total), []
            if self.depth == len(self.plan):
                self.down = False
                self.depth -= 1
            return
        spot = self.spot()
        ways = len(self.hops()) + 1
        rows = total[0].shape[0] // ways
        pieces = []
        for k in range(ways):
            at = (spot ^ k) * rows
            pieces.append(added([lax.dynamic_slice_in_dim(v, at, rows, 0) for v in total]))
        self.value, self.sent = pieces[0], pieces[1:]

    def joined(self, got):
        if self.plan[self.depth] is None:
            return got[0]
        spot = self.spot()
        if len(got) == 1:
            first = spot == 0
            return jnp.concatenate(
                [jnp.where(first, self.value, got[0]), jnp.where(first, got[0], self.value)]
            )
        rows = self.value.shape[0]
        whole = jnp.zeros((4 * rows, self.value.shape[1]), self.value.dtype)
        for k, piece in enumerate([self.value] + got):
            whole = lax.dynamic_update_slice_in_dim(whole, piece, (spot ^ k) * rows, 0)
        return whole

    @property
    def last(self):
        return not self.down and self.depth == 0

    def live(self):
        return [self.value] + self.sent

    def put(self, values):
        self.value, self.sent = values[0], list(values[1:])

    def halves(self):
        while True:
            if self.got is None:
                self.start()
            if self.last:
                return self.value, self.got[0]
            self.finish()


def tick(finish, start, held=()):
    for chain in finish:
        if chain.got is not None and not chain.last:
            chain.finish()
    chains = [chain for chain in dict.fromkeys(list(finish) + list(start)) if chain.got is None]
    flat = [v for chain in chains for v in chain.live()]
    tied = lax.optimization_barrier(tuple(flat) + tuple(held))
    at = 0
    for chain in chains:
        n = len(chain.live())
        chain.put(tied[at : at + n])
        at += n
    for chain in start:
        if chain.got is None:
            chain.start()
    return tied[at:]


def local(sizes):
    chips = sizes["chip"]
    along = 2 * chips
    count = along * sizes["branch"]
    masks = [2 << n for n in range(chips.bit_length() - 1)]
    masks.insert(min(2, len(masks)), along)
    swapped = list(masks)
    for n in range(0, len(masks) - 1, 2):
        swapped[n], swapped[n + 1] = masks[n + 1], masks[n]
    pairs = [[both] for both in zip(masks, swapped)]
    near = [along] + [m for m in masks if m != along]
    fours = [[(m, m) for m in near[n : n + 2]] for n in range(0, len(near), 2)]

    def run(
        inputs, segments, query_weight, query_bias, branch_weights, value_bias, depthwise,
        point_bias, kernel_weight, kernel_bias, conv_bias, output_weight, output_bias, first_gain,
        first_shift, up_weight, up_bias, down_weight, down_bias, second_gain, second_shift,
        cotangent,
    ):
        seqs, length, width = inputs.shape
        inner = query_weight.shape[1]
        hidden = up_weight.shape[2]
        part = width // GROUPS
        side = lax.axis_index("branch").astype(jnp.int32)
        core = lax.axis_index("core").astype(jnp.int32)
        index = side * along + 2 * lax.axis_index("chip").astype(jnp.int32) + core
        place = jnp.stack([side, core])
        first = side == 0

        def across(value):
            return joint(value, count, (along, along))

        got = across(lax.dynamic_index_in_dim(branch_weights[0], core, 0, keepdims=False))
        x = lax.dynamic_index_in_dim(inputs, side, 0, keepdims=False)
        seg = lax.dynamic_index_in_dim(segments, side, 0, keepdims=False)

        spots = jnp.arange(length)
        around = spots[None, :] + (jnp.arange(KERNEL) - HALF)[:, None]
        inside = (around >= 0) & (around < length)
        padded = jnp.pad(seg, (HALF, HALF), constant_values=-1)
        near = jnp.stack([lax.slice_in_dim(padded, j, j + length) for j in range(KERNEL)])
        maskr = ((near == seg[None, :]) & inside).astype(f32)
        maskr = jnp.pad(maskr, ((0, 16 - KERNEL), (0, 0)))
        maskc = maskr.T
        segc = jnp.broadcast_to(seg[:, None], (length, LANES))

        kw = kernel_weight.reshape(inner, HEADS, KERNEL).transpose(2, 1, 0)
        kw = jnp.pad(kw, ((0, 0), (0, 8 - HEADS), (0, 0))).reshape(8 * KERNEL, inner)
        kw_wide = jnp.pad(kw, ((0, LANES - 8 * KERNEL), (0, 0)))
        kb = kernel_bias.reshape(HEADS, KERNEL).T
        kb = jnp.pad(kb, ((0, 0), (0, 8 - HEADS))).reshape(8 * KERNEL, 1)
        kb = jnp.broadcast_to(kb, (8 * KERNEL, LANES))

        lane = jnp.arange(KERNEL * inner)
        slot = (lane // inner) * 8 + (lane % inner) // HEAD
        expand = (jnp.arange(LANES)[:, None] == slot[None, :]).astype(bf16)
        gather = (slot[:, None] == jnp.arange(LANES)[None, :]).astype(bf16)

        q, dl = front(x, maskc, query_weight, query_bias[None], depthwise)
        cot_sent = lax.dynamic_index_in_dim(cotangent, 1 - side, 0, keepdims=False)
        got, cot_sent = lax.optimization_barrier((got, cot_sent))
        got2 = joint(got, count, (1, 1))
        cot_far = across(cot_sent)
        k, v, kc, cv, probs, mixed, weights = mixers(
            place, x, q, dl, maskr, branch_weights[0], got, got2, value_bias[None],
            point_bias[None], conv_bias[None], kw, kb, expand,
        )
        attended, attended_f, lse = attend(q, k, v, segc)

        act_own, act_far, resid, cg, keep, send, small_f = ffn(
            attended, mixed, x, cotangent, cot_far, place, output_weight, output_bias[None],
            first_gain[None], first_shift[None], up_weight, up_bias, down_weight,
            down_bias, second_gain[None], second_shift[None],
        )
        ffn_sum = Sum(keep, send, index, count, pairs)
        token = place

        def turn(finish, start, held=()):
            nonlocal token
            *out, token = tick(finish, start, [*held, token])
            return out

        (cg,) = turn([], [ffn_sum], [cg])
        act_got = across(act_far)
        qc, dg, kcg, kwg, small_c = conv_back(
            q, kc, cv, probs, cg, maskr, weights, kw_wide, gather
        )
        cg, qc = turn([ffn_sum], [ffn_sum], [cg, qc])
        back = []
        for pair in range(inner // LANES):
            out = attend_back(pair, q, k, v, cg, attended_f, lse, segc)
            if pair == 0:
                cg, *out = turn([], [], [cg, *out])
            else:
                cg, act_got, *out = turn([ffn_sum], [ffn_sum], [cg, act_got, *out])
            back.append(tuple(out))
        dqs, dks, dvs = zip(*back)
        keep, send, dqkv, small_w = wgrad(place, x, dqs, dks, dvs, qc)
        last_sum = Sum(keep, send, index, count, fours)
        (kcg,) = turn([], [last_sum], [kcg])
        vg, keep, send, small_v = conv_values(place, x, dl, kcg, probs, cg, maskr, expand)
        dg, vg = turn([ffn_sum, last_sum], [ffn_sum, last_sum], [dg, vg])
        dxd, keep, send = depth_back(
            place, x, dg, maskc, depthwise, kwg, small_f, small_c, small_v, small_w, keep, send
        )
        conv_sum = Sum(keep, send, index, count, [None])
        (dxd,) = turn([ffn_sum, last_sum], [ffn_sum, last_sum, conv_sum], [dxd])
        far = xgrad(place, True, dqkv, vg, dxd, resid, query_weight, weights)
        dxd, far = turn([], [], [dxd, far])
        own = xgrad(place, False, dqkv, vg, dxd, resid, query_weight, weights)
        every = [conv_sum, ffn_sum, last_sum]
        own, far = turn(every, every, [own, far])
        activations = jnp.stack(
            [jnp.where(first, act_own, act_got), jnp.where(first, act_got, act_own)]
        )
        activations, far = turn([ffn_sum, last_sum], [ffn_sum, last_sum], [activations, far])
        grad_got = across(far)
        turn([ffn_sum], [ffn_sum])
        (grad_got,) = turn([conv_sum], [conv_sum], [grad_got])
        turn([last_sum], [last_sum])
        grad_far = grad_got.astype(f32)
        input_grad = jnp.stack([jnp.where(first, own, grad_far), jnp.where(first, grad_far, own)])
        (input_grad,) = turn([ffn_sum], [ffn_sum], [input_grad])
        turn([conv_sum], [conv_sum])
        down, up, out = unpack_ffn(place, *ffn_sum.halves(), hidden)
        down = down.reshape(GROUPS, hidden, part)
        spots = jnp.arange(HEADS * KERNEL)
        order = (spots % KERNEL) * 8 + spots // KERNEL
        order = (jnp.arange(LANES)[:, None] == order[None, :]).astype(bf16)
        (
            query_grad, query_bias_grad, stack, value_bias_grad, depth_grad, point_bias_grad,
            kernel_grad, kernel_bias_grad, conv_bias_grad, output_bias_grad, first_gain_grad,
            first_shift_grad, up_bias_grad, down_bias_grad, second_gain_grad, second_shift_grad,
        ) = unpack_mixers(place, *conv_sum.halves(), *last_sum.halves(), order, hidden)

        return (
            activations, input_grad, query_grad, query_bias_grad[0], stack[None],
            value_bias_grad[0], depth_grad, point_bias_grad[0], kernel_grad, kernel_bias_grad[0],
            conv_bias_grad[0], out, output_bias_grad[0], first_gain_grad[0], first_shift_grad[0],
            up, up_bias_grad, down, down_bias_grad, second_gain_grad[0], second_shift_grad[0],
        )

    return run


def solution(mesh):
    branches, ranks = mesh.shape["branch"], mesh.shape["dp"]
    fine = Mesh(mesh.devices.reshape(branches, ranks // 2, 2), AXES)
    whole = P()
    rows = ("chip", "core")
    tokens = P(rows, "branch", None)
    stack = P("branch", None, None, None)
    placed = (
        (P(rows, None, None), P(rows, None), whole, whole, stack) + (whole,) * 16 + (tokens,)
    )
    return jax.shard_map(
        local(dict(fine.shape)),
        mesh=fine,
        in_specs=placed,
        out_specs=(tokens, tokens, whole, whole, stack) + (whole,) * 16,
        check_vma=False,
    )
```

```python
import jax
import jax.numpy as jnp
from jax import lax
from jax.experimental import pallas as pl
from jax.experimental.pallas import tpu as pltpu
from jax.sharding import Mesh
from jax.sharding import PartitionSpec as P

HEADS = 6
HEAD = 64
KERNEL = 9
HALF = KERNEL // 2
GROUPS = 2
DOCS = 8
EPS = 1e-12
BIG = -1e30
SCALE = HEAD**-0.5

PAD = 16
SLOTS = 10
LANES = 128
f32 = jnp.float32
bf16 = jnp.bfloat16


def mm(a, b):
    return jnp.dot(a, b, preferred_element_type=f32)


def mm_nt(a, b):
    return lax.dot_general(a, b, (((1,), (1,)), ((), ())), preferred_element_type=f32)


def mm_tn(a, b):
    return lax.dot_general(a, b, (((0,), (0,)), ((), ())), preferred_element_type=f32)


def params(mib):
    return pltpu.CompilerParams(vmem_limit_bytes=mib * 1024 * 1024)


def cost(flops, nbytes):
    return pl.CostEstimate(flops=int(flops), bytes_accessed=int(nbytes), transcendentals=0)


def window(ref, start, rows, cols):
    return ref[pl.ds(pl.multiple_of(start + PAD - 8, 8), rows + 16), cols]


def moved(win, offset, rows):
    total = rows + 16
    if offset == 0:
        return win[8 : 8 + rows]
    return pltpu.roll(win, (-offset) % total, 0)[8 : 8 + rows]


def clear_pads(ref, length):
    width = ref.shape[1]
    ref[0:PAD, :] = jnp.zeros((PAD, width), f32)
    ref[PAD + length : PAD + length + PAD, :] = jnp.zeros((PAD, width), f32)


def front_body(x_ref, maskc_ref, wq_ref, bq_ref, dw_ref, q_ref, dl_ref, pad):
    length, width = x_ref.shape
    clear_pads(pad, length)
    rows = 32

    @pl.loop(0, length // 128)
    def _(i):
        t0 = pl.multiple_of(i * 128, 128)
        pad[pl.ds(pl.multiple_of(t0 + PAD, 16), 128), :] = x_ref[pl.ds(t0, 128), :].astype(f32)

    @pl.loop(0, length // 256)
    def _(i):
        t0 = pl.multiple_of(i * 256, 256)
        q_ref[pl.ds(t0, 256), :] = (mm(x_ref[pl.ds(t0, 256), :], wq_ref[...]) + bq_ref[...]).astype(
            bf16
        )

    @pl.loop(0, length // rows)
    def _(i):
        t0 = pl.multiple_of(i * rows, rows)
        mask = maskc_ref[pl.ds(t0, rows), :]
        masks = [jnp.broadcast_to(mask[:, j : j + 1], (rows, LANES)) for j in range(KERNEL)]
        for c in range(width // LANES):
            cols = slice(c * LANES, (c + 1) * LANES)
            win = window(pad, t0, rows, cols)
            total = jnp.zeros((rows, LANES), f32)
            for j in range(KERNEL):
                total = total + dw_ref[j : j + 1, cols] * moved(win, j - HALF, rows) * masks[j]
            dl_ref[pl.ds(t0, rows), cols] = total.astype(bf16)


def front(x, maskc, wq, bq, dw):
    length, width = x.shape
    inner = wq.shape[1]
    return pl.pallas_call(
        front_body,
        out_shape=(
            jax.ShapeDtypeStruct((length, inner), bf16),
            jax.ShapeDtypeStruct((length, width), bf16),
        ),
        scratch_shapes=[pltpu.VMEM((length + 2 * PAD, width), f32)],
        compiler_params=params(40),
        cost_estimate=cost(2e10, 8e6),
        name="front",
    )(x, maskc, wq, bq, dw)


def conv_taps(taps, pad, expand_ref, spread, out_ref, length):
    rows = 32
    block = 256
    inner = out_ref.shape[1]

    @pl.loop(0, length // block)
    def _(b):
        b0 = pl.multiple_of(b * block, block)
        for j in range(KERNEL):
            spread[:, j * inner : (j + 1) * inner] = mm(
                taps[pl.ds(b0, block), :], expand_ref[:, j * inner : (j + 1) * inner]
            )

        @pl.loop(0, block // rows)
        def _(i):
            r0 = pl.multiple_of(i * rows, rows)
            t0 = pl.multiple_of(b0 + r0, rows)
            for c in range(inner // LANES):
                cols = slice(c * LANES, (c + 1) * LANES)
                win = window(pad, t0, rows, cols)
                total = jnp.zeros((rows, LANES), f32)
                for j in range(KERNEL):
                    part = spread[pl.ds(r0, rows), j * inner + c * LANES : j * inner + (c + 1) * LANES]
                    total = total + part * moved(win, j - HALF, rows)
                out_ref[pl.ds(t0, rows), cols] = total.astype(bf16)


def taps_in_rows(low_taps, taps, length):
    stacked = jnp.concatenate(low_taps + [jnp.zeros((LANES - 8 * KERNEL, length), f32)], axis=0)
    for b in range(length // LANES):
        piece = stacked[:, b * LANES : (b + 1) * LANES]
        taps[b * LANES : (b + 1) * LANES, :] = jnp.transpose(piece).astype(bf16)


def mixers_body(
    place_ref, x_ref, q_ref, dl_ref, maskr_ref, own_ref, got_ref, got2_ref, bv_ref, bp_ref, bc_ref,
    kw_ref, kb_ref, expand_ref,
    k_ref, v_ref, kc_ref, cv_ref, probs_ref, mixed_ref, w_ref,
    pad, mixing, taps, spread,
):
    length = x_ref.shape[0]
    clear_pads(pad, length)
    side, core = place_ref[0], place_ref[1]
    for n in range(2):
        w_ref[2 * side + n] = own_ref[n]
    w_ref[2 - 2 * side + core] = got_ref[...]
    w_ref[3 - 2 * side - core] = got2_ref[...]

    @pl.loop(0, length // 256)
    def _(i):
        t0 = pl.multiple_of(i * 256, 256)
        now = pl.ds(t0, 256)
        x = x_ref[now, :]
        cv = (mm(x, w_ref[3]) + bc_ref[...]).astype(bf16)
        cv_ref[now, :] = cv
        pad[pl.ds(pl.multiple_of(t0 + PAD, 16), 256), :] = cv.astype(f32)
        kc = (mm(dl_ref[now, :], w_ref[2]) + bp_ref[...]).astype(bf16)
        kc_ref[now, :] = kc
        mixing[now, :] = (kc.astype(f32) * q_ref[now, :].astype(f32)).astype(bf16)
        k_ref[now, :] = mm(x, w_ref[0]).astype(bf16)
        v_ref[now, :] = (mm(x, w_ref[1]) + bv_ref[...]).astype(bf16)

    logits = mm_nt(kw_ref[...], mixing[...]) + kb_ref[:, 0:1]
    rows = [logits[8 * j : 8 * j + 8, :] for j in range(KERNEL)]
    peak = rows[0]
    for r in rows[1:]:
        peak = jnp.maximum(peak, r)
    powers = [jnp.exp(r - peak) for r in rows]
    whole = powers[0]
    for r in powers[1:]:
        whole = whole + r
    share = 1.0 / whole
    low_taps = []
    for j in range(KERNEL):
        probs = powers[j] * share
        probs_ref[8 * j : 8 * j + 8, :] = probs
        low_taps.append(probs.astype(bf16).astype(f32) * maskr_ref[j : j + 1, :])
    taps_in_rows(low_taps, taps, length)
    conv_taps(taps, pad, expand_ref, spread, mixed_ref, length)


def mixers(place, x, q, dl, maskr, own, got, got2, bv, bp, bc, kw, kb, expand):
    length, width = x.shape
    inner = q.shape[1]
    act = jax.ShapeDtypeStruct((length, inner), bf16)
    vm = pl.BlockSpec(memory_space=pltpu.VMEM)
    return pl.pallas_call(
        mixers_body,
        in_specs=[pl.BlockSpec(memory_space=pltpu.SMEM)] + [vm] * 13,
        out_specs=(vm,) * 7,
        out_shape=(
            act, act, act, act, jax.ShapeDtypeStruct((8 * KERNEL, length), f32), act,
            jax.ShapeDtypeStruct((4, width, inner), bf16),
        ),
        scratch_shapes=[
            pltpu.VMEM((length + 2 * PAD, inner), f32),
            pltpu.VMEM((length, inner), bf16),
            pltpu.VMEM((length, LANES), bf16),
            pltpu.VMEM((256, KERNEL * inner), f32),
        ],
        compiler_params=params(48),
        cost_estimate=cost(2e10, 1e7),
        name="mixers",
    )(place, x, q, dl, maskr, own, got, got2, bv, bp, bc, kw, kb, expand)


def head_lanes(shape, head):
    lane = lax.broadcasted_iota(jnp.int32, shape, 1)
    return (lane < HEAD) if head == 0 else (lane >= HEAD)


def only(pair, head):
    return jnp.where(head_lanes(pair.shape, head), pair, jnp.zeros_like(pair))


def attend_body(q_ref, k_ref, v_ref, segc_ref, o_ref, of_ref, lse_ref, kx, vx, qx):
    length = q_ref.shape[0]
    block = length
    lane = lax.broadcasted_iota(jnp.int32, (length, LANES), 1)
    seg = segc_ref[:, 0:LANES]
    same = seg == lane
    qx[:, 0:LANES] = (q_ref[...].astype(f32) * SCALE).astype(bf16)
    qx[:, LANES:] = jnp.where(same, 1.0, 0.0).astype(bf16)
    other = jnp.where((lane < DOCS) & jnp.logical_not(same), BIG, 0.0).astype(bf16)
    for h in range(2):
        kx[h, :, 0:LANES] = only(k_ref[...].astype(f32), h).astype(bf16)
        kx[h, :, LANES:] = other
    vx[:, 0:LANES] = v_ref[...]
    vx[:, LANES:] = jnp.ones((length, LANES), bf16)

    @pl.loop(0, length // block)
    def _(i):
        t0 = pl.multiple_of(i * block, block)
        now = pl.ds(t0, block)
        outs, totals = [], []
        for h in range(2):
            scores = mm_nt(qx[now, :], kx[h])
            peak = jnp.max(scores, axis=-1, keepdims=True)
            powers = jnp.exp(scores - peak).astype(bf16)
            both = mm(powers, vx[...])
            whole = both[:, LANES:]
            outs.append(both[:, 0:LANES] / whole)
            totals.append(peak + jnp.log(whole))
        left = head_lanes((block, LANES), 0)
        out = jnp.where(left, outs[0], outs[1])
        of_ref[now, :] = out
        o_ref[now, :] = out.astype(bf16)
        lse_ref[now, :] = jnp.where(left, totals[0], totals[1])


def attend(q, k, v, segc):
    length, inner = q.shape
    pair = pl.BlockSpec((length, LANES), lambda p: (0, p))
    fixed = pl.BlockSpec((length, LANES), lambda p: (0, 0))
    return pl.pallas_call(
        attend_body,
        grid=(inner // LANES,),
        in_specs=[pair, pair, pair, fixed],
        out_specs=(pair, pair, pair),
        out_shape=(
            jax.ShapeDtypeStruct((length, inner), bf16),
            jax.ShapeDtypeStruct((length, inner), f32),
            jax.ShapeDtypeStruct((length, inner), f32),
        ),
        scratch_shapes=[
            pltpu.VMEM((2, length, 2 * LANES), bf16),
            pltpu.VMEM((length, 2 * LANES), bf16),
            pltpu.VMEM((length, 2 * LANES), bf16),
        ],
        compiler_params=params(62),
        cost_estimate=cost(2e10, 1e7),
        name="attend",
    )(q, k, v, segc)


def pieces(value):
    first = value.astype(bf16).astype(f32)
    rest = value - first
    second = rest.astype(bf16).astype(f32)
    return first, second, rest - second


def extra_lanes(base, values, lane):
    out = base
    for n, value in enumerate(values):
        out = jnp.where(lane == DOCS + n, value, out)
    return out


def attend_back_body(
    q_ref, k_ref, v_ref, do_ref, of_ref, lse_ref, segc_ref, dq_ref, dk_ref, dv_ref,
    kx, vx, qx, dx, kt,
):
    length = q_ref.shape[0]
    lane = lax.broadcasted_iota(jnp.int32, (length, LANES), 1)
    seg = segc_ref[:, 0:LANES]
    same = seg == lane
    q = q_ref[...].astype(f32) * SCALE
    k = k_ref[...].astype(f32)
    v = v_ref[...].astype(f32)
    do = do_ref[...].astype(f32)
    dots = do * of_ref[...]
    lses = lse_ref[...]
    here = jnp.where(same, 1.0, 0.0)
    other = jnp.where((lane < DOCS) & jnp.logical_not(same), BIG, 0.0)
    ones = jnp.where((lane >= DOCS) & (lane < DOCS + 3), 1.0, 0.0)
    for h in range(2):
        kx[h, :, 0:LANES] = only(k, h).astype(bf16)
        kx[h, :, LANES:] = (other + ones).astype(bf16)
        vx[h, :, 0:LANES] = only(v, h).astype(bf16)
        vx[h, :, LANES:] = ones.astype(bf16)
        qx[h, :, 0:LANES] = only(q, h).astype(bf16)
        minus = [-p for p in pieces(lses[:, h * HEAD : h * HEAD + 1])]
        qx[h, :, LANES:] = extra_lanes(here, minus, lane).astype(bf16)
        dx[h, :, 0:LANES] = only(do, h).astype(bf16)
        dot = jnp.sum(only(dots, h), axis=-1, keepdims=True)
        minus = [-p for p in pieces(dot)]
        dx[h, :, LANES:] = extra_lanes(jnp.zeros_like(here), minus, lane).astype(bf16)
        kt[h] = jnp.transpose(only(k, h)).astype(bf16)
    dq, dk, dv = [], [], []
    for h in range(2):
        probs = jnp.exp(mm_nt(kx[h], qx[h]))
        grads = mm_nt(vx[h], dx[h])
        score = (probs * grads).astype(bf16)
        dv.append(mm(probs.astype(bf16), dx[h, :, 0:LANES]))
        dk.append(mm(score, qx[h, :, 0:LANES]))
        dq.append(mm(kt[h], score))
    dq_ref[...] = jnp.transpose(dq[0] + dq[1]) * SCALE
    dk_ref[...] = (dk[0] + dk[1]).astype(bf16)
    dv_ref[...] = (dv[0] + dv[1]).astype(bf16)


def attend_back(pair_no, q, k, v, do, of, lse, segc):
    length, inner = q.shape
    pair = pl.BlockSpec((length, LANES), lambda p: (0, pair_no))
    fixed = pl.BlockSpec((length, LANES), lambda p: (0, 0))
    wide = pltpu.VMEM((2, length, 2 * LANES), bf16)
    return pl.pallas_call(
        attend_back_body,
        grid=(1,),
        in_specs=[pair] * 6 + [fixed],
        out_specs=(fixed, fixed, fixed),
        out_shape=(
            jax.ShapeDtypeStruct((length, LANES), f32),
            jax.ShapeDtypeStruct((length, LANES), bf16),
            jax.ShapeDtypeStruct((length, LANES), bf16),
        ),
        scratch_shapes=[
            wide, wide, wide, wide,
            pltpu.VMEM((2, LANES, length), bf16),
        ],
        compiler_params=params(48),
        cost_estimate=cost(1.2e10, 4e6),
        name="attend_back",
    )(q, k, v, do, of, lse, segc)


def normal_cdf(value):
    power = jnp.exp(-0.5 * (value * value))
    size = jnp.abs(value)
    t = 1.0 / (1.0 + (0.3275911 * 0.7071067811865476) * size)
    poly = 1.061405429 * t - 1.453152027
    poly = poly * t + 1.421413741
    poly = poly * t - 0.284496736
    poly = poly * t + 0.254829592
    tail = (0.5 * poly) * (t * power)
    return jnp.where(value < 0.0, tail, 1.0 - tail), power * 0.3989422804014327


def row_mean(value):
    return jnp.mean(value, axis=-1, keepdims=True)


def fold(value):
    rows, width = value.shape
    return jnp.sum(value.reshape(rows // 8, 8, width), axis=0)


def slabs(count, rows, unroll, body):
    def step(i, carry):
        body(pl.ds(pl.multiple_of(i * rows, rows), rows))
        return carry

    lax.fori_loop(0, count // rows, step, 0, unroll=unroll)


def ffn_body(
    place_ref, at_ref, mx_ref, x_ref, cot_a_ref, cot_b_ref, wo_ref, bo_ref, g1_ref, s1_ref, wu_ref,
    bu_ref, wd_ref, bd_ref, g2_ref, s2_ref,
    act_own_ref, act_far_ref, res_ref, cg_ref, keep_ref, send_ref, small_ref,
    slope, active, up_grad, grouped, low_grad, hid_grad, joined, sums, up_sums, wide, norm, inverse,
):
    step = pl.program_id(0)
    block = at_ref.shape[0]
    blocks = active.shape[0] // block
    inner = at_ref.shape[1]
    width = x_ref.shape[1]
    part = width // GROUPS
    hidden = wu_ref.shape[2]
    chunk = 768
    rows, unroll = block, 1

    @pl.when(step == 0)
    def _():
        sums[...] = jnp.zeros_like(sums)
        up_sums[...] = jnp.zeros_like(up_sums)

    @pl.when(step < blocks)
    def _():
        t0 = pl.multiple_of(step * block, block)
        now = pl.ds(t0, block)
        own = step < blocks // 2
        joined[now, 0:inner] = at_ref[...]
        joined[now, inner:] = mx_ref[...]
        wide[...] = mm(joined[now, :], wo_ref[...])

        def first(slab):
            resid = x_ref[slab, :].astype(f32) + (wide[slab, :] + bo_ref[...])
            center = resid - row_mean(resid)
            inv = lax.rsqrt(row_mean(center * center) + EPS)
            inverse[slab, :] = jnp.broadcast_to(inv, (rows, LANES))
            normed = center * inv
            norm[slab, :] = normed
            grouped[pl.ds(pl.multiple_of(t0 + slab.start, rows), rows), :] = (
                normed * g1_ref[...] + s1_ref[...]
            ).astype(bf16)

        slabs(block, rows, unroll, first)

        for g in range(GROUPS):
            mine = slice(g * part, (g + 1) * part)
            low = None
            for c in range(hidden // chunk):
                cols = slice(c * chunk, (c + 1) * chunk)
                up = mm(grouped[now, mine], wu_ref[g, :, cols]) + bu_ref[g : g + 1, cols]
                cdf, density = normal_cdf(up)
                act = (up * cdf).astype(bf16)
                at = slice(g * hidden + c * chunk, g * hidden + (c + 1) * chunk)
                active[now, at] = act
                slope[:, at] = cdf + up * density
                add = mm(act, wd_ref[g, cols, :])
                low = add if low is None else low + add
            wide[:, mine] = low + bd_ref[g : g + 1, :]

        def second(slab):
            here = pl.ds(pl.multiple_of(t0 + slab.start, rows), rows)
            resid = (norm[slab, :] * g1_ref[...] + s1_ref[...]) + wide[slab, :]
            center = resid - row_mean(resid)
            inv = lax.rsqrt(row_mean(center * center) + EPS)
            normed = center * inv
            result = (normed * g2_ref[...] + s2_ref[...]).astype(bf16)
            hid_grad[here, :] = result
            grad = jnp.where(own, cot_a_ref[slab, :], cot_b_ref[slab, :]).astype(f32)
            sums[0:8, :] += fold(grad * normed)
            sums[8:16, :] += fold(grad)
            gs = grad * g2_ref[...]
            resid = inv * (gs - row_mean(gs) - normed * row_mean(gs * normed))
            wide[slab, :] = resid
            lg = resid.astype(bf16)
            low_grad[here, :] = lg
            sums[16:24, :] += fold(lg.astype(f32))

        slabs(block, rows, unroll, second)

        @pl.when(own)
        def _():
            act_own_ref[...] = hid_grad[now, :]

        @pl.when(jnp.logical_not(own))
        def _():
            act_far_ref[...] = hid_grad[now, :]

        for g in range(GROUPS):
            mine = slice(g * part, (g + 1) * part)
            back = None
            for c in range(hidden // chunk):
                cols = slice(c * chunk, (c + 1) * chunk)
                at = slice(g * hidden + c * chunk, g * hidden + (c + 1) * chunk)
                ag = mm_nt(low_grad[now, mine], wd_ref[g, cols, :])
                ug = (ag * slope[:, at]).astype(bf16)
                up_grad[now, at] = ug
                up_sums[:, at] += fold(ug.astype(f32))
                add = mm_nt(ug, wu_ref[g, :, cols])
                back = add if back is None else back + add
            wide[:, mine] += back

        def third(slab):
            here = pl.ds(pl.multiple_of(t0 + slab.start, rows), rows)
            grad = wide[slab, :]
            normed = norm[slab, :]
            inv = inverse[slab, 0:1]
            sums[24:32, :] += fold(grad * normed)
            sums[32:40, :] += fold(grad)
            gs = grad * g1_ref[...]
            resid = inv * (gs - row_mean(gs) - normed * row_mean(gs * normed))
            res_ref[slab, :] = resid
            hg = resid.astype(bf16)
            hid_grad[here, :] = hg
            sums[40:48, :] += fold(hg.astype(f32))

        slabs(block, rows, unroll, third)
        cg_ref[...] = mm_nt(hid_grad[now, :], wo_ref[...]).astype(bf16)

    per = hidden // 768

    def weight_grad(half, n):
        mine = slice(half * part, (half + 1) * part)
        if n < per:
            cols = slice(half * hidden + n * 768, half * hidden + (n + 1) * 768)
            return mm_tn(active[:, cols], low_grad[:, mine]).astype(bf16)
        if n < 2 * per:
            n -= per
            cols = slice(half * hidden + n * 768, half * hidden + (n + 1) * 768)
            value = mm_tn(grouped[:, mine], up_grad[:, cols]).astype(bf16)
        else:
            value = mm_tn(joined[:, mine], hid_grad[...]).astype(bf16)
        return jnp.concatenate([value[:, 0:part], value[:, part:]], axis=0)

    for n in range(2 * per + 1):

        @pl.when(step == blocks + n)
        def _():
            for half in range(2):
                store_half(
                    place_ref[1], half, keep_ref, send_ref, slice(None), weight_grad(half, n)
                )

    @pl.when(step == blocks)
    def _():
        across = width // 384
        small_ref[...] = jnp.zeros_like(small_ref)
        for n in range(6):
            line = jnp.sum(sums[8 * n : 8 * n + 8, :], axis=0, keepdims=True)
            for c in range(across):
                small_ref[across * n + c : across * n + c + 1, :] = line[:, c * 384 : (c + 1) * 384]
        line = jnp.sum(up_sums[...], axis=0, keepdims=True)
        for c in range(GROUPS * hidden // 384):
            at = 6 * across + c
            small_ref[at : at + 1, :] = line[:, c * 384 : (c + 1) * 384]


def store_half(core, half, keep_ref, send_ref, rows, value):
    @pl.when(core == half)
    def _():
        keep_ref[rows, :] = value

    @pl.when(core != half)
    def _():
        send_ref[rows, :] = value


def ffn(at, mx, x, cot, cot_far, place, wo, bo, g1, s1, wu, bu, wd, bd, g2, s2):
    length, width = x.shape
    inner = at.shape[1]
    block = length // 2
    blocks = length // block
    near = blocks // 2
    hidden = wu.shape[2]
    gsteps = 2 * (hidden // 768) + 1

    def turn(step, side_ref):
        s = jnp.minimum(step, blocks - 1)
        return (s + side_ref[0] * near) % blocks

    def tok(cols):
        return pl.BlockSpec((block, cols), lambda s, b: (turn(s, b), 0))

    def full(shape):
        return pl.BlockSpec(shape, lambda s, b: (0,) * len(shape), pipeline_mode=pl.Buffered(1))

    def near_map(s, b):
        return (jnp.minimum(s, near - 1), 0)

    def far_map(s, b):
        return (jnp.clip(s - near, 0, near - 1), 0)

    def cot_map(s, b):
        return (b[0], jnp.minimum(s, near - 1), 0)

    return pl.pallas_call(
        ffn_body,
        grid_spec=pltpu.PrefetchScalarGridSpec(
            num_scalar_prefetch=1,
            grid=(blocks + gsteps,),
            in_specs=[
                tok(inner), tok(inner), tok(width),
                pl.BlockSpec((None, block, width), cot_map),
                pl.BlockSpec((block, width), far_map),
                full(wo.shape), full(bo.shape), full(g1.shape), full(s1.shape), full(wu.shape),
                full(bu.shape), full(wd.shape), full(bd.shape), full(g2.shape), full(s2.shape),
            ],
            out_specs=(
                pl.BlockSpec((block, width), near_map),
                pl.BlockSpec((block, width), far_map),
                tok(width),
                tok(width),
                pl.BlockSpec((768, 384), lambda s, b: (jnp.maximum(s - blocks, 0), 0)),
                pl.BlockSpec((768, 384), lambda s, b: (jnp.maximum(s - blocks, 0), 0)),
                pl.BlockSpec((32, 384), lambda s, b: (0, 0)),
            ),
            scratch_shapes=[
                pltpu.VMEM((block, GROUPS * hidden), f32),
                pltpu.VMEM((length, GROUPS * hidden), bf16),
                pltpu.VMEM((length, GROUPS * hidden), bf16),
                pltpu.VMEM((length, width), bf16),
                pltpu.VMEM((length, width), bf16),
                pltpu.VMEM((length, width), bf16),
                pltpu.VMEM((length, width), bf16),
                pltpu.VMEM((48, width), f32),
                pltpu.VMEM((8, GROUPS * hidden), f32),
                pltpu.VMEM((block, width), f32),
                pltpu.VMEM((block, width), f32),
                pltpu.VMEM((block, LANES), f32),
            ],
        ),
        out_shape=(
            jax.ShapeDtypeStruct((length // 2, width), bf16),
            jax.ShapeDtypeStruct((length // 2, width), bf16),
            jax.ShapeDtypeStruct((length, width), f32),
            jax.ShapeDtypeStruct((length, width), bf16),
            jax.ShapeDtypeStruct((gsteps * 768, 384), bf16),
            jax.ShapeDtypeStruct((gsteps * 768, 384), bf16),
            jax.ShapeDtypeStruct((32, 384), f32),
        ),
        compiler_params=params(60),
        cost_estimate=cost(4e10, 3e7),
        name="ffn",
    )(place, at, mx, x, cot, cot_far, wo, bo, g1, s1, wu, bu, wd, bd, g2, s2)


def conv_back_body(
    q_ref, kc_ref, cv_ref, probs_ref, cg_ref, maskr_ref, w_ref, kw_ref, gather_ref,
    qc_ref, dg_ref, kcg, kwg_ref, small_ref,
    pad, prod, taps, kvg, sums,
):
    length, inner = q_ref.shape
    block, rows = 256, 32
    clear_pads(pad, length)

    @pl.loop(0, length // block)
    def _(i):
        t0 = pl.multiple_of(i * block, block)
        pad[pl.ds(pl.multiple_of(t0 + PAD, 16), block), :] = cv_ref[pl.ds(t0, block), :].astype(f32)

    tap_grads = []
    for b in range(length // block):

        @pl.loop(0, block // rows)
        def _(i):
            r0 = pl.multiple_of(i * rows, rows)
            t0 = pl.multiple_of(b * block + r0, rows)
            for c in range(inner // LANES):
                cols = slice(c * LANES, (c + 1) * LANES)
                win = window(pad, t0, rows, cols)
                mg = cg_ref[pl.ds(t0, rows), inner + c * LANES : inner + (c + 1) * LANES].astype(f32)
                for j in range(KERNEL):
                    prod[pl.ds(r0, rows), j * inner + c * LANES : j * inner + (c + 1) * LANES] = (
                        mg * moved(win, j - HALF, rows)
                    ).astype(bf16)

        tap_grads.append(jnp.transpose(mm(prod[...], gather_ref[...])))
    tap_grad = jnp.concatenate(tap_grads, axis=1)
    probs = [probs_ref[8 * j : 8 * j + 8, :] for j in range(KERNEL)]
    grads = [tap_grad[8 * j : 8 * j + 8, :] * maskr_ref[j : j + 1, :] for j in range(KERNEL)]
    dot = probs[0] * grads[0]
    for j in range(1, KERNEL):
        dot = dot + probs[j] * grads[j]
    rest = jnp.zeros((LANES - 8 * KERNEL, length), f32)
    logit = [(probs[j] * (grads[j] - dot)).astype(bf16).astype(f32) for j in range(KERNEL)]
    logit = jnp.concatenate(logit + [rest], axis=0)
    small_ref[...] = jnp.zeros_like(small_ref)
    for b in range(length // LANES):
        taps[b * LANES : (b + 1) * LANES, :] = jnp.transpose(
            logit[:, b * LANES : (b + 1) * LANES]
        ).astype(bf16)
    small_ref[0:1, 0:LANES] = jnp.sum(taps[...].astype(f32), axis=0, keepdims=True)
    sums[...] = jnp.zeros_like(sums)

    @pl.loop(0, length // block)
    def _(i):
        now = pl.ds(pl.multiple_of(i * block, block), block)
        mix_grad = mm(taps[now, :], kw_ref[...])
        q = q_ref[now, :].astype(f32)
        kc = kc_ref[now, :].astype(f32)
        low = (mix_grad * q).astype(bf16)
        kcg[now, :] = low
        kvg[now, :] = (kc * q).astype(bf16)
        sums[...] += fold(low.astype(f32))
        qc_ref[now, :] = mix_grad * kc
        dg_ref[now, :] = mm_nt(low, w_ref[2])

    kwg_ref[...] = mm_tn(taps[...], kvg[...]).astype(bf16)
    small_ref[1:2, :] = jnp.sum(sums[...], axis=0, keepdims=True)


def conv_back(q, kc, cv, probs, cg, maskr, weights, kw, gather):
    length, inner = q.shape
    width = cg.shape[1]
    return pl.pallas_call(
        conv_back_body,
        out_shape=(
            jax.ShapeDtypeStruct((length, inner), f32),
            jax.ShapeDtypeStruct((length, width), f32),
            jax.ShapeDtypeStruct((length, inner), bf16),
            jax.ShapeDtypeStruct((LANES, inner), bf16),
            jax.ShapeDtypeStruct((8, inner), f32),
        ),
        scratch_shapes=[
            pltpu.VMEM((length + 2 * PAD, inner), f32),
            pltpu.VMEM((256, KERNEL * inner), bf16),
            pltpu.VMEM((length, LANES), bf16),
            pltpu.VMEM((length, inner), bf16),
            pltpu.VMEM((8, inner), f32),
        ],
        compiler_params=params(48),
        cost_estimate=cost(1.2e10, 1e7),
        name="conv_back",
    )(q, kc, cv, probs, cg, maskr, weights, kw, gather)


def conv_values_body(
    place_ref, x_ref, dl_ref, kcg_ref, probs_ref, cg_ref, maskr_ref, expand_ref,
    vg_ref, kept_ref, sent_ref, small_ref,
    pad, taps, spread,
):
    length, width = x_ref.shape
    inner = kcg_ref.shape[1]
    block = 256
    clear_pads(pad, length)

    @pl.loop(0, length // block)
    def _(i):
        t0 = pl.multiple_of(i * block, block)
        pad[pl.ds(pl.multiple_of(t0 + PAD, 16), block), :] = cg_ref[
            pl.ds(t0, block), inner:
        ].astype(f32)

    low_taps = []
    for j in range(KERNEL):
        back = KERNEL - 1 - j
        low = probs_ref[8 * back : 8 * back + 8, :].astype(bf16).astype(f32)
        low = low * maskr_ref[back : back + 1, :]
        shift = (HALF - j) % length
        low_taps.append(pltpu.roll(low, shift, 1) if shift else low)
    taps_in_rows(low_taps, taps, length)
    conv_taps(taps, pad, expand_ref, spread, vg_ref, length)
    total = jnp.zeros((8, inner), f32)
    for i in range(length // block):
        total = total + fold(vg_ref[i * block : (i + 1) * block, :].astype(f32))
    small_ref[...] = jnp.zeros_like(small_ref)
    small_ref[0:1, :] = jnp.sum(total, axis=0, keepdims=True)
    core = place_ref[1]
    rows = slice(0, width)
    store_half(core, 0, kept_ref, sent_ref, rows, mm_tn(dl_ref[...], kcg_ref[...]).astype(bf16))
    store_half(core, 1, kept_ref, sent_ref, rows, mm_tn(x_ref[...], vg_ref[...]).astype(bf16))


def conv_values(place, x, dl, kcg, probs, cg, maskr, expand):
    length, width = x.shape
    inner = kcg.shape[1]
    vm = pl.BlockSpec(memory_space=pltpu.VMEM)
    return pl.pallas_call(
        conv_values_body,
        in_specs=[pl.BlockSpec(memory_space=pltpu.SMEM)] + [vm] * 7,
        out_specs=(vm,) * 4,
        out_shape=(
            jax.ShapeDtypeStruct((length, inner), bf16),
            jax.ShapeDtypeStruct((width + LANES, inner), bf16),
            jax.ShapeDtypeStruct((width + LANES, inner), bf16),
            jax.ShapeDtypeStruct((8, inner), f32),
        ),
        scratch_shapes=[
            pltpu.VMEM((length + 2 * PAD, inner), f32),
            pltpu.VMEM((length, LANES), bf16),
            pltpu.VMEM((256, KERNEL * inner), f32),
        ],
        compiler_params=params(48),
        cost_estimate=cost(1.2e10, 1e7),
        name="conv_values",
    )(place, x, dl, kcg, probs, cg, maskr, expand)


def depth_back_body(
    place_ref, x_ref, dg_ref, maskc_ref, dw_ref, kwg_ref, sf_ref, sc_ref, sv_ref, sw_ref,
    kept_ref, sent_ref, dx_ref, keep_ref, send_ref, gpad, dkg,
):
    length, width = x_ref.shape
    block, rows = 256, 32
    clear_pads(gpad, length)
    dkg[...] = jnp.zeros_like(dkg)

    @pl.loop(0, length // block)
    def _(i):
        t0 = pl.multiple_of(i * block, block)
        gpad[pl.ds(pl.multiple_of(t0 + PAD, 16), block), :] = dg_ref[pl.ds(t0, block), :]

    @pl.loop(0, length // rows)
    def _(i):
        t0 = pl.multiple_of(i * rows, rows)
        mask = maskc_ref[pl.ds(t0, rows), :]
        masks = [jnp.broadcast_to(mask[:, j : j + 1], (rows, LANES)) for j in range(KERNEL)]
        for c in range(width // LANES):
            cols = slice(c * LANES, (c + 1) * LANES)
            win = window(gpad, t0, rows, cols)
            x = x_ref[pl.ds(t0, rows), cols].astype(f32)
            total = jnp.zeros((rows, LANES), f32)
            for j in range(KERNEL):
                back = KERNEL - 1 - j
                part = moved(win, j - HALF, rows) * masks[j]
                total = total + dw_ref[back : back + 1, cols] * part
                dkg[8 * back : 8 * back + 8, cols] += fold(part * x)
            dx_ref[pl.ds(t0, rows), cols] = total

    across = width // 384
    lines = []
    for j in range(KERNEL):
        line = jnp.sum(dkg[8 * j : 8 * j + 8, :], axis=0, keepdims=True)
        lines += [line[:, c * 384 : (c + 1) * 384] for c in range(across)]
    smalls = [sf_ref[...], sc_ref[...], sv_ref[...], sw_ref[...]] + lines
    used = sum(v.shape[0] for v in smalls)
    smalls = jnp.concatenate(smalls + [jnp.zeros((LANES - used, 384), f32)], axis=0)
    core = place_ref[1]
    keep_ref[0:width, :] = kept_ref[0:width, :]
    send_ref[0:width, :] = sent_ref[0:width, :]
    rows = slice(width, width + LANES)
    store_half(core, 0, keep_ref, send_ref, rows, kwg_ref[...])
    store_half(core, 1, keep_ref, send_ref, rows, smalls.astype(bf16))


def depth_back(place, x, dg, maskc, dw, kwg, sf, sc, sv, sw, kept, sent):
    length, width = x.shape
    vm = pl.BlockSpec(memory_space=pltpu.VMEM)
    return pl.pallas_call(
        depth_back_body,
        in_specs=[pl.BlockSpec(memory_space=pltpu.SMEM)] + [vm] * 11,
        out_specs=(vm,) * 3,
        out_shape=(
            jax.ShapeDtypeStruct((length, width), f32),
            jax.ShapeDtypeStruct(kept.shape, bf16),
            jax.ShapeDtypeStruct(kept.shape, bf16),
        ),
        scratch_shapes=[
            pltpu.VMEM((length + 2 * PAD, width), f32),
            pltpu.VMEM((8 * KERNEL, width), f32),
        ],
        compiler_params=params(40),
        cost_estimate=cost(1.2e10, 1e7),
        name="depth_back",
    )(place, x, dg, maskc, dw, kwg, sf, sc, sv, sw, kept, sent)


def wgrad_body(
    place_ref, x_ref, *refs
):
    pairs = 3
    dqs, dks, dvs = refs[0:pairs], refs[pairs : 2 * pairs], refs[2 * pairs : 3 * pairs]
    qc_ref, keep_ref, send_ref, dqkv_ref, small_ref = refs[3 * pairs :]
    length, width = x_ref.shape
    inner = qc_ref.shape[1]
    for p in range(pairs):
        cols = slice(p * LANES, (p + 1) * LANES)
        dqkv_ref[:, cols] = (dqs[p][...] + qc_ref[:, cols]).astype(bf16)
        dqkv_ref[:, inner + p * LANES : inner + (p + 1) * LANES] = dks[p][...]
        dqkv_ref[:, 2 * inner + p * LANES : 2 * inner + (p + 1) * LANES] = dvs[p][...]
    core = place_ref[1]
    step = 384
    count = 3 * (width // step)
    for n in range(count):
        which, piece = divmod(n, width // step)
        value = mm_tn(
            x_ref[:, piece * step : (piece + 1) * step],
            dqkv_ref[:, which * inner : (which + 1) * inner],
        ).astype(bf16)
        half, at = divmod(n, count // 2)
        store_half(core, half, keep_ref, send_ref, slice(at * step, (at + 1) * step), value)
    total = jnp.zeros((8, 3 * inner), f32)
    for i in range(length // 256):
        total = total + fold(dqkv_ref[i * 256 : (i + 1) * 256, :].astype(f32))
    line = jnp.sum(total, axis=0, keepdims=True)
    small_ref[...] = jnp.zeros_like(small_ref)
    for which in range(3):
        small_ref[which : which + 1, :] = line[:, which * inner : (which + 1) * inner]


def wgrad(place, x, dqs, dks, dvs, qc):
    length, width = x.shape
    inner = qc.shape[1]
    rows = 3 * width // 2
    vm = pl.BlockSpec(memory_space=pltpu.VMEM)
    return pl.pallas_call(
        wgrad_body,
        in_specs=[pl.BlockSpec(memory_space=pltpu.SMEM)] + [vm] * 11,
        out_specs=(vm,) * 4,
        out_shape=(
            jax.ShapeDtypeStruct((rows, inner), bf16),
            jax.ShapeDtypeStruct((rows, inner), bf16),
            jax.ShapeDtypeStruct((length, 3 * inner), bf16),
            jax.ShapeDtypeStruct((8, inner), f32),
        ),
        compiler_params=params(40),
        cost_estimate=cost(6e9, 1e7),
        name="wgrad",
    )(place, x, *dqs, *dks, *dvs, qc)


def xgrad_body(place_ref, dqkv_ref, vg_ref, dxd_ref, res_ref, wq_ref, w_ref, out_ref):
    inner = vg_ref.shape[1]
    total = res_ref[...] + dxd_ref[...]
    total = total + mm_nt(vg_ref[...], w_ref[3])
    total = total + mm_nt(dqkv_ref[:, 0:inner], wq_ref[...])
    total = total + mm_nt(dqkv_ref[:, inner : 2 * inner], w_ref[0])
    total = total + mm_nt(dqkv_ref[:, 2 * inner :], w_ref[1])
    out_ref[...] = total.astype(out_ref.dtype)


def xgrad(place, far, dqkv, vg, dxd, res, wq, weights):
    length, width = res.shape
    inner = vg.shape[1]
    block = 256
    near = length // 2 // block

    def tok(cols):
        def index(s, b):
            half = 1 - b[0] if far else b[0]
            return (half * near + s, 0)

        return pl.BlockSpec((block, cols), index)

    def full(shape):
        return pl.BlockSpec(shape, lambda s, b: (0,) * len(shape), pipeline_mode=pl.Buffered(1))

    return pl.pallas_call(
        xgrad_body,
        grid_spec=pltpu.PrefetchScalarGridSpec(
            num_scalar_prefetch=1,
            grid=(near,),
            in_specs=[
                tok(3 * inner), tok(inner), tok(width), tok(width), full(wq.shape),
                full(weights.shape),
            ],
            out_specs=pl.BlockSpec((block, width), lambda s, b: (s, 0)),
        ),
        out_shape=jax.ShapeDtypeStruct((length // 2, width), bf16 if far else f32),
        compiler_params=params(40),
        cost_estimate=cost(3e9, 8e6),
        name="xgrad_far" if far else "xgrad_own",
    )(place, dqkv, vg, dxd, res, wq, weights)


def unpack_ffn_body(place_ref, source_ref, *refs):
    down_ref, up_ref, out_ref = refs[-3:]
    step = pl.program_id(0)
    per = pl.num_programs(0)
    value = source_ref[...].astype(f32)
    half = value.shape[0] // 2

    @pl.when(step < per // 2)
    def _():
        down_ref[...] = value

    @pl.when((step >= per // 2) & (step < per - 1))
    def _():
        up_ref[:, 0:384] = value[:half]
        up_ref[:, 384:] = value[half:]

    @pl.when(step == per - 1)
    def _():
        out_ref[:, 0:384] = value[:half]
        out_ref[:, 384:] = value[half:]


def unpack_ffn(place, mine, source, hidden, before=()):
    rows, part = source.shape
    per = rows // 768
    each = per // 2

    def half(b):
        return b[1] if mine else 1 - b[1]

    return pl.pallas_call(
        unpack_ffn_body,
        grid_spec=pltpu.PrefetchScalarGridSpec(
            num_scalar_prefetch=1,
            grid=(per,),
            in_specs=[pl.BlockSpec((768, part), lambda s, b: (s, 0))]
            + [pl.BlockSpec(memory_space=pl.ANY)] * len(before),
            out_specs=(
                pl.BlockSpec(
                    (768, part), lambda s, b: (each * half(b) + jnp.minimum(s, each - 1), 0)
                ),
                pl.BlockSpec(
                    (None, part, 768), lambda s, b: (half(b), 0, jnp.clip(s - each, 0, each - 1))
                ),
                pl.BlockSpec((part, 2 * part), lambda s, b: (half(b), 0)),
            ),
        ),
        out_shape=(
            jax.ShapeDtypeStruct((GROUPS * hidden, part), f32),
            jax.ShapeDtypeStruct((GROUPS, part, hidden), f32),
            jax.ShapeDtypeStruct((2 * part, 2 * part), f32),
        ),
        input_output_aliases={2 + n: n for n in range(len(before))},
        compiler_params=params(32),
        cost_estimate=cost(1e6, 1e7),
        name="unpack_mine" if mine else "unpack_theirs",
    )(place, source, *before)


def unpack_mixers_body(place_ref, cm_ref, cg_ref, am_ref, ag_ref, order_ref, *outs):
    (
        query_ref, query_bias_ref, stack_ref, value_bias_ref, depth_ref, point_ref, kernel_ref,
        kernel_bias_ref, conv_ref, out_bias_ref, gain1_ref, shift1_ref, up_bias_ref, down_bias_ref,
        gain2_ref, shift2_ref,
    ) = outs
    width = query_ref.shape[0]
    half = width // 2
    across = width // 384
    for core in range(2):

        @pl.when(place_ref[1] == core)
        def _():
            conv = (cm_ref, cg_ref) if core == 0 else (cg_ref, cm_ref)
            rest = (am_ref, ag_ref) if core == 0 else (ag_ref, am_ref)
            query_ref[...] = rest[0][0:width, :].astype(f32)

            @pl.when(place_ref[0] == 0)
            def _():
                stack_ref[0, 0:half, :] = rest[0][width:, :].astype(f32)
                stack_ref[0, half:, :] = rest[1][0:half, :].astype(f32)
                stack_ref[1] = rest[1][half:, :].astype(f32)

            @pl.when(place_ref[0] != 0)
            def _():
                stack_ref[0] = conv[0][0:width, :].astype(f32)
                stack_ref[1] = conv[1][0:width, :].astype(f32)

            kernel_ref[...] = mm_tn(conv[0][width:, :], order_ref[...])
            small = conv[1][width:, :]
            kernel_bias_ref[...] = mm(small[32:40, 0:LANES], order_ref[...])[0:1]
            small = small.astype(f32)
            for n, ref in enumerate((gain2_ref, shift2_ref, None, gain1_ref, shift1_ref, out_bias_ref)):
                for c in range(across):
                    line = small[across * n + c : across * n + c + 1, :]
                    if ref is None:
                        down_bias_ref[c : c + 1, :] = line
                    else:
                        ref[c * 384 : (c + 1) * 384] = line.reshape(384)
            per = up_bias_ref.shape[1] // 384
            for g in range(GROUPS):
                for c in range(per):
                    at = 6 * across + g * per + c
                    up_bias_ref[g : g + 1, c * 384 : (c + 1) * 384] = small[at : at + 1, :]
            point_ref[...] = small[33:34, :].reshape(384)
            conv_ref[...] = small[40:41, :].reshape(384)
            query_bias_ref[...] = small[48:49, :].reshape(384)
            value_bias_ref[...] = small[50:51, :].reshape(384)
            for j in range(KERNEL):
                for c in range(across):
                    at = 56 + across * j + c
                    depth_ref[j : j + 1, c * 384 : (c + 1) * 384] = small[at : at + 1, :]


def unpack_mixers(place, conv_mine, conv_got, mine, got, order, hidden):
    inner = conv_mine.shape[1]
    width = mine.shape[0] * 2 // 3
    vm = pl.BlockSpec(memory_space=pltpu.VMEM)
    shapes = (
        (width, inner), (inner,), (2, width, inner), (inner,), (KERNEL, width), (inner,),
        (inner, HEADS * KERNEL), (1, HEADS * KERNEL), (inner,), (width,), (width,), (width,),
        (GROUPS, hidden), (GROUPS, width // GROUPS), (width,), (width,),
    )
    return pl.pallas_call(
        unpack_mixers_body,
        in_specs=[pl.BlockSpec(memory_space=pltpu.SMEM)] + [vm] * 5,
        out_specs=(vm,) * len(shapes),
        out_shape=tuple(jax.ShapeDtypeStruct(shape, f32) for shape in shapes),
        compiler_params=params(32),
        cost_estimate=cost(1e6, 8e6),
        name="unpack_mixers",
    )(place, conv_mine, conv_got, mine, got, order)


AXES = ("branch", "chip", "core")
CHIPS = ("branch", "chip")


def joint(value, count, masks):
    return lax.ppermute(value, AXES, [(i, i ^ masks[i & 1]) for i in range(count)])


def added(values):
    total = values[0].astype(f32)
    for v in values[1:]:
        total = total + v.astype(f32)
    return total.astype(bf16)


class Sum:
    def __init__(self, kept, sent, index, count, plan):
        self.index, self.count = index, count
        self.plan = [[(1, 1)]] + plan
        self.depth = 0
        self.value, self.sent = kept, [sent]
        self.got = None
        self.down = True

    def hops(self):
        phase = self.plan[self.depth]
        if len(phase) == 1:
            return phase
        (a, b), (c, d) = phase
        return [(a, b), (c, d), (a ^ c, b ^ d)]

    def spot(self):
        at = jnp.int32(0)
        for n, masks in enumerate(self.plan[self.depth]):
            mask = jnp.where(self.index % 2 == 0, masks[0], masks[1])
            at = at + jnp.where((self.index & mask) != 0, 1 << n, 0)
        return at

    def start(self):
        if self.plan[self.depth] is None:
            ways = self.count // 2
            sent = self.value
            if not self.down:
                sent = jnp.broadcast_to(sent[None], (ways,) + sent.shape)
                sent = sent.reshape(-1, sent.shape[-1])
            self.got = [lax.all_to_all(sent, CHIPS, split_axis=0, concat_axis=0, tiled=True)]
            return
        hops = self.hops()
        sent = self.sent if self.down else [self.value] * len(hops)
        self.got = [joint(v, self.count, masks) for v, masks in zip(sent, hops)]

    def finish(self):
        got, self.got = self.got, None
        if not self.down:
            self.value = self.joined(got)
            self.depth -= 1
            return
        if self.plan[self.depth] is None:
            ways = self.count // 2
            pieces = got[0].reshape(ways, got[0].shape[0] // ways, got[0].shape[1])
            total = [jnp.sum(pieces.astype(f32), axis=0)]
        else:
            total = [self.value] + got
        self.depth += 1
        if self.depth == len(self.plan) or self.plan[self.depth] is None:
            self.value, self.sent = added(total), []
            if self.depth == len(self.plan):
                self.down = False
                self.depth -= 1
            return
        spot = self.spot()
        ways = len(self.hops()) + 1
        rows = total[0].shape[0] // ways
        pieces = []
        for k in range(ways):
            at = (spot ^ k) * rows
            pieces.append(added([lax.dynamic_slice_in_dim(v, at, rows, 0) for v in total]))
        self.value, self.sent = pieces[0], pieces[1:]

    def joined(self, got):
        if self.plan[self.depth] is None:
            return got[0]
        spot = self.spot()
        if len(got) == 1:
            first = spot == 0
            return jnp.concatenate(
                [jnp.where(first, self.value, got[0]), jnp.where(first, got[0], self.value)]
            )
        rows = self.value.shape[0]
        whole = jnp.zeros((4 * rows, self.value.shape[1]), self.value.dtype)
        for k, piece in enumerate([self.value] + got):
            whole = lax.dynamic_update_slice_in_dim(whole, piece, (spot ^ k) * rows, 0)
        return whole

    @property
    def last(self):
        return not self.down and self.depth == 0

    def live(self):
        return [self.value] + self.sent

    def put(self, values):
        self.value, self.sent = values[0], list(values[1:])

    def halves(self):
        while True:
            if self.got is None:
                self.start()
            if self.last:
                return self.value, self.got[0]
            self.finish()


def tick(finish, start, held=()):
    for chain in finish:
        if chain.got is not None and not chain.last:
            chain.finish()
    chains = [chain for chain in dict.fromkeys(list(finish) + list(start)) if chain.got is None]
    flat = [v for chain in chains for v in chain.live()]
    tied = lax.optimization_barrier(tuple(flat) + tuple(held))
    at = 0
    for chain in chains:
        n = len(chain.live())
        chain.put(tied[at : at + n])
        at += n
    for chain in start:
        if chain.got is None:
            chain.start()
    return tied[at:]


def local(sizes):
    chips = sizes["chip"]
    along = 2 * chips
    count = along * sizes["branch"]
    masks = [2 << n for n in range(chips.bit_length() - 1)]
    masks.insert(min(2, len(masks)), along)
    swapped = list(masks)
    for n in range(0, len(masks) - 1, 2):
        swapped[n], swapped[n + 1] = masks[n + 1], masks[n]
    pairs = [[both] for both in zip(masks, swapped)]
    near = [along] + [m for m in masks if m != along]
    fours = [[(m, m) for m in near[n : n + 2]] for n in range(0, len(near), 2)]

    def run(
        inputs, segments, query_weight, query_bias, branch_weights, value_bias, depthwise,
        point_bias, kernel_weight, kernel_bias, conv_bias, output_weight, output_bias, first_gain,
        first_shift, up_weight, up_bias, down_weight, down_bias, second_gain, second_shift,
        cotangent,
    ):
        seqs, length, width = inputs.shape
        inner = query_weight.shape[1]
        hidden = up_weight.shape[2]
        part = width // GROUPS
        side = lax.axis_index("branch").astype(jnp.int32)
        core = lax.axis_index("core").astype(jnp.int32)
        index = side * along + 2 * lax.axis_index("chip").astype(jnp.int32) + core
        place = jnp.stack([side, core])
        first = side == 0

        def across(value):
            return joint(value, count, (along, along))

        got = across(lax.dynamic_index_in_dim(branch_weights[0], core, 0, keepdims=False))
        x = lax.dynamic_index_in_dim(inputs, side, 0, keepdims=False)
        seg = lax.dynamic_index_in_dim(segments, side, 0, keepdims=False)

        spots = jnp.arange(length)
        around = spots[None, :] + (jnp.arange(KERNEL) - HALF)[:, None]
        inside = (around >= 0) & (around < length)
        padded = jnp.pad(seg, (HALF, HALF), constant_values=-1)
        near = jnp.stack([lax.slice_in_dim(padded, j, j + length) for j in range(KERNEL)])
        maskr = ((near == seg[None, :]) & inside).astype(f32)
        maskr = jnp.pad(maskr, ((0, 16 - KERNEL), (0, 0)))
        maskc = maskr.T
        segc = jnp.broadcast_to(seg[:, None], (length, LANES))

        kw = kernel_weight.reshape(inner, HEADS, KERNEL).transpose(2, 1, 0)
        kw = jnp.pad(kw, ((0, 0), (0, 8 - HEADS), (0, 0))).reshape(8 * KERNEL, inner)
        kw_wide = jnp.pad(kw, ((0, LANES - 8 * KERNEL), (0, 0)))
        kb = kernel_bias.reshape(HEADS, KERNEL).T
        kb = jnp.pad(kb, ((0, 0), (0, 8 - HEADS))).reshape(8 * KERNEL, 1)
        kb = jnp.broadcast_to(kb, (8 * KERNEL, LANES))

        lane = jnp.arange(KERNEL * inner)
        slot = (lane // inner) * 8 + (lane % inner) // HEAD
        expand = (jnp.arange(LANES)[:, None] == slot[None, :]).astype(bf16)
        gather = (slot[:, None] == jnp.arange(LANES)[None, :]).astype(bf16)

        q, dl = front(x, maskc, query_weight, query_bias[None], depthwise)
        cot_sent = lax.dynamic_index_in_dim(cotangent, 1 - side, 0, keepdims=False)
        got, cot_sent = lax.optimization_barrier((got, cot_sent))
        got2 = joint(got, count, (1, 1))
        cot_far = across(cot_sent)
        k, v, kc, cv, probs, mixed, weights = mixers(
            place, x, q, dl, maskr, branch_weights[0], got, got2, value_bias[None],
            point_bias[None], conv_bias[None], kw, kb, expand,
        )
        attended, attended_f, lse = attend(q, k, v, segc)

        act_own, act_far, resid, cg, keep, send, small_f = ffn(
            attended, mixed, x, cotangent, cot_far, place, output_weight, output_bias[None],
            first_gain[None], first_shift[None], up_weight, up_bias, down_weight,
            down_bias, second_gain[None], second_shift[None],
        )
        ffn_sum = Sum(keep, send, index, count, pairs)
        marks = []

        def turn(finish, start, held=()):
            held = list(held)
            out = tick(finish, start, held + marks)[: len(held)]
            marks[:] = [chain.value for chain in finish]
            return out

        (cg,) = turn([], [ffn_sum], [cg])
        act_got = across(act_far)
        qc, dg, kcg, kwg, small_c = conv_back(
            q, kc, cv, probs, cg, maskr, weights, kw_wide, gather
        )
        cg, qc = turn([ffn_sum], [ffn_sum], [cg, qc])
        back = []
        for pair in range(inner // LANES):
            out = attend_back(pair, q, k, v, cg, attended_f, lse, segc)
            if pair == 0:
                cg, *out = turn([], [], [cg, *out])
            else:
                cg, act_got, *out = turn([ffn_sum], [ffn_sum], [cg, act_got, *out])
            back.append(tuple(out))
        dqs, dks, dvs = zip(*back)
        keep, send, dqkv, small_w = wgrad(place, x, dqs, dks, dvs, qc)
        last_sum = Sum(keep, send, index, count, fours)
        (kcg,) = turn([], [last_sum], [kcg])
        vg, keep, send, small_v = conv_values(place, x, dl, kcg, probs, cg, maskr, expand)
        dg, vg = turn([ffn_sum, last_sum], [ffn_sum, last_sum], [dg, vg])
        dxd, keep, send = depth_back(
            place, x, dg, maskc, depthwise, kwg, small_f, small_c, small_v, small_w, keep, send
        )
        conv_sum = Sum(keep, send, index, count, [None])
        (dxd,) = turn([ffn_sum, last_sum], [ffn_sum, last_sum, conv_sum], [dxd])
        far = xgrad(place, True, dqkv, vg, dxd, resid, query_weight, weights)
        dxd, far = turn([], [], [dxd, far])
        own = xgrad(place, False, dqkv, vg, dxd, resid, query_weight, weights)
        every = [conv_sum, ffn_sum, last_sum]
        own, far = turn(every, every, [own, far])
        activations = jnp.stack(
            [jnp.where(first, act_own, act_got), jnp.where(first, act_got, act_own)]
        )
        activations, far = turn([ffn_sum, last_sum], [ffn_sum, last_sum], [activations, far])
        grad_got = across(far)
        turn([ffn_sum], [ffn_sum])
        turn([conv_sum], [conv_sum])
        every = [ffn_sum, last_sum, conv_sum]
        (grad_got,) = turn(every, every, [grad_got])
        grad_far = grad_got.astype(f32)
        input_grad = jnp.stack([jnp.where(first, own, grad_far), jnp.where(first, grad_far, own)])
        mine, theirs = ffn_sum.halves()
        down, up, out = unpack_ffn(place, True, mine, hidden)
        down, up, out = unpack_ffn(place, False, theirs, hidden, (down, up, out))
        down = down.reshape(GROUPS, hidden, part)
        spots = jnp.arange(HEADS * KERNEL)
        order = (spots % KERNEL) * 8 + spots // KERNEL
        order = (jnp.arange(LANES)[:, None] == order[None, :]).astype(bf16)
        (
            query_grad, query_bias_grad, stack, value_bias_grad, depth_grad, point_bias_grad,
            kernel_grad, kernel_bias_grad, conv_bias_grad, output_bias_grad, first_gain_grad,
            first_shift_grad, up_bias_grad, down_bias_grad, second_gain_grad, second_shift_grad,
        ) = unpack_mixers(place, *conv_sum.halves(), *last_sum.halves(), order, hidden)

        return (
            activations, input_grad, query_grad, query_bias_grad, stack[None], value_bias_grad,
            depth_grad, point_bias_grad, kernel_grad, kernel_bias_grad[0], conv_bias_grad, out,
            output_bias_grad, first_gain_grad, first_shift_grad, up, up_bias_grad, down,
            down_bias_grad, second_gain_grad, second_shift_grad,
        )

    return run


def solution(mesh):
    branches, ranks = mesh.shape["branch"], mesh.shape["dp"]
    fine = Mesh(mesh.devices.reshape(branches, ranks // 2, 2), AXES)
    whole = P()
    rows = ("chip", "core")
    tokens = P(rows, "branch", None)
    stack = P("branch", None, None, None)
    placed = (
        (P(rows, None, None), P(rows, None), whole, whole, stack) + (whole,) * 16 + (tokens,)
    )
    return jax.shard_map(
        local(dict(fine.shape)),
        mesh=fine,
        in_specs=placed,
        out_specs=(tokens, tokens, whole, whole, stack) + (whole,) * 16,
        check_vma=False,
    )
```

```python
import jax
import jax.numpy as jnp
from jax import lax
from jax.experimental import pallas as pl
from jax.experimental.pallas import tpu as pltpu
from jax.sharding import Mesh
from jax.sharding import PartitionSpec as P

HEADS = 6
HEAD = 64
KERNEL = 9
HALF = KERNEL // 2
GROUPS = 2
DOCS = 8
EPS = 1e-12
BIG = -1e30
SCALE = HEAD**-0.5

PAD = 16
SLOTS = 10
LANES = 128
f32 = jnp.float32
bf16 = jnp.bfloat16


def mm(a, b):
    return jnp.dot(a, b, preferred_element_type=f32)


def mm_nt(a, b):
    return lax.dot_general(a, b, (((1,), (1,)), ((), ())), preferred_element_type=f32)


def mm_tn(a, b):
    return lax.dot_general(a, b, (((0,), (0,)), ((), ())), preferred_element_type=f32)


def params(mib):
    return pltpu.CompilerParams(vmem_limit_bytes=mib * 1024 * 1024)


def cost(flops, nbytes):
    return pl.CostEstimate(flops=int(flops), bytes_accessed=int(nbytes), transcendentals=0)


def window(ref, start, rows, cols):
    return ref[pl.ds(pl.multiple_of(start + PAD - 8, 8), rows + 16), cols]


def moved(win, offset, rows):
    total = rows + 16
    if offset == 0:
        return win[8 : 8 + rows]
    return pltpu.roll(win, (-offset) % total, 0)[8 : 8 + rows]


def clear_pads(ref, length):
    width = ref.shape[1]
    ref[0:PAD, :] = jnp.zeros((PAD, width), f32)
    ref[PAD + length : PAD + length + PAD, :] = jnp.zeros((PAD, width), f32)


def front_body(x_ref, maskc_ref, wq_ref, bq_ref, dw_ref, q_ref, dl_ref, pad):
    length, width = x_ref.shape
    clear_pads(pad, length)
    rows = 32

    @pl.loop(0, length // 128)
    def _(i):
        t0 = pl.multiple_of(i * 128, 128)
        pad[pl.ds(pl.multiple_of(t0 + PAD, 16), 128), :] = x_ref[pl.ds(t0, 128), :].astype(f32)

    @pl.loop(0, length // 256)
    def _(i):
        t0 = pl.multiple_of(i * 256, 256)
        q_ref[pl.ds(t0, 256), :] = (mm(x_ref[pl.ds(t0, 256), :], wq_ref[...]) + bq_ref[...]).astype(
            bf16
        )

    @pl.loop(0, length // rows)
    def _(i):
        t0 = pl.multiple_of(i * rows, rows)
        mask = maskc_ref[pl.ds(t0, rows), :]
        masks = [jnp.broadcast_to(mask[:, j : j + 1], (rows, LANES)) for j in range(KERNEL)]
        for c in range(width // LANES):
            cols = slice(c * LANES, (c + 1) * LANES)
            win = window(pad, t0, rows, cols)
            total = jnp.zeros((rows, LANES), f32)
            for j in range(KERNEL):
                total = total + dw_ref[j : j + 1, cols] * moved(win, j - HALF, rows) * masks[j]
            dl_ref[pl.ds(t0, rows), cols] = total.astype(bf16)


def front(x, maskc, wq, bq, dw):
    length, width = x.shape
    inner = wq.shape[1]
    return pl.pallas_call(
        front_body,
        out_shape=(
            jax.ShapeDtypeStruct((length, inner), bf16),
            jax.ShapeDtypeStruct((length, width), bf16),
        ),
        scratch_shapes=[pltpu.VMEM((length + 2 * PAD, width), f32)],
        compiler_params=params(40),
        cost_estimate=cost(2e10, 8e6),
        name="front",
    )(x, maskc, wq, bq, dw)


def conv_taps(taps, pad, expand_ref, spread, out_ref, length):
    rows = 32
    block = 256
    inner = out_ref.shape[1]

    @pl.loop(0, length // block)
    def _(b):
        b0 = pl.multiple_of(b * block, block)
        for j in range(KERNEL):
            spread[:, j * inner : (j + 1) * inner] = mm(
                taps[pl.ds(b0, block), :], expand_ref[:, j * inner : (j + 1) * inner]
            )

        @pl.loop(0, block // rows)
        def _(i):
            r0 = pl.multiple_of(i * rows, rows)
            t0 = pl.multiple_of(b0 + r0, rows)
            for c in range(inner // LANES):
                cols = slice(c * LANES, (c + 1) * LANES)
                win = window(pad, t0, rows, cols)
                total = jnp.zeros((rows, LANES), f32)
                for j in range(KERNEL):
                    part = spread[pl.ds(r0, rows), j * inner + c * LANES : j * inner + (c + 1) * LANES]
                    total = total + part * moved(win, j - HALF, rows)
                out_ref[pl.ds(t0, rows), cols] = total.astype(bf16)


def taps_in_rows(low_taps, taps, length):
    stacked = jnp.concatenate(low_taps + [jnp.zeros((LANES - 8 * KERNEL, length), f32)], axis=0)
    for b in range(length // LANES):
        piece = stacked[:, b * LANES : (b + 1) * LANES]
        taps[b * LANES : (b + 1) * LANES, :] = jnp.transpose(piece).astype(bf16)


def mixers_body(
    place_ref, x_ref, q_ref, dl_ref, maskr_ref, own_ref, got_ref, got2_ref, bv_ref, bp_ref, bc_ref,
    kw_ref, kb_ref, expand_ref,
    k_ref, v_ref, kc_ref, cv_ref, probs_ref, mixed_ref, w_ref,
    pad, mixing, taps, spread,
):
    length = x_ref.shape[0]
    clear_pads(pad, length)
    side, core = place_ref[0], place_ref[1]
    for n in range(2):
        w_ref[2 * side + n] = own_ref[n]
    w_ref[2 - 2 * side + core] = got_ref[...]
    w_ref[3 - 2 * side - core] = got2_ref[...]

    @pl.loop(0, length // 256)
    def _(i):
        t0 = pl.multiple_of(i * 256, 256)
        now = pl.ds(t0, 256)
        x = x_ref[now, :]
        cv = (mm(x, w_ref[3]) + bc_ref[...]).astype(bf16)
        cv_ref[now, :] = cv
        pad[pl.ds(pl.multiple_of(t0 + PAD, 16), 256), :] = cv.astype(f32)
        kc = (mm(dl_ref[now, :], w_ref[2]) + bp_ref[...]).astype(bf16)
        kc_ref[now, :] = kc
        mixing[now, :] = (kc.astype(f32) * q_ref[now, :].astype(f32)).astype(bf16)
        k_ref[now, :] = mm(x, w_ref[0]).astype(bf16)
        v_ref[now, :] = (mm(x, w_ref[1]) + bv_ref[...]).astype(bf16)

    logits = mm_nt(kw_ref[...], mixing[...]) + kb_ref[:, 0:1]
    rows = [logits[8 * j : 8 * j + 8, :] for j in range(KERNEL)]
    peak = rows[0]
    for r in rows[1:]:
        peak = jnp.maximum(peak, r)
    powers = [jnp.exp(r - peak) for r in rows]
    whole = powers[0]
    for r in powers[1:]:
        whole = whole + r
    share = 1.0 / whole
    low_taps = []
    for j in range(KERNEL):
        probs = powers[j] * share
        probs_ref[8 * j : 8 * j + 8, :] = probs
        low_taps.append(probs.astype(bf16).astype(f32) * maskr_ref[j : j + 1, :])
    taps_in_rows(low_taps, taps, length)
    conv_taps(taps, pad, expand_ref, spread, mixed_ref, length)


def mixers(place, x, q, dl, maskr, own, got, got2, bv, bp, bc, kw, kb, expand):
    length, width = x.shape
    inner = q.shape[1]
    act = jax.ShapeDtypeStruct((length, inner), bf16)
    vm = pl.BlockSpec(memory_space=pltpu.VMEM)
    return pl.pallas_call(
        mixers_body,
        in_specs=[pl.BlockSpec(memory_space=pltpu.SMEM)] + [vm] * 13,
        out_specs=(vm,) * 7,
        out_shape=(
            act, act, act, act, jax.ShapeDtypeStruct((8 * KERNEL, length), f32), act,
            jax.ShapeDtypeStruct((4, width, inner), bf16),
        ),
        scratch_shapes=[
            pltpu.VMEM((length + 2 * PAD, inner), f32),
            pltpu.VMEM((length, inner), bf16),
            pltpu.VMEM((length, LANES), bf16),
            pltpu.VMEM((256, KERNEL * inner), f32),
        ],
        compiler_params=params(48),
        cost_estimate=cost(2e10, 1e7),
        name="mixers",
    )(place, x, q, dl, maskr, own, got, got2, bv, bp, bc, kw, kb, expand)


def head_lanes(shape, head):
    lane = lax.broadcasted_iota(jnp.int32, shape, 1)
    return (lane < HEAD) if head == 0 else (lane >= HEAD)


def only(pair, head):
    return jnp.where(head_lanes(pair.shape, head), pair, jnp.zeros_like(pair))


def attend_body(q_ref, k_ref, v_ref, segc_ref, o_ref, of_ref, lse_ref, kx, vx, qx):
    length = q_ref.shape[0]
    block = length
    lane = lax.broadcasted_iota(jnp.int32, (length, LANES), 1)
    seg = segc_ref[:, 0:LANES]
    same = seg == lane
    qx[:, 0:LANES] = (q_ref[...].astype(f32) * SCALE).astype(bf16)
    qx[:, LANES:] = jnp.where(same, 1.0, 0.0).astype(bf16)
    other = jnp.where((lane < DOCS) & jnp.logical_not(same), BIG, 0.0).astype(bf16)
    for h in range(2):
        kx[h, :, 0:LANES] = only(k_ref[...].astype(f32), h).astype(bf16)
        kx[h, :, LANES:] = other
    vx[:, 0:LANES] = v_ref[...]
    vx[:, LANES:] = jnp.ones((length, LANES), bf16)

    @pl.loop(0, length // block)
    def _(i):
        t0 = pl.multiple_of(i * block, block)
        now = pl.ds(t0, block)
        outs, totals = [], []
        for h in range(2):
            scores = mm_nt(qx[now, :], kx[h])
            peak = jnp.max(scores, axis=-1, keepdims=True)
            powers = jnp.exp(scores - peak).astype(bf16)
            both = mm(powers, vx[...])
            whole = both[:, LANES:]
            outs.append(both[:, 0:LANES] / whole)
            totals.append(peak + jnp.log(whole))
        left = head_lanes((block, LANES), 0)
        out = jnp.where(left, outs[0], outs[1])
        of_ref[now, :] = out
        o_ref[now, :] = out.astype(bf16)
        lse_ref[now, :] = jnp.where(left, totals[0], totals[1])


def attend(q, k, v, segc):
    length, inner = q.shape
    pair = pl.BlockSpec((length, LANES), lambda p: (0, p))
    fixed = pl.BlockSpec((length, LANES), lambda p: (0, 0))
    return pl.pallas_call(
        attend_body,
        grid=(inner // LANES,),
        in_specs=[pair, pair, pair, fixed],
        out_specs=(pair, pair, pair),
        out_shape=(
            jax.ShapeDtypeStruct((length, inner), bf16),
            jax.ShapeDtypeStruct((length, inner), f32),
            jax.ShapeDtypeStruct((length, inner), f32),
        ),
        scratch_shapes=[
            pltpu.VMEM((2, length, 2 * LANES), bf16),
            pltpu.VMEM((length, 2 * LANES), bf16),
            pltpu.VMEM((length, 2 * LANES), bf16),
        ],
        compiler_params=params(62),
        cost_estimate=cost(2e10, 1e7),
        name="attend",
    )(q, k, v, segc)


def pieces(value):
    first = value.astype(bf16).astype(f32)
    rest = value - first
    second = rest.astype(bf16).astype(f32)
    return first, second, rest - second


def extra_lanes(base, values, lane):
    out = base
    for n, value in enumerate(values):
        out = jnp.where(lane == DOCS + n, value, out)
    return out


def attend_back_body(
    q_ref, k_ref, v_ref, do_ref, of_ref, lse_ref, segc_ref, dq_ref, dk_ref, dv_ref,
    kx, vx, qx, dx, kt,
):
    length = q_ref.shape[0]
    lane = lax.broadcasted_iota(jnp.int32, (length, LANES), 1)
    seg = segc_ref[:, 0:LANES]
    same = seg == lane
    q = q_ref[...].astype(f32) * SCALE
    k = k_ref[...].astype(f32)
    v = v_ref[...].astype(f32)
    do = do_ref[...].astype(f32)
    dots = do * of_ref[...]
    lses = lse_ref[...]
    here = jnp.where(same, 1.0, 0.0)
    other = jnp.where((lane < DOCS) & jnp.logical_not(same), BIG, 0.0)
    ones = jnp.where((lane >= DOCS) & (lane < DOCS + 3), 1.0, 0.0)
    for h in range(2):
        kx[h, :, 0:LANES] = only(k, h).astype(bf16)
        kx[h, :, LANES:] = (other + ones).astype(bf16)
        vx[h, :, 0:LANES] = only(v, h).astype(bf16)
        vx[h, :, LANES:] = ones.astype(bf16)
        qx[h, :, 0:LANES] = only(q, h).astype(bf16)
        minus = [-p for p in pieces(lses[:, h * HEAD : h * HEAD + 1])]
        qx[h, :, LANES:] = extra_lanes(here, minus, lane).astype(bf16)
        dx[h, :, 0:LANES] = only(do, h).astype(bf16)
        dot = jnp.sum(only(dots, h), axis=-1, keepdims=True)
        minus = [-p for p in pieces(dot)]
        dx[h, :, LANES:] = extra_lanes(jnp.zeros_like(here), minus, lane).astype(bf16)
        kt[h] = jnp.transpose(only(k, h)).astype(bf16)
    dq, dk, dv = [], [], []
    for h in range(2):
        probs = jnp.exp(mm_nt(kx[h], qx[h]))
        grads = mm_nt(vx[h], dx[h])
        score = (probs * grads).astype(bf16)
        dv.append(mm(probs.astype(bf16), dx[h, :, 0:LANES]))
        dk.append(mm(score, qx[h, :, 0:LANES]))
        dq.append(mm(kt[h], score))
    dq_ref[...] = jnp.transpose(dq[0] + dq[1]) * SCALE
    dk_ref[...] = (dk[0] + dk[1]).astype(bf16)
    dv_ref[...] = (dv[0] + dv[1]).astype(bf16)


def attend_back(pair_no, q, k, v, do, of, lse, segc):
    length, inner = q.shape
    pair = pl.BlockSpec((length, LANES), lambda p: (0, pair_no))
    fixed = pl.BlockSpec((length, LANES), lambda p: (0, 0))
    wide = pltpu.VMEM((2, length, 2 * LANES), bf16)
    return pl.pallas_call(
        attend_back_body,
        grid=(1,),
        in_specs=[pair] * 6 + [fixed],
        out_specs=(fixed, fixed, fixed),
        out_shape=(
            jax.ShapeDtypeStruct((length, LANES), f32),
            jax.ShapeDtypeStruct((length, LANES), bf16),
            jax.ShapeDtypeStruct((length, LANES), bf16),
        ),
        scratch_shapes=[
            wide, wide, wide, wide,
            pltpu.VMEM((2, LANES, length), bf16),
        ],
        compiler_params=params(48),
        cost_estimate=cost(1.2e10, 4e6),
        name="attend_back",
    )(q, k, v, do, of, lse, segc)


def normal_cdf(value):
    power = jnp.exp(-0.5 * (value * value))
    size = jnp.abs(value)
    t = 1.0 / (1.0 + (0.3275911 * 0.7071067811865476) * size)
    poly = 1.061405429 * t - 1.453152027
    poly = poly * t + 1.421413741
    poly = poly * t - 0.284496736
    poly = poly * t + 0.254829592
    tail = (0.5 * poly) * (t * power)
    return jnp.where(value < 0.0, tail, 1.0 - tail), power * 0.3989422804014327


def row_mean(value):
    return jnp.mean(value, axis=-1, keepdims=True)


def fold(value):
    rows, width = value.shape
    return jnp.sum(value.reshape(rows // 8, 8, width), axis=0)


def slabs(count, rows, unroll, body):
    def step(i, carry):
        body(pl.ds(pl.multiple_of(i * rows, rows), rows))
        return carry

    lax.fori_loop(0, count // rows, step, 0, unroll=unroll)


def ffn_body(
    place_ref, at_ref, mx_ref, x_ref, cot_a_ref, cot_b_ref, wo_ref, bo_ref, g1_ref, s1_ref, wu_ref,
    bu_ref, wd_ref, bd_ref, g2_ref, s2_ref,
    act_own_ref, act_far_ref, res_ref, cg_ref, keep_ref, send_ref, small_ref,
    slope, active, up_grad, grouped, low_grad, hid_grad, joined, sums, up_sums, wide, norm, inverse,
):
    step = pl.program_id(0)
    block = at_ref.shape[0]
    blocks = active.shape[0] // block
    inner = at_ref.shape[1]
    width = x_ref.shape[1]
    part = width // GROUPS
    hidden = wu_ref.shape[2]
    chunk = 768
    rows, unroll = block, 1

    @pl.when(step == 0)
    def _():
        sums[...] = jnp.zeros_like(sums)
        up_sums[...] = jnp.zeros_like(up_sums)

    @pl.when(step < blocks)
    def _():
        t0 = pl.multiple_of(step * block, block)
        now = pl.ds(t0, block)
        own = step < blocks // 2
        joined[now, 0:inner] = at_ref[...]
        joined[now, inner:] = mx_ref[...]
        wide[...] = mm(joined[now, :], wo_ref[...])

        def first(slab):
            resid = x_ref[slab, :].astype(f32) + (wide[slab, :] + bo_ref[...])
            center = resid - row_mean(resid)
            inv = lax.rsqrt(row_mean(center * center) + EPS)
            inverse[slab, :] = jnp.broadcast_to(inv, (rows, LANES))
            normed = center * inv
            norm[slab, :] = normed
            grouped[pl.ds(pl.multiple_of(t0 + slab.start, rows), rows), :] = (
                normed * g1_ref[...] + s1_ref[...]
            ).astype(bf16)

        slabs(block, rows, unroll, first)

        for g in range(GROUPS):
            mine = slice(g * part, (g + 1) * part)
            low = None
            for c in range(hidden // chunk):
                cols = slice(c * chunk, (c + 1) * chunk)
                up = mm(grouped[now, mine], wu_ref[g, :, cols]) + bu_ref[g : g + 1, cols]
                cdf, density = normal_cdf(up)
                act = (up * cdf).astype(bf16)
                at = slice(g * hidden + c * chunk, g * hidden + (c + 1) * chunk)
                active[now, at] = act
                slope[:, at] = cdf + up * density
                add = mm(act, wd_ref[g, cols, :])
                low = add if low is None else low + add
            wide[:, mine] = low + bd_ref[g : g + 1, :]

        def second(slab):
            here = pl.ds(pl.multiple_of(t0 + slab.start, rows), rows)
            resid = (norm[slab, :] * g1_ref[...] + s1_ref[...]) + wide[slab, :]
            center = resid - row_mean(resid)
            inv = lax.rsqrt(row_mean(center * center) + EPS)
            normed = center * inv
            result = (normed * g2_ref[...] + s2_ref[...]).astype(bf16)
            hid_grad[here, :] = result
            grad = jnp.where(own, cot_a_ref[slab, :], cot_b_ref[slab, :]).astype(f32)
            sums[0:8, :] += fold(grad * normed)
            sums[8:16, :] += fold(grad)
            gs = grad * g2_ref[...]
            resid = inv * (gs - row_mean(gs) - normed * row_mean(gs * normed))
            wide[slab, :] = resid
            lg = resid.astype(bf16)
            low_grad[here, :] = lg
            sums[16:24, :] += fold(lg.astype(f32))

        slabs(block, rows, unroll, second)

        @pl.when(own)
        def _():
            act_own_ref[...] = hid_grad[now, :]

        @pl.when(jnp.logical_not(own))
        def _():
            act_far_ref[...] = hid_grad[now, :]

        for g in range(GROUPS):
            mine = slice(g * part, (g + 1) * part)
            back = None
            for c in range(hidden // chunk):
                cols = slice(c * chunk, (c + 1) * chunk)
                at = slice(g * hidden + c * chunk, g * hidden + (c + 1) * chunk)
                ag = mm_nt(low_grad[now, mine], wd_ref[g, cols, :])
                ug = (ag * slope[:, at]).astype(bf16)
                up_grad[now, at] = ug
                up_sums[:, at] += fold(ug.astype(f32))
                add = mm_nt(ug, wu_ref[g, :, cols])
                back = add if back is None else back + add
            wide[:, mine] += back

        def third(slab):
            here = pl.ds(pl.multiple_of(t0 + slab.start, rows), rows)
            grad = wide[slab, :]
            normed = norm[slab, :]
            inv = inverse[slab, 0:1]
            sums[24:32, :] += fold(grad * normed)
            sums[32:40, :] += fold(grad)
            gs = grad * g1_ref[...]
            resid = inv * (gs - row_mean(gs) - normed * row_mean(gs * normed))
            res_ref[slab, :] = resid
            hg = resid.astype(bf16)
            hid_grad[here, :] = hg
            sums[40:48, :] += fold(hg.astype(f32))

        slabs(block, rows, unroll, third)
        cg_ref[...] = mm_nt(hid_grad[now, :], wo_ref[...]).astype(bf16)

    per = hidden // 768

    def weight_grad(half, n):
        mine = slice(half * part, (half + 1) * part)
        if n < per:
            cols = slice(half * hidden + n * 768, half * hidden + (n + 1) * 768)
            return mm_tn(active[:, cols], low_grad[:, mine]).astype(bf16)
        if n < 2 * per:
            n -= per
            cols = slice(half * hidden + n * 768, half * hidden + (n + 1) * 768)
            value = mm_tn(grouped[:, mine], up_grad[:, cols]).astype(bf16)
        else:
            value = mm_tn(joined[:, mine], hid_grad[...]).astype(bf16)
        return jnp.concatenate([value[:, 0:part], value[:, part:]], axis=0)

    for n in range(2 * per + 1):

        @pl.when(step == blocks + n)
        def _():
            for half in range(2):
                store_half(
                    place_ref[1], half, keep_ref, send_ref, slice(None), weight_grad(half, n)
                )

    @pl.when(step == blocks)
    def _():
        across = width // 384
        small_ref[...] = jnp.zeros_like(small_ref)
        for n in range(6):
            line = jnp.sum(sums[8 * n : 8 * n + 8, :], axis=0, keepdims=True)
            for c in range(across):
                small_ref[across * n + c : across * n + c + 1, :] = line[:, c * 384 : (c + 1) * 384]
        line = jnp.sum(up_sums[...], axis=0, keepdims=True)
        for c in range(GROUPS * hidden // 384):
            at = 6 * across + c
            small_ref[at : at + 1, :] = line[:, c * 384 : (c + 1) * 384]


def store_half(core, half, keep_ref, send_ref, rows, value):
    @pl.when(core == half)
    def _():
        keep_ref[rows, :] = value

    @pl.when(core != half)
    def _():
        send_ref[rows, :] = value


def ffn(at, mx, x, cot, cot_far, place, wo, bo, g1, s1, wu, bu, wd, bd, g2, s2):
    length, width = x.shape
    inner = at.shape[1]
    block = length // 2
    blocks = length // block
    near = blocks // 2
    hidden = wu.shape[2]
    gsteps = 2 * (hidden // 768) + 1

    def turn(step, side_ref):
        s = jnp.minimum(step, blocks - 1)
        return (s + side_ref[0] * near) % blocks

    def tok(cols):
        return pl.BlockSpec((block, cols), lambda s, b: (turn(s, b), 0))

    def full(shape):
        return pl.BlockSpec(shape, lambda s, b: (0,) * len(shape), pipeline_mode=pl.Buffered(1))

    def near_map(s, b):
        return (jnp.minimum(s, near - 1), 0)

    def far_map(s, b):
        return (jnp.clip(s - near, 0, near - 1), 0)

    def cot_map(s, b):
        return (b[0], jnp.minimum(s, near - 1), 0)

    return pl.pallas_call(
        ffn_body,
        grid_spec=pltpu.PrefetchScalarGridSpec(
            num_scalar_prefetch=1,
            grid=(blocks + gsteps,),
            in_specs=[
                tok(inner), tok(inner), tok(width),
                pl.BlockSpec((None, block, width), cot_map),
                pl.BlockSpec((block, width), far_map),
                full(wo.shape), full(bo.shape), full(g1.shape), full(s1.shape), full(wu.shape),
                full(bu.shape), full(wd.shape), full(bd.shape), full(g2.shape), full(s2.shape),
            ],
            out_specs=(
                pl.BlockSpec((block, width), near_map),
                pl.BlockSpec((block, width), far_map),
                tok(width),
                tok(width),
                pl.BlockSpec((768, 384), lambda s, b: (jnp.maximum(s - blocks, 0), 0)),
                pl.BlockSpec((768, 384), lambda s, b: (jnp.maximum(s - blocks, 0), 0)),
                pl.BlockSpec((32, 384), lambda s, b: (0, 0)),
            ),
            scratch_shapes=[
                pltpu.VMEM((block, GROUPS * hidden), f32),
                pltpu.VMEM((length, GROUPS * hidden), bf16),
                pltpu.VMEM((length, GROUPS * hidden), bf16),
                pltpu.VMEM((length, width), bf16),
                pltpu.VMEM((length, width), bf16),
                pltpu.VMEM((length, width), bf16),
                pltpu.VMEM((length, width), bf16),
                pltpu.VMEM((48, width), f32),
                pltpu.VMEM((8, GROUPS * hidden), f32),
                pltpu.VMEM((block, width), f32),
                pltpu.VMEM((block, width), f32),
                pltpu.VMEM((block, LANES), f32),
            ],
        ),
        out_shape=(
            jax.ShapeDtypeStruct((length // 2, width), bf16),
            jax.ShapeDtypeStruct((length // 2, width), bf16),
            jax.ShapeDtypeStruct((length, width), f32),
            jax.ShapeDtypeStruct((length, width), bf16),
            jax.ShapeDtypeStruct((gsteps * 768, 384), bf16),
            jax.ShapeDtypeStruct((gsteps * 768, 384), bf16),
            jax.ShapeDtypeStruct((32, 384), f32),
        ),
        compiler_params=params(60),
        cost_estimate=cost(4e10, 3e7),
        name="ffn",
    )(place, at, mx, x, cot, cot_far, wo, bo, g1, s1, wu, bu, wd, bd, g2, s2)


def conv_back_body(
    q_ref, kc_ref, cv_ref, probs_ref, cg_ref, maskr_ref, w_ref, kw_ref, gather_ref,
    qc_ref, dg_ref, kcg, kwg_ref, small_ref,
    pad, prod, taps, kvg, sums,
):
    length, inner = q_ref.shape
    block, rows = 256, 32
    clear_pads(pad, length)

    @pl.loop(0, length // block)
    def _(i):
        t0 = pl.multiple_of(i * block, block)
        pad[pl.ds(pl.multiple_of(t0 + PAD, 16), block), :] = cv_ref[pl.ds(t0, block), :].astype(f32)

    tap_grads = []
    for b in range(length // block):

        @pl.loop(0, block // rows)
        def _(i):
            r0 = pl.multiple_of(i * rows, rows)
            t0 = pl.multiple_of(b * block + r0, rows)
            for c in range(inner // LANES):
                cols = slice(c * LANES, (c + 1) * LANES)
                win = window(pad, t0, rows, cols)
                mg = cg_ref[pl.ds(t0, rows), inner + c * LANES : inner + (c + 1) * LANES].astype(f32)
                for j in range(KERNEL):
                    prod[pl.ds(r0, rows), j * inner + c * LANES : j * inner + (c + 1) * LANES] = (
                        mg * moved(win, j - HALF, rows)
                    ).astype(bf16)

        tap_grads.append(jnp.transpose(mm(prod[...], gather_ref[...])))
    tap_grad = jnp.concatenate(tap_grads, axis=1)
    probs = [probs_ref[8 * j : 8 * j + 8, :] for j in range(KERNEL)]
    grads = [tap_grad[8 * j : 8 * j + 8, :] * maskr_ref[j : j + 1, :] for j in range(KERNEL)]
    dot = probs[0] * grads[0]
    for j in range(1, KERNEL):
        dot = dot + probs[j] * grads[j]
    rest = jnp.zeros((LANES - 8 * KERNEL, length), f32)
    logit = [(probs[j] * (grads[j] - dot)).astype(bf16).astype(f32) for j in range(KERNEL)]
    logit = jnp.concatenate(logit + [rest], axis=0)
    small_ref[...] = jnp.zeros_like(small_ref)
    for b in range(length // LANES):
        taps[b * LANES : (b + 1) * LANES, :] = jnp.transpose(
            logit[:, b * LANES : (b + 1) * LANES]
        ).astype(bf16)
    small_ref[0:1, 0:LANES] = jnp.sum(taps[...].astype(f32), axis=0, keepdims=True)
    sums[...] = jnp.zeros_like(sums)

    @pl.loop(0, length // block)
    def _(i):
        now = pl.ds(pl.multiple_of(i * block, block), block)
        mix_grad = mm(taps[now, :], kw_ref[...])
        q = q_ref[now, :].astype(f32)
        kc = kc_ref[now, :].astype(f32)
        low = (mix_grad * q).astype(bf16)
        kcg[now, :] = low
        kvg[now, :] = (kc * q).astype(bf16)
        sums[...] += fold(low.astype(f32))
        qc_ref[now, :] = mix_grad * kc
        dg_ref[now, :] = mm_nt(low, w_ref[2])

    kwg_ref[...] = mm_tn(taps[...], kvg[...]).astype(bf16)
    small_ref[1:2, :] = jnp.sum(sums[...], axis=0, keepdims=True)


def conv_back(q, kc, cv, probs, cg, maskr, weights, kw, gather):
    length, inner = q.shape
    width = cg.shape[1]
    return pl.pallas_call(
        conv_back_body,
        out_shape=(
            jax.ShapeDtypeStruct((length, inner), f32),
            jax.ShapeDtypeStruct((length, width), f32),
            jax.ShapeDtypeStruct((length, inner), bf16),
            jax.ShapeDtypeStruct((LANES, inner), bf16),
            jax.ShapeDtypeStruct((8, inner), f32),
        ),
        scratch_shapes=[
            pltpu.VMEM((length + 2 * PAD, inner), f32),
            pltpu.VMEM((256, KERNEL * inner), bf16),
            pltpu.VMEM((length, LANES), bf16),
            pltpu.VMEM((length, inner), bf16),
            pltpu.VMEM((8, inner), f32),
        ],
        compiler_params=params(48),
        cost_estimate=cost(1.2e10, 1e7),
        name="conv_back",
    )(q, kc, cv, probs, cg, maskr, weights, kw, gather)


def conv_values_body(
    place_ref, x_ref, dl_ref, kcg_ref, probs_ref, cg_ref, maskr_ref, expand_ref,
    vg_ref, kept_ref, sent_ref, small_ref,
    pad, taps, spread,
):
    length, width = x_ref.shape
    inner = kcg_ref.shape[1]
    block = 256
    clear_pads(pad, length)

    @pl.loop(0, length // block)
    def _(i):
        t0 = pl.multiple_of(i * block, block)
        pad[pl.ds(pl.multiple_of(t0 + PAD, 16), block), :] = cg_ref[
            pl.ds(t0, block), inner:
        ].astype(f32)

    low_taps = []
    for j in range(KERNEL):
        back = KERNEL - 1 - j
        low = probs_ref[8 * back : 8 * back + 8, :].astype(bf16).astype(f32)
        low = low * maskr_ref[back : back + 1, :]
        shift = (HALF - j) % length
        low_taps.append(pltpu.roll(low, shift, 1) if shift else low)
    taps_in_rows(low_taps, taps, length)
    conv_taps(taps, pad, expand_ref, spread, vg_ref, length)
    total = jnp.zeros((8, inner), f32)
    for i in range(length // block):
        total = total + fold(vg_ref[i * block : (i + 1) * block, :].astype(f32))
    small_ref[...] = jnp.zeros_like(small_ref)
    small_ref[0:1, :] = jnp.sum(total, axis=0, keepdims=True)
    core = place_ref[1]
    rows = slice(0, width)
    store_half(core, 0, kept_ref, sent_ref, rows, mm_tn(dl_ref[...], kcg_ref[...]).astype(bf16))
    store_half(core, 1, kept_ref, sent_ref, rows, mm_tn(x_ref[...], vg_ref[...]).astype(bf16))


def conv_values(place, x, dl, kcg, probs, cg, maskr, expand):
    length, width = x.shape
    inner = kcg.shape[1]
    vm = pl.BlockSpec(memory_space=pltpu.VMEM)
    return pl.pallas_call(
        conv_values_body,
        in_specs=[pl.BlockSpec(memory_space=pltpu.SMEM)] + [vm] * 7,
        out_specs=(vm,) * 4,
        out_shape=(
            jax.ShapeDtypeStruct((length, inner), bf16),
            jax.ShapeDtypeStruct((width + LANES, inner), bf16),
            jax.ShapeDtypeStruct((width + LANES, inner), bf16),
            jax.ShapeDtypeStruct((8, inner), f32),
        ),
        scratch_shapes=[
            pltpu.VMEM((length + 2 * PAD, inner), f32),
            pltpu.VMEM((length, LANES), bf16),
            pltpu.VMEM((256, KERNEL * inner), f32),
        ],
        compiler_params=params(48),
        cost_estimate=cost(1.2e10, 1e7),
        name="conv_values",
    )(place, x, dl, kcg, probs, cg, maskr, expand)


def depth_back_body(
    place_ref, x_ref, dg_ref, maskc_ref, dw_ref, kwg_ref, sf_ref, sc_ref, sv_ref, sw_ref,
    kept_ref, sent_ref, dx_ref, keep_ref, send_ref, gpad, dkg,
):
    length, width = x_ref.shape
    block, rows = 256, 32
    clear_pads(gpad, length)
    dkg[...] = jnp.zeros_like(dkg)

    @pl.loop(0, length // block)
    def _(i):
        t0 = pl.multiple_of(i * block, block)
        gpad[pl.ds(pl.multiple_of(t0 + PAD, 16), block), :] = dg_ref[pl.ds(t0, block), :]

    @pl.loop(0, length // rows)
    def _(i):
        t0 = pl.multiple_of(i * rows, rows)
        mask = maskc_ref[pl.ds(t0, rows), :]
        masks = [jnp.broadcast_to(mask[:, j : j + 1], (rows, LANES)) for j in range(KERNEL)]
        for c in range(width // LANES):
            cols = slice(c * LANES, (c + 1) * LANES)
            win = window(gpad, t0, rows, cols)
            x = x_ref[pl.ds(t0, rows), cols].astype(f32)
            total = jnp.zeros((rows, LANES), f32)
            for j in range(KERNEL):
                back = KERNEL - 1 - j
                part = moved(win, j - HALF, rows) * masks[j]
                total = total + dw_ref[back : back + 1, cols] * part
                dkg[8 * back : 8 * back + 8, cols] += fold(part * x)
            dx_ref[pl.ds(t0, rows), cols] = total

    across = width // 384
    lines = []
    for j in range(KERNEL):
        line = jnp.sum(dkg[8 * j : 8 * j + 8, :], axis=0, keepdims=True)
        lines += [line[:, c * 384 : (c + 1) * 384] for c in range(across)]
    smalls = [sf_ref[...], sc_ref[...], sv_ref[...], sw_ref[...]] + lines
    used = sum(v.shape[0] for v in smalls)
    smalls = jnp.concatenate(smalls + [jnp.zeros((LANES - used, 384), f32)], axis=0)
    core = place_ref[1]
    keep_ref[0:width, :] = kept_ref[0:width, :]
    send_ref[0:width, :] = sent_ref[0:width, :]
    rows = slice(width, width + LANES)
    store_half(core, 0, keep_ref, send_ref, rows, kwg_ref[...])
    store_half(core, 1, keep_ref, send_ref, rows, smalls.astype(bf16))


def depth_back(place, x, dg, maskc, dw, kwg, sf, sc, sv, sw, kept, sent):
    length, width = x.shape
    vm = pl.BlockSpec(memory_space=pltpu.VMEM)
    return pl.pallas_call(
        depth_back_body,
        in_specs=[pl.BlockSpec(memory_space=pltpu.SMEM)] + [vm] * 11,
        out_specs=(vm,) * 3,
        out_shape=(
            jax.ShapeDtypeStruct((length, width), f32),
            jax.ShapeDtypeStruct(kept.shape, bf16),
            jax.ShapeDtypeStruct(kept.shape, bf16),
        ),
        scratch_shapes=[
            pltpu.VMEM((length + 2 * PAD, width), f32),
            pltpu.VMEM((8 * KERNEL, width), f32),
        ],
        compiler_params=params(40),
        cost_estimate=cost(1.2e10, 1e7),
        name="depth_back",
    )(place, x, dg, maskc, dw, kwg, sf, sc, sv, sw, kept, sent)


def wgrad_body(
    place_ref, x_ref, *refs
):
    pairs = 3
    dqs, dks, dvs = refs[0:pairs], refs[pairs : 2 * pairs], refs[2 * pairs : 3 * pairs]
    qc_ref, keep_ref, send_ref, dqkv_ref, small_ref = refs[3 * pairs :]
    length, width = x_ref.shape
    inner = qc_ref.shape[1]
    for p in range(pairs):
        cols = slice(p * LANES, (p + 1) * LANES)
        dqkv_ref[:, cols] = (dqs[p][...] + qc_ref[:, cols]).astype(bf16)
        dqkv_ref[:, inner + p * LANES : inner + (p + 1) * LANES] = dks[p][...]
        dqkv_ref[:, 2 * inner + p * LANES : 2 * inner + (p + 1) * LANES] = dvs[p][...]
    core = place_ref[1]
    step = 384
    count = 3 * (width // step)
    for n in range(count):
        which, piece = divmod(n, width // step)
        value = mm_tn(
            x_ref[:, piece * step : (piece + 1) * step],
            dqkv_ref[:, which * inner : (which + 1) * inner],
        ).astype(bf16)
        half, at = divmod(n, count // 2)
        store_half(core, half, keep_ref, send_ref, slice(at * step, (at + 1) * step), value)
    total = jnp.zeros((8, 3 * inner), f32)
    for i in range(length // 256):
        total = total + fold(dqkv_ref[i * 256 : (i + 1) * 256, :].astype(f32))
    line = jnp.sum(total, axis=0, keepdims=True)
    small_ref[...] = jnp.zeros_like(small_ref)
    for which in range(3):
        small_ref[which : which + 1, :] = line[:, which * inner : (which + 1) * inner]


def wgrad(place, x, dqs, dks, dvs, qc):
    length, width = x.shape
    inner = qc.shape[1]
    rows = 3 * width // 2
    vm = pl.BlockSpec(memory_space=pltpu.VMEM)
    return pl.pallas_call(
        wgrad_body,
        in_specs=[pl.BlockSpec(memory_space=pltpu.SMEM)] + [vm] * 11,
        out_specs=(vm,) * 4,
        out_shape=(
            jax.ShapeDtypeStruct((rows, inner), bf16),
            jax.ShapeDtypeStruct((rows, inner), bf16),
            jax.ShapeDtypeStruct((length, 3 * inner), bf16),
            jax.ShapeDtypeStruct((8, inner), f32),
        ),
        compiler_params=params(40),
        cost_estimate=cost(6e9, 1e7),
        name="wgrad",
    )(place, x, *dqs, *dks, *dvs, qc)


def xgrad_body(place_ref, dqkv_ref, vg_ref, dxd_ref, res_ref, wq_ref, w_ref, out_ref):
    inner = vg_ref.shape[1]
    total = res_ref[...] + dxd_ref[...]
    total = total + mm_nt(vg_ref[...], w_ref[3])
    total = total + mm_nt(dqkv_ref[:, 0:inner], wq_ref[...])
    total = total + mm_nt(dqkv_ref[:, inner : 2 * inner], w_ref[0])
    total = total + mm_nt(dqkv_ref[:, 2 * inner :], w_ref[1])
    out_ref[...] = total.astype(out_ref.dtype)


def xgrad(place, far, dqkv, vg, dxd, res, wq, weights):
    length, width = res.shape
    inner = vg.shape[1]
    block = 256
    near = length // 2 // block

    def tok(cols):
        def index(s, b):
            half = 1 - b[0] if far else b[0]
            return (half * near + s, 0)

        return pl.BlockSpec((block, cols), index)

    def full(shape):
        return pl.BlockSpec(shape, lambda s, b: (0,) * len(shape), pipeline_mode=pl.Buffered(1))

    return pl.pallas_call(
        xgrad_body,
        grid_spec=pltpu.PrefetchScalarGridSpec(
            num_scalar_prefetch=1,
            grid=(near,),
            in_specs=[
                tok(3 * inner), tok(inner), tok(width), tok(width), full(wq.shape),
                full(weights.shape),
            ],
            out_specs=pl.BlockSpec((block, width), lambda s, b: (s, 0)),
        ),
        out_shape=jax.ShapeDtypeStruct((length // 2, width), bf16 if far else f32),
        compiler_params=params(40),
        cost_estimate=cost(1e6, 1e4),
        name="xgrad_far" if far else "xgrad_own",
    )(place, dqkv, vg, dxd, res, wq, weights)


def unpack_ffn_body(place_ref, source_ref, *refs):
    down_ref, up_ref, out_ref = refs[-3:]
    step = pl.program_id(0)
    per = pl.num_programs(0)
    value = source_ref[...].astype(f32)
    half = value.shape[0] // 2

    @pl.when(step < per // 2)
    def _():
        down_ref[...] = value

    @pl.when((step >= per // 2) & (step < per - 1))
    def _():
        up_ref[:, 0:384] = value[:half]
        up_ref[:, 384:] = value[half:]

    @pl.when(step == per - 1)
    def _():
        out_ref[:, 0:384] = value[:half]
        out_ref[:, 384:] = value[half:]


def unpack_ffn(place, mine, source, hidden, before=()):
    rows, part = source.shape
    per = rows // 768
    each = per // 2

    def half(b):
        return b[1] if mine else 1 - b[1]

    return pl.pallas_call(
        unpack_ffn_body,
        grid_spec=pltpu.PrefetchScalarGridSpec(
            num_scalar_prefetch=1,
            grid=(per,),
            in_specs=[pl.BlockSpec((768, part), lambda s, b: (s, 0))]
            + [pl.BlockSpec(memory_space=pl.ANY)] * len(before),
            out_specs=(
                pl.BlockSpec(
                    (768, part), lambda s, b: (each * half(b) + jnp.minimum(s, each - 1), 0)
                ),
                pl.BlockSpec(
                    (None, part, 768), lambda s, b: (half(b), 0, jnp.clip(s - each, 0, each - 1))
                ),
                pl.BlockSpec((part, 2 * part), lambda s, b: (half(b), 0)),
            ),
        ),
        out_shape=(
            jax.ShapeDtypeStruct((GROUPS * hidden, part), f32),
            jax.ShapeDtypeStruct((GROUPS, part, hidden), f32),
            jax.ShapeDtypeStruct((2 * part, 2 * part), f32),
        ),
        input_output_aliases={2 + n: n for n in range(len(before))},
        compiler_params=params(32),
        cost_estimate=cost(1e6, 1e7),
        name="unpack_mine" if mine else "unpack_theirs",
    )(place, source, *before)


def unpack_mixers_body(place_ref, cm_ref, cg_ref, am_ref, ag_ref, order_ref, *outs):
    (
        query_ref, query_bias_ref, stack_ref, value_bias_ref, depth_ref, point_ref, kernel_ref,
        kernel_bias_ref, conv_ref, out_bias_ref, gain1_ref, shift1_ref, up_bias_ref, down_bias_ref,
        gain2_ref, shift2_ref,
    ) = outs
    width = query_ref.shape[0]
    half = width // 2
    across = width // 384
    for core in range(2):

        @pl.when(place_ref[1] == core)
        def _():
            conv = (cm_ref, cg_ref) if core == 0 else (cg_ref, cm_ref)
            rest = (am_ref, ag_ref) if core == 0 else (ag_ref, am_ref)
            query_ref[...] = rest[0][0:width, :].astype(f32)

            @pl.when(place_ref[0] == 0)
            def _():
                stack_ref[0, 0:half, :] = rest[0][width:, :].astype(f32)
                stack_ref[0, half:, :] = rest[1][0:half, :].astype(f32)
                stack_ref[1] = rest[1][half:, :].astype(f32)

            @pl.when(place_ref[0] != 0)
            def _():
                stack_ref[0] = conv[0][0:width, :].astype(f32)
                stack_ref[1] = conv[1][0:width, :].astype(f32)

            kernel_ref[...] = mm_tn(conv[0][width:, :], order_ref[...])
            small = conv[1][width:, :]
            kernel_bias_ref[...] = mm(small[32:40, 0:LANES], order_ref[...])[0:1]
            small = small.astype(f32)
            for n, ref in enumerate((gain2_ref, shift2_ref, None, gain1_ref, shift1_ref, out_bias_ref)):
                for c in range(across):
                    line = small[across * n + c : across * n + c + 1, :]
                    if ref is None:
                        down_bias_ref[c : c + 1, :] = line
                    else:
                        ref[c * 384 : (c + 1) * 384] = line.reshape(384)
            per = up_bias_ref.shape[1] // 384
            for g in range(GROUPS):
                for c in range(per):
                    at = 6 * across + g * per + c
                    up_bias_ref[g : g + 1, c * 384 : (c + 1) * 384] = small[at : at + 1, :]
            point_ref[...] = small[33:34, :].reshape(384)
            conv_ref[...] = small[40:41, :].reshape(384)
            query_bias_ref[...] = small[48:49, :].reshape(384)
            value_bias_ref[...] = small[50:51, :].reshape(384)
            for j in range(KERNEL):
                for c in range(across):
                    at = 56 + across * j + c
                    depth_ref[j : j + 1, c * 384 : (c + 1) * 384] = small[at : at + 1, :]


def unpack_mixers(place, conv_mine, conv_got, mine, got, order, hidden):
    inner = conv_mine.shape[1]
    width = mine.shape[0] * 2 // 3
    vm = pl.BlockSpec(memory_space=pltpu.VMEM)
    shapes = (
        (width, inner), (inner,), (2, width, inner), (inner,), (KERNEL, width), (inner,),
        (inner, HEADS * KERNEL), (1, HEADS * KERNEL), (inner,), (width,), (width,), (width,),
        (GROUPS, hidden), (GROUPS, width // GROUPS), (width,), (width,),
    )
    return pl.pallas_call(
        unpack_mixers_body,
        in_specs=[pl.BlockSpec(memory_space=pltpu.SMEM)] + [vm] * 5,
        out_specs=(vm,) * len(shapes),
        out_shape=tuple(jax.ShapeDtypeStruct(shape, f32) for shape in shapes),
        compiler_params=params(32),
        cost_estimate=cost(1e6, 8e6),
        name="unpack_mixers",
    )(place, conv_mine, conv_got, mine, got, order)


AXES = ("branch", "chip", "core")
CHIPS = ("branch", "chip")


def joint(value, count, masks):
    return lax.ppermute(value, AXES, [(i, i ^ masks[i & 1]) for i in range(count)])


def added(values):
    total = values[0].astype(f32)
    for v in values[1:]:
        total = total + v.astype(f32)
    return total.astype(bf16)


class Sum:
    def __init__(self, kept, sent, index, count, plan):
        self.index, self.count = index, count
        self.plan = [[(1, 1)]] + plan
        self.depth = 0
        self.value, self.sent = kept, [sent]
        self.got = None
        self.down = True

    def hops(self):
        phase = self.plan[self.depth]
        if len(phase) == 1:
            return phase
        (a, b), (c, d) = phase
        return [(a, b), (c, d), (a ^ c, b ^ d)]

    def spot(self):
        at = jnp.int32(0)
        for n, masks in enumerate(self.plan[self.depth]):
            mask = jnp.where(self.index % 2 == 0, masks[0], masks[1])
            at = at + jnp.where((self.index & mask) != 0, 1 << n, 0)
        return at

    def start(self):
        if self.plan[self.depth] is None:
            ways = self.count // 2
            sent = self.value
            if not self.down:
                sent = jnp.broadcast_to(sent[None], (ways,) + sent.shape)
                sent = sent.reshape(-1, sent.shape[-1])
            self.got = [lax.all_to_all(sent, CHIPS, split_axis=0, concat_axis=0, tiled=True)]
            return
        hops = self.hops()
        sent = self.sent if self.down else [self.value] * len(hops)
        self.got = [joint(v, self.count, masks) for v, masks in zip(sent, hops)]

    def finish(self):
        got, self.got = self.got, None
        if not self.down:
            self.value = self.joined(got)
            self.depth -= 1
            return
        if self.plan[self.depth] is None:
            ways = self.count // 2
            pieces = got[0].reshape(ways, got[0].shape[0] // ways, got[0].shape[1])
            total = [jnp.sum(pieces.astype(f32), axis=0)]
        else:
            total = [self.value] + got
        self.depth += 1
        if self.depth == len(self.plan) or self.plan[self.depth] is None:
            self.value, self.sent = added(total), []
            if self.depth == len(self.plan):
                self.down = False
                self.depth -= 1
            return
        spot = self.spot()
        ways = len(self.hops()) + 1
        rows = total[0].shape[0] // ways
        pieces = []
        for k in range(ways):
            at = (spot ^ k) * rows
            pieces.append(added([lax.dynamic_slice_in_dim(v, at, rows, 0) for v in total]))
        self.value, self.sent = pieces[0], pieces[1:]

    def joined(self, got):
        if self.plan[self.depth] is None:
            return got[0]
        spot = self.spot()
        if len(got) == 1:
            first = spot == 0
            return jnp.concatenate(
                [jnp.where(first, self.value, got[0]), jnp.where(first, got[0], self.value)]
            )
        rows = self.value.shape[0]
        whole = jnp.zeros((4 * rows, self.value.shape[1]), self.value.dtype)
        for k, piece in enumerate([self.value] + got):
            whole = lax.dynamic_update_slice_in_dim(whole, piece, (spot ^ k) * rows, 0)
        return whole

    @property
    def last(self):
        return not self.down and self.depth == 0

    def live(self):
        return [self.value] + self.sent

    def put(self, values):
        self.value, self.sent = values[0], list(values[1:])

    def halves(self):
        while True:
            if self.got is None:
                self.start()
            if self.last:
                return self.value, self.got[0]
            self.finish()


def tick(finish, start, held=()):
    for chain in finish:
        if chain.got is not None and not chain.last:
            chain.finish()
    chains = [chain for chain in dict.fromkeys(list(finish) + list(start)) if chain.got is None]
    flat = [v for chain in chains for v in chain.live()]
    tied = lax.optimization_barrier(tuple(flat) + tuple(held))
    at = 0
    for chain in chains:
        n = len(chain.live())
        chain.put(tied[at : at + n])
        at += n
    for chain in start:
        if chain.got is None:
            chain.start()
    return tied[at:]


def local(sizes):
    chips = sizes["chip"]
    along = 2 * chips
    count = along * sizes["branch"]
    masks = [2 << n for n in range(chips.bit_length() - 1)]
    masks.insert(min(2, len(masks)), along)
    swapped = list(masks)
    for n in range(0, len(masks) - 1, 2):
        swapped[n], swapped[n + 1] = masks[n + 1], masks[n]
    pairs = [[both] for both in zip(masks, swapped)]
    near = [along] + [m for m in masks if m != along]
    fours = [[(m, m) for m in near[n : n + 2]] for n in range(0, len(near), 2)]

    def run(
        inputs, segments, query_weight, query_bias, branch_weights, value_bias, depthwise,
        point_bias, kernel_weight, kernel_bias, conv_bias, output_weight, output_bias, first_gain,
        first_shift, up_weight, up_bias, down_weight, down_bias, second_gain, second_shift,
        cotangent,
    ):
        seqs, length, width = inputs.shape
        inner = query_weight.shape[1]
        hidden = up_weight.shape[2]
        part = width // GROUPS
        side = lax.axis_index("branch").astype(jnp.int32)
        core = lax.axis_index("core").astype(jnp.int32)
        index = side * along + 2 * lax.axis_index("chip").astype(jnp.int32) + core
        place = jnp.stack([side, core])
        first = side == 0

        def across(value):
            return joint(value, count, (along, along))

        got = across(lax.dynamic_index_in_dim(branch_weights[0], core, 0, keepdims=False))
        x = lax.dynamic_index_in_dim(inputs, side, 0, keepdims=False)
        seg = lax.dynamic_index_in_dim(segments, side, 0, keepdims=False)

        spots = jnp.arange(length)
        around = spots[None, :] + (jnp.arange(KERNEL) - HALF)[:, None]
        inside = (around >= 0) & (around < length)
        padded = jnp.pad(seg, (HALF, HALF), constant_values=-1)
        near = jnp.stack([lax.slice_in_dim(padded, j, j + length) for j in range(KERNEL)])
        maskr = ((near == seg[None, :]) & inside).astype(f32)
        maskr = jnp.pad(maskr, ((0, 16 - KERNEL), (0, 0)))
        maskc = maskr.T
        segc = jnp.broadcast_to(seg[:, None], (length, LANES))

        kw = kernel_weight.reshape(inner, HEADS, KERNEL).transpose(2, 1, 0)
        kw = jnp.pad(kw, ((0, 0), (0, 8 - HEADS), (0, 0))).reshape(8 * KERNEL, inner)
        kw_wide = jnp.pad(kw, ((0, LANES - 8 * KERNEL), (0, 0)))
        kb = kernel_bias.reshape(HEADS, KERNEL).T
        kb = jnp.pad(kb, ((0, 0), (0, 8 - HEADS))).reshape(8 * KERNEL, 1)
        kb = jnp.broadcast_to(kb, (8 * KERNEL, LANES))

        lane = jnp.arange(KERNEL * inner)
        slot = (lane // inner) * 8 + (lane % inner) // HEAD
        expand = (jnp.arange(LANES)[:, None] == slot[None, :]).astype(bf16)
        gather = (slot[:, None] == jnp.arange(LANES)[None, :]).astype(bf16)

        q, dl = front(x, maskc, query_weight, query_bias[None], depthwise)
        cot_sent = lax.dynamic_index_in_dim(cotangent, 1 - side, 0, keepdims=False)
        got, cot_sent = lax.optimization_barrier((got, cot_sent))
        got2 = joint(got, count, (1, 1))
        cot_far = across(cot_sent)
        k, v, kc, cv, probs, mixed, weights = mixers(
            place, x, q, dl, maskr, branch_weights[0], got, got2, value_bias[None],
            point_bias[None], conv_bias[None], kw, kb, expand,
        )
        attended, attended_f, lse = attend(q, k, v, segc)

        act_own, act_far, resid, cg, keep, send, small_f = ffn(
            attended, mixed, x, cotangent, cot_far, place, output_weight, output_bias[None],
            first_gain[None], first_shift[None], up_weight, up_bias, down_weight,
            down_bias, second_gain[None], second_shift[None],
        )
        ffn_sum = Sum(keep, send, index, count, pairs)
        marks = []

        def turn(finish, start, held=()):
            held = list(held)
            out = tick(finish, start, held + marks)[: len(held)]
            marks[:] = [chain.value for chain in finish]
            return out

        (cg,) = turn([], [ffn_sum], [cg])
        act_got = across(act_far)
        qc, dg, kcg, kwg, small_c = conv_back(
            q, kc, cv, probs, cg, maskr, weights, kw_wide, gather
        )
        cg, qc = turn([ffn_sum], [ffn_sum], [cg, qc])
        back = []
        for pair in range(inner // LANES):
            out = attend_back(pair, q, k, v, cg, attended_f, lse, segc)
            if pair == 0:
                cg, *out = turn([], [], [cg, *out])
            else:
                cg, act_got, *out = turn([ffn_sum], [ffn_sum], [cg, act_got, *out])
            back.append(tuple(out))
        dqs, dks, dvs = zip(*back)
        keep, send, dqkv, small_w = wgrad(place, x, dqs, dks, dvs, qc)
        last_sum = Sum(keep, send, index, count, fours)
        (kcg,) = turn([], [last_sum], [kcg])
        vg, keep, send, small_v = conv_values(place, x, dl, kcg, probs, cg, maskr, expand)
        dg, vg = turn([ffn_sum, last_sum], [ffn_sum, last_sum], [dg, vg])
        dxd, keep, send = depth_back(
            place, x, dg, maskc, depthwise, kwg, small_f, small_c, small_v, small_w, keep, send
        )
        conv_sum = Sum(keep, send, index, count, [None])
        (dxd,) = turn([ffn_sum, last_sum], [ffn_sum, last_sum, conv_sum], [dxd])
        far = xgrad(place, True, dqkv, vg, dxd, resid, query_weight, weights)
        dxd, far = turn([], [], [dxd, far])
        own = xgrad(place, False, dqkv, vg, dxd, resid, query_weight, weights)
        every = [conv_sum, ffn_sum, last_sum]
        own, far = turn(every, every, [own, far])
        activations = jnp.stack(
            [jnp.where(first, act_own, act_got), jnp.where(first, act_got, act_own)]
        )
        activations, far = turn([ffn_sum, last_sum], [ffn_sum, last_sum], [activations, far])
        grad_got = across(far)
        turn([ffn_sum], [ffn_sum])
        turn([conv_sum], [conv_sum])
        every = [ffn_sum, last_sum, conv_sum]
        (grad_got,) = turn(every, every, [grad_got])
        grad_far = grad_got.astype(f32)
        input_grad = jnp.stack([jnp.where(first, own, grad_far), jnp.where(first, grad_far, own)])
        mine, theirs = ffn_sum.halves()
        down, up, out = unpack_ffn(place, True, mine, hidden)
        down, up, out = unpack_ffn(place, False, theirs, hidden, (down, up, out))
        down = down.reshape(GROUPS, hidden, part)
        spots = jnp.arange(HEADS * KERNEL)
        order = (spots % KERNEL) * 8 + spots // KERNEL
        order = (jnp.arange(LANES)[:, None] == order[None, :]).astype(bf16)
        (
            query_grad, query_bias_grad, stack, value_bias_grad, depth_grad, point_bias_grad,
            kernel_grad, kernel_bias_grad, conv_bias_grad, output_bias_grad, first_gain_grad,
            first_shift_grad, up_bias_grad, down_bias_grad, second_gain_grad, second_shift_grad,
        ) = unpack_mixers(place, *conv_sum.halves(), *last_sum.halves(), order, hidden)

        return (
            activations, input_grad, query_grad, query_bias_grad, stack[None], value_bias_grad,
            depth_grad, point_bias_grad, kernel_grad, kernel_bias_grad[0], conv_bias_grad, out,
            output_bias_grad, first_gain_grad, first_shift_grad, up, up_bias_grad, down,
            down_bias_grad, second_gain_grad, second_shift_grad,
        )

    return run


def solution(mesh):
    branches, ranks = mesh.shape["branch"], mesh.shape["dp"]
    fine = Mesh(mesh.devices.reshape(branches, ranks // 2, 2), AXES)
    whole = P()
    rows = ("chip", "core")
    tokens = P(rows, "branch", None)
    stack = P("branch", None, None, None)
    placed = (
        (P(rows, None, None), P(rows, None), whole, whole, stack) + (whole,) * 16 + (tokens,)
    )
    return jax.shard_map(
        local(dict(fine.shape)),
        mesh=fine,
        in_specs=placed,
        out_specs=(tokens, tokens, whole, whole, stack) + (whole,) * 16,
        check_vma=False,
    )
```
